1024 devices in a mesh: py: 64 (over z, y), pz: 16 (over x, core).
Axes of the slice: x: 8, y: 8, z: 8, core: 2. Of those that a mesh axis runs over, the one named last changes fastest.
Arguments:
- velocity: float32 [3, 256, 128, 512], P(None, 'py', 'pz'), may hold values from -24 to 24
- fraction: float32 [256, 128, 512], P('py', 'pz'), may hold values from 0 to 1
- wall_flags: int32 [2, 256, 128], P(None, 'py', 'pz'), may hold values from 0 to 1
Outputs:
- velocity_next: float32 [3, 256, 128, 512], P(None, 'py', 'pz')
- pressure_step: float32 [256, 128, 512], P('py', 'pz')
The draws below stay inside these ranges and needn't reach their ends.
Inputs may be any that keep to these rules, and one draw needn't show every extreme that they name: `wall_flags`: 1 marks a free-slip wall, 0 a no-slip wall.
All inputs are finite; a program needn't handle non-finite values.
Results may differ from the reference program's by a relative error of at most 0.0003.
Values sent between devices are 32-bit elements; how exact they have to be, the bound alone decides.
No kernel may reach another device: no remote copies, remote signals or barrier semaphores. Data moves between devices by JAX's collectives and lax.ppermute only.
A program may use at most 32 MiB of HBM per device.

```python
import math
import jax
import jax.numpy as jnp
from jax import lax

NX = 512
CY = 4
ITERS = 2
NY = 256
NZ = 128


def draw_velocity(key, part):
    key_noise, key_rows, key_columns = jax.random.split(key, 3)
    y_centers = (jnp.arange(NY, dtype=jnp.float32) + 0.5) / NY
    z_centers = (jnp.arange(NZ, dtype=jnp.float32) + 0.5) / NZ
    row_scale = jnp.exp(jax.random.uniform(key_rows, (NY,), jnp.float32, -0.9, 0.9))
    column_scale = jnp.exp(jax.random.uniform(key_columns, (NZ,), jnp.float32, -0.9, 0.9))
    noise = jnp.clip(jax.random.normal(key_noise, (3, NY, NZ, NX), jnp.float32), -3.5, 3.5)
    amplitude = 0.35 * jnp.exp(0.55 * (y_centers[:, None] + z_centers[None, :])) * row_scale[:, None] * column_scale[None, :]
    result = noise * amplitude[None, :, :, None]
    return result


def place_ends(values, rng, least, largest):
    longest = values.shape.index(max(values.shape))
    spots = []
    for shift in (0, 1):
        where = [jax.random.randint(jax.random.fold_in(rng, axis), (), 0, length) for axis, length in enumerate(values.shape)]
        where[longest] = (where[longest] + shift) % values.shape[longest]
        spots.append(tuple(where))
    return values.at[spots[0]].set(least).at[spots[1]].set(largest)


def levels(rng, extent, shards, least, largest):
    loudness, own = 1.0, jax.random.fold_in(rng, 6)
    for axis_at, shards_of in shards:
        steps = jnp.exp(jax.random.uniform(jax.random.fold_in(own, axis_at), (shards_of,), jnp.float32, least / len(shards), largest / len(shards)))
        loudness = loudness * jnp.repeat(steps, extent[axis_at] // shards_of).reshape([-1 if axis == axis_at else 1 for axis in range(len(extent))])
    return loudness


def setup_inputs(seed: int = 0) -> dict:
    key_list = jax.random.split(jax.random.key(seed), 4)
    velocity = draw_velocity(jax.random.fold_in(key_list[3], 71), 0)
    fraction = jnp.clip(1.0 * jax.random.uniform(key_list[1], (NY, NZ, NX), jnp.float32) ** levels(key_list[1], (NY, NZ, NX), ((0, 64), (1, 16)), -0.2, 0.2), 0.0, 1.0)
    wall_flags = place_ends(jax.random.randint(key_list[2], (2, NY, NZ), 0, 2), jax.random.fold_in(key_list[2], 1), 0, 1).astype(jnp.int32)
    return dict(velocity=velocity, fraction=fraction, wall_flags=wall_flags)


time_step = 0.05
heavy_density = 8.0
light_viscosity = 0.3
heavy_viscosity = 0.6
compressibility = 0.001
mean_inverse = 0.5
weno_epsilon = 1e-06

def weno_blend(slope_one, slope_two, slope_three, slope_four, slope_five):
    smooth_one = 13.0 / 12.0 * (slope_one - 2.0 * slope_two + slope_three) ** 2 + 0.25 * (slope_one - 4.0 * slope_two + 3.0 * slope_three) ** 2
    smooth_two = 13.0 / 12.0 * (slope_two - 2.0 * slope_three + slope_four) ** 2 + 0.25 * (slope_two - slope_four) ** 2
    smooth_three = 13.0 / 12.0 * (slope_three - 2.0 * slope_four + slope_five) ** 2 + 0.25 * (3.0 * slope_three - 4.0 * slope_four + slope_five) ** 2
    alpha_one = 0.1 / (weno_epsilon + smooth_one) ** 2
    alpha_two = 0.6 / (weno_epsilon + smooth_two) ** 2
    alpha_three = 0.3 / (weno_epsilon + smooth_three) ** 2
    weight_sum = alpha_one + alpha_two + alpha_three
    blended = alpha_one * (slope_one / 3.0 - 7.0 * slope_two / 6.0 + 11.0 * slope_three / 6.0)
    blended = blended + alpha_two * (-slope_two / 6.0 + 5.0 * slope_three / 6.0 + slope_four / 3.0)
    blended = blended + alpha_three * (slope_three / 3.0 + 5.0 * slope_four / 6.0 - slope_five / 6.0)
    return blended / weight_sum

def upwind_derivative(padded, direction_axis, advecting):
    length = padded.shape[direction_axis] - 6
    differences = jnp.diff(padded, axis=direction_axis)

    def window(offset):
        return lax.slice_in_dim(differences, offset, offset + length, axis=direction_axis)
    lower_side = weno_blend(window(0), window(1), window(2), window(3), window(4))
    upper_side = weno_blend(window(5), window(4), window(3), window(2), window(1))
    return jnp.where(advecting > 0, lower_side, upper_side)

def predicted(center, along_x, along_y, along_z, fraction):
    slope_x = upwind_derivative(along_x, 3, center[0][None])
    slope_y = upwind_derivative(along_y, 1, center[1][None])
    slope_z = upwind_derivative(along_z, 2, center[2][None])
    transport = center[0] * slope_x + center[1] * slope_y + center[2] * slope_z
    spread = along_x[..., 4:-2] + along_x[..., 2:-4] - 2.0 * center
    spread = spread + (along_y[:, 4:-2] + along_y[:, 2:-4] - 2.0 * center)
    spread = spread + (along_z[:, :, 4:-2] + along_z[:, :, 2:-4] - 2.0 * center)
    density = 1.0 + (heavy_density - 1.0) * fraction
    kinematic = (light_viscosity + (heavy_viscosity - light_viscosity) * fraction) / density
    return center + time_step * (kinematic * spread - transport)

def wall_ghosts(velocity, wall_flags):
    tangential = 2.0 * wall_flags.astype(jnp.float32) - 1.0
    normal = -jnp.ones_like(tangential)
    mirror_signs = jnp.stack([normal, tangential, tangential])
    lower_ghost = velocity[..., :3][..., ::-1] * mirror_signs[:, 0, :, :, None]
    upper_ghost = velocity[..., -3:][..., ::-1] * mirror_signs[:, 1, :, :, None]
    return jnp.concatenate([lower_ghost, velocity, upper_ghost], axis=-1)

def cosine_forward(values):
    length = values.shape[-1]
    reordered = jnp.concatenate([values[..., ::2], values[..., 1::2][..., ::-1]], axis=-1)
    spectrum = jnp.fft.fft(reordered, axis=-1)
    wave_index = jnp.arange(length, dtype=jnp.float32)
    twiddle = jnp.exp(-0.5j * math.pi / length * wave_index)
    norm_scale = jnp.where(wave_index == 0, math.sqrt(1.0 / length), math.sqrt(2.0 / length))
    return jnp.real(spectrum * twiddle) * norm_scale

def cosine_inverse(values):
    length = values.shape[-1]
    wave_index = jnp.arange(length, dtype=jnp.float32)
    norm_scale = jnp.where(wave_index == 0, math.sqrt(1.0 / length), math.sqrt(2.0 / length))
    scaled = values / norm_scale
    mirrored = jnp.concatenate([jnp.zeros_like(scaled[..., :1]), scaled[..., :0:-1]], axis=-1)
    spectrum = jnp.exp(0.5j * math.pi / length * wave_index) * (scaled - 1j * mirrored)
    reordered = jnp.real(jnp.fft.ifft(spectrum, axis=-1))
    half_length = length // 2
    even_part = reordered[..., :half_length]
    odd_part = reordered[..., half_length:][..., ::-1]
    return jnp.stack([even_part, odd_part], axis=-1).reshape(values.shape)

def along_dimension(function, values, dimension):
    return jnp.moveaxis(function(jnp.moveaxis(values, dimension, -1)), -1, dimension)

def eigenvalue(length):
    return 2.0 - 2.0 * jnp.cos(math.pi / length * jnp.arange(length, dtype=jnp.float32))

def precondition(values):
    spectral = values
    for dimension in range(3):
        spectral = along_dimension(cosine_forward, spectral, dimension)
    denominator = compressibility + mean_inverse * (eigenvalue(NY)[:, None, None] + eigenvalue(NZ)[None, :, None] + eigenvalue(NX)[None, None, :])
    spectral = spectral / denominator
    for dimension in range(3):
        spectral = along_dimension(cosine_inverse, spectral, dimension)
    return spectral

def face_flux(values, beta, dimension):
    length = values.shape[dimension]
    difference = lax.slice_in_dim(values, 1, length, axis=dimension) - lax.slice_in_dim(values, 0, length - 1, axis=dimension)
    padding = [(0, 0), (0, 0), (0, 0)]
    padding[dimension] = (1, 1)
    return jnp.pad(beta * difference, padding)

def flux_parts(values, face_betas):
    return [face_flux(values, face_betas[dimension], dimension) for dimension in range(3)]

def differenced(fluxes, dimension):
    length = fluxes.shape[dimension]
    return lax.slice_in_dim(fluxes, 1, length, axis=dimension) - lax.slice_in_dim(fluxes, 0, length - 1, axis=dimension)

def averaged(fluxes, dimension):
    length = fluxes.shape[dimension]
    return 0.5 * (lax.slice_in_dim(fluxes, 1, length, axis=dimension) + lax.slice_in_dim(fluxes, 0, length - 1, axis=dimension))

def apply_operator(values, face_betas):
    parts = flux_parts(values, face_betas)
    return compressibility * values - (differenced(parts[2], 2) + differenced(parts[0], 0) + differenced(parts[1], 1))

def reference(velocity, fraction, wall_flags):
    extended = wall_ghosts(velocity, wall_flags)
    padded = jnp.pad(extended, ((0, 0), (3, 3), (3, 3), (0, 0)))

    def slab_update(first_row):
        slab_cells = lax.dynamic_slice(padded, (jnp.int32(0), first_row, jnp.int32(0), jnp.int32(0)), (3, CY + 6, NZ + 6, NX + 6))
        slab_fraction = lax.dynamic_slice(fraction, (first_row, jnp.int32(0), jnp.int32(0)), (CY, NZ, NX))
        center = slab_cells[:, 3:-3, 3:-3, 3:-3]
        return predicted(center, slab_cells[:, 3:-3, 3:-3, :], slab_cells[:, :, 3:-3, 3:-3], slab_cells[:, 3:-3, :, 3:-3], slab_fraction)
    row_starts = jnp.arange(NY // CY, dtype=jnp.int32) * CY
    slab_results = lax.map(slab_update, row_starts)
    provisional = jnp.moveaxis(slab_results, 1, 0).reshape(3, NY, NZ, NX)
    normal_x = provisional[0]
    forward_x = jnp.concatenate([normal_x[:, :, 1:], -normal_x[:, :, -1:]], axis=2)
    backward_x = jnp.concatenate([-normal_x[:, :, :1], normal_x[:, :, :-1]], axis=2)
    padded_y = jnp.pad(provisional[1], ((1, 1), (0, 0), (0, 0)))
    padded_z = jnp.pad(provisional[2], ((0, 0), (1, 1), (0, 0)))
    spread_x = 0.5 * (forward_x - backward_x)
    spread_y = 0.5 * (padded_y[2:] - padded_y[:-2])
    spread_z = 0.5 * (padded_z[:, 2:] - padded_z[:, :-2])
    source = -(spread_x + spread_y + spread_z)
    density = 1.0 + (heavy_density - 1.0) * fraction
    face_betas = []
    for dimension in range(3):
        length = density.shape[dimension]
        upper_cells = lax.slice_in_dim(density, 1, length, axis=dimension)
        lower_cells = lax.slice_in_dim(density, 0, length - 1, axis=dimension)
        face_betas.append(2.0 / (upper_cells + lower_cells))
    solution = jnp.zeros_like(source)
    residual = source
    search = precondition(residual)
    aligned = jnp.sum(residual * search)
    direction = search
    for iteration in range(ITERS):
        applied = apply_operator(direction, face_betas)
        step_size = aligned / jnp.sum(direction * applied)
        solution = solution + step_size * direction
        if iteration + 1 < ITERS:
            residual = residual - step_size * applied
            search = precondition(residual)
            renewed = jnp.sum(residual * search)
            direction = search + renewed / aligned * direction
            aligned = renewed
    parts = flux_parts(solution, face_betas)
    correction = jnp.stack([averaged(parts[2], 2), averaged(parts[0], 0), averaged(parts[1], 1)])
    return (provisional - correction, solution)
```

```python
import math

import jax
import jax.numpy as jnp
import numpy as np
from jax import lax
from jax.sharding import PartitionSpec as P

NX = 512
ITERS = 2


time_step = 0.05
heavy_density = 8.0
light_viscosity = 0.3
heavy_viscosity = 0.6
compressibility = 0.001
mean_inverse = 0.5
weno_epsilon = 1e-06
highest = lax.Precision.HIGHEST


def weno_blend(slope_one, slope_two, slope_three, slope_four, slope_five):
    smooth_one = (
        13.0 / 12.0 * (slope_one - 2.0 * slope_two + slope_three) ** 2
        + 0.25 * (slope_one - 4.0 * slope_two + 3.0 * slope_three) ** 2
    )
    smooth_two = (
        13.0 / 12.0 * (slope_two - 2.0 * slope_three + slope_four) ** 2
        + 0.25 * (slope_two - slope_four) ** 2
    )
    smooth_three = (
        13.0 / 12.0 * (slope_three - 2.0 * slope_four + slope_five) ** 2
        + 0.25 * (3.0 * slope_three - 4.0 * slope_four + slope_five) ** 2
    )
    alpha_one = 0.1 / (weno_epsilon + smooth_one) ** 2
    alpha_two = 0.6 / (weno_epsilon + smooth_two) ** 2
    alpha_three = 0.3 / (weno_epsilon + smooth_three) ** 2
    weight_sum = alpha_one + alpha_two + alpha_three
    blended = alpha_one * (slope_one / 3.0 - 7.0 * slope_two / 6.0 + 11.0 * slope_three / 6.0)
    blended = blended + alpha_two * (-slope_two / 6.0 + 5.0 * slope_three / 6.0 + slope_four / 3.0)
    blended = blended + alpha_three * (
        slope_three / 3.0 + 5.0 * slope_four / 6.0 - slope_five / 6.0
    )
    return blended / weight_sum


def upwind_derivative(padded, direction_axis, advecting):
    length = padded.shape[direction_axis] - 6
    differences = jnp.diff(padded, axis=direction_axis)

    def window(offset):
        return lax.slice_in_dim(differences, offset, offset + length, axis=direction_axis)

    lower_side = weno_blend(window(0), window(1), window(2), window(3), window(4))
    upper_side = weno_blend(window(5), window(4), window(3), window(2), window(1))
    return jnp.where(advecting > 0, lower_side, upper_side)


def predicted(center, along_x, along_y, along_z, fraction):
    slope_x = upwind_derivative(along_x, 3, center[0][None])
    slope_y = upwind_derivative(along_y, 1, center[1][None])
    slope_z = upwind_derivative(along_z, 2, center[2][None])
    transport = center[0] * slope_x + center[1] * slope_y + center[2] * slope_z
    spread = along_x[..., 4:-2] + along_x[..., 2:-4] - 2.0 * center
    spread = spread + (along_y[:, 4:-2] + along_y[:, 2:-4] - 2.0 * center)
    spread = spread + (along_z[:, :, 4:-2] + along_z[:, :, 2:-4] - 2.0 * center)
    density = 1.0 + (heavy_density - 1.0) * fraction
    kinematic = (light_viscosity + (heavy_viscosity - light_viscosity) * fraction) / density
    return center + time_step * (kinematic * spread - transport)


def wall_ghosts(velocity, wall_flags):
    tangential = 2.0 * wall_flags.astype(jnp.float32) - 1.0
    normal = -jnp.ones_like(tangential)
    mirror_signs = jnp.stack([normal, tangential, tangential])
    lower_ghost = velocity[..., :3][..., ::-1] * mirror_signs[:, 0, :, :, None]
    upper_ghost = velocity[..., -3:][..., ::-1] * mirror_signs[:, 1, :, :, None]
    return jnp.concatenate([lower_ghost, velocity, upper_ghost], axis=-1)


def shifted_pair(head, tail, axis):
    count = lax.axis_size(axis)
    up = [(i, i + 1) for i in range(count - 1)]
    down = [(i + 1, i) for i in range(count - 1)]
    return lax.ppermute(tail, axis, up), lax.ppermute(head, axis, down)


def cosine_table(length):
    wave_index = np.arange(length)[:, None]
    position = np.arange(length)[None, :]
    angle = np.pi / (2 * length) * (wave_index * (2 * position + 1) % (4 * length))
    weight = np.where(wave_index == 0, np.sqrt(1.0 / length), np.sqrt(2.0 / length))
    return weight * np.cos(angle)


def central_table(length):
    return 0.5 * (np.eye(length, k=1) - np.eye(length, k=-1))


def with_rims(table, blocks):
    length = table.shape[0]
    inverse = np.concatenate([np.zeros((1, length)), table.T, np.zeros((1, length))])
    size = length // blocks
    return np.concatenate([inverse[i * size : i * size + size + 2] for i in range(blocks)])


def eigenvalue(wave_index, length):
    return 2.0 - 2.0 * jnp.cos(math.pi / length * wave_index.astype(jnp.float32))


def face_weights(density, y_low, y_high, z_low, z_high, edges):
    inner_x = 2.0 / (density[:, :, 1:] + density[:, :, :-1])
    plus_x = jnp.concatenate([inner_x, jnp.zeros_like(density[:, :, :1])], axis=2)
    along_y = jnp.concatenate([y_low, density, y_high], axis=0)
    along_z = jnp.concatenate([z_low, density, z_high], axis=1)
    first_y, last_y, first_z, last_z = edges
    beta_y = 2.0 / (along_y[1:] + along_y[:-1])
    beta_z = 2.0 / (along_z[:, 1:] + along_z[:, :-1])
    rows, cols = density.shape[:2]
    face_y = jnp.arange(rows + 1, dtype=jnp.int32)[:, None, None]
    face_z = jnp.arange(cols + 1, dtype=jnp.int32)[None, :, None]
    wall_y = (first_y & (face_y == 0)) | (last_y & (face_y == rows))
    wall_z = (first_z & (face_z == 0)) | (last_z & (face_z == cols))
    return plus_x, jnp.where(wall_y, 0.0, beta_y), jnp.where(wall_z, 0.0, beta_z)


def face_fluxes(rimmed, weights):
    plus_x, beta_y, beta_z = weights
    values = rimmed[1:-1, 1:-1]
    forward_x = plus_x * (jnp.roll(values, -1, axis=2) - values)
    backward_x = jnp.roll(forward_x, 1, axis=2)
    flux_y = beta_y * (rimmed[1:, 1:-1] - rimmed[:-1, 1:-1])
    flux_z = beta_z * (rimmed[1:-1, 1:] - rimmed[1:-1, :-1])
    return forward_x, backward_x, flux_y[1:], flux_y[:-1], flux_z[:, 1:], flux_z[:, :-1]


def apply_operator(rimmed, weights):
    forward_x, backward_x, forward_y, backward_y, forward_z, backward_z = face_fluxes(
        rimmed, weights
    )
    return compressibility * rimmed[1:-1, 1:-1] - (
        forward_x - backward_x + (forward_y - backward_y) + (forward_z - backward_z)
    )


def exchange(message, axis):
    return lax.all_to_all(message, axis, split_axis=0, concat_axis=0, tiled=True)


def packed(rows, extras, width):
    count = rows.shape[0]
    tail = jnp.broadcast_to(jnp.stack(extras)[None], (count, len(extras))) if extras else rows[:, :0]
    fill = jnp.zeros((count, width - rows.shape[1] - len(extras)), rows.dtype)
    return jnp.concatenate([rows, tail, fill], axis=1).reshape(count, width // 128, 128)


def summed(partials):
    row = jnp.concatenate([jnp.stack(partials), jnp.zeros((128 - len(partials),), jnp.float32)])
    for axis in ("py", "pz"):
        count = lax.axis_size(axis)
        parts = exchange(jnp.broadcast_to(row[None, None], (count, 1, 128)), axis)
        row = jnp.sum(parts[:, 0], axis=0)
    return [row[i] for i in range(len(partials))]


def dot(left, right):
    return jnp.dot(left, right, precision=highest)


def on_device(velocity, fraction, wall_flags):
    rows, cols = (fraction.shape[0], fraction.shape[1])
    rows_devices = lax.axis_size("py")
    cols_devices = lax.axis_size("pz")
    total_rows = rows * rows_devices
    total_cols = cols * cols_devices
    row_index = lax.axis_index("py")
    col_index = lax.axis_index("pz")
    edges = (row_index == 0, row_index == rows_devices - 1, col_index == 0, col_index == cols_devices - 1)

    def y_layers(part, width):
        return part.reshape(3 * width, cols, NX)

    y_head = jnp.concatenate([y_layers(velocity[:, :3], 3), fraction[:1]], axis=0)
    y_tail = jnp.concatenate([y_layers(velocity[:, -3:], 3), fraction[-1:]], axis=0)
    y_low, y_high = shifted_pair(y_head, y_tail, "py")

    def z_layers(first, only):
        lanes = jnp.transpose(velocity[:, :, first : first + 3], (0, 2, 1, 3)).reshape(9, rows, NX)
        return jnp.concatenate([lanes, fraction[:, only][None]], axis=0)

    z_low, z_high = shifted_pair(z_layers(0, 0), z_layers(cols - 3, cols - 1), "pz")

    def unlayered(z_rim):
        return jnp.transpose(z_rim[:9].reshape(3, 3, rows, NX), (0, 2, 1, 3))

    provisional = predicted(
        velocity,
        wall_ghosts(velocity, wall_flags),
        jnp.concatenate([y_low[:9].reshape(3, 3, cols, NX), velocity, y_high[:9].reshape(3, 3, cols, NX)], axis=1),
        jnp.concatenate([unlayered(z_low), velocity, unlayered(z_high)], axis=2),
        fraction,
    )

    def density_of(part):
        return 1.0 + (heavy_density - 1.0) * part

    weights = face_weights(
        density_of(fraction),
        density_of(y_low[9:]),
        density_of(y_high[9:]),
        density_of(z_low[9][:, None]),
        density_of(z_high[9][:, None]),
        edges,
    )
    normal_x = provisional[0]
    forward_x = jnp.concatenate([normal_x[:, :, 1:], -normal_x[:, :, -1:]], axis=2)
    backward_x = jnp.concatenate([-normal_x[:, :, :1], normal_x[:, :, :-1]], axis=2)
    source_x = -0.5 * (forward_x - backward_x)

    plain_x = cosine_table(NX)
    plain_y = cosine_table(total_rows)
    plain_z = cosine_table(total_cols)

    def constant(table):
        return jnp.asarray(table, dtype=jnp.float32)

    table_x = constant(plain_x)
    table_y = constant(plain_y)
    table_z = constant(plain_z)
    source_y = constant(np.concatenate([plain_y, -plain_y @ central_table(total_rows)], axis=1))
    source_z = constant(np.concatenate([plain_z, -plain_z @ central_table(total_cols)], axis=1))
    back_y = constant(with_rims(plain_y, rows_devices))
    back_z = constant(with_rims(plain_z, cols_devices))

    part_x = NX // rows_devices
    part_y = total_rows // cols_devices
    wave_y = col_index * part_y + jnp.arange(part_y, dtype=jnp.int32)
    wave_z = jnp.arange(total_cols, dtype=jnp.int32)
    wave_x = row_index * part_x + jnp.arange(part_x, dtype=jnp.int32)
    modes = (eigenvalue(wave_y, total_rows)[:, None] + eigenvalue(wave_x, NX)[None, :]).reshape(1, -1)
    denominator = compressibility + mean_inverse * (modes + eigenvalue(wave_z, total_cols)[:, None])
    block = rows * cols * part_x

    def along_x(fields):
        count = fields.shape[0]
        spectral = lax.dot_general(
            table_x, fields.reshape(-1, NX), (((1,), (1,)), ((), ())), precision=highest
        )
        return spectral.reshape(rows_devices, -1), count

    def to_rows(message, count):
        cells = message.reshape(rows_devices, part_x, count, rows, cols)
        return jnp.transpose(cells, (2, 0, 3, 1, 4)).reshape(count, total_rows, part_x * cols)

    def to_cols(message, count):
        cells = message.reshape(cols_devices, count, part_y, part_x, cols)
        return jnp.transpose(cells, (1, 0, 4, 2, 3)).reshape(count * total_cols, part_y * part_x)

    def back(spectral):
        wide = dot(back_z, spectral).reshape(cols_devices, -1)
        wide = exchange(packed(wide, [], wide.shape[1]), "pz").reshape(
            cols_devices, cols + 2, part_y, part_x
        )
        wide = jnp.transpose(wide, (0, 2, 1, 3)).reshape(total_rows, -1)
        wide = dot(back_y, wide).reshape(rows_devices, -1)
        size = wide.shape[1]
        wide = exchange(packed(wide, [], 512), "py").reshape(rows_devices, 512)[:, :size]
        wide = wide.reshape(rows_devices, (rows + 2) * (cols + 2), part_x)
        wide = jnp.transpose(wide, (1, 0, 2)).reshape((rows + 2) * (cols + 2), NX)
        return dot(wide, table_x).reshape(rows + 2, cols + 2, NX)

    fields = jnp.stack([source_x, provisional[1], provisional[2]])
    message, count = along_x(fields)
    message = exchange(packed(message, [], 1024), "py").reshape(rows_devices, -1)[:, : count * block]
    cells = to_rows(message, count)
    joined = dot(source_y, cells[:2].reshape(2 * total_rows, -1))
    third = dot(table_y, cells[2])
    message = jnp.stack(
        [joined.reshape(cols_devices, -1), third.reshape(cols_devices, -1)], axis=1
    ).reshape(cols_devices, -1)
    message = exchange(packed(message, [], message.shape[1]), "pz")
    residual = dot(source_z, to_cols(message, 2))
    search = residual / denominator
    aligned = jnp.sum(residual * search)

    first = back(search)
    applied = apply_operator(first, weights)
    curvature = jnp.sum(first[1:-1, 1:-1] * applied)

    message, count = along_x(applied[None])
    message = exchange(packed(message, [aligned, curvature], 512), "py").reshape(rows_devices, 512)
    totals = jnp.sum(message[:, block : block + 2], axis=0)
    image = dot(table_y, to_rows(message[:, :block], 1)[0]).reshape(cols_devices, -1)
    size = image.shape[1]
    message = exchange(packed(image, [totals[0], totals[1]], size + 128), "pz").reshape(cols_devices, -1)
    totals = jnp.sum(message[:, size : size + 2], axis=0)
    aligned, curvature = totals[0], totals[1]
    image = dot(table_z, to_cols(message[:, :size], 1))
    first_step = aligned / curvature
    residual = residual - first_step * image
    search = residual / denominator
    renewed = jnp.sum(residual * search)

    second = back(search)
    core = second[1:-1, 1:-1]
    bent = jnp.sum(core * apply_operator(second, weights))
    crossed = jnp.sum(core * applied)
    renewed, bent, crossed = summed([renewed, bent, crossed])
    ratio = renewed / aligned
    second_step = renewed / (bent + 2.0 * ratio * crossed + ratio * ratio * curvature)
    solution = first_step * first + second_step * (second + ratio * first)
    forward_x, backward_x, forward_y, backward_y, forward_z, backward_z = face_fluxes(
        solution, weights
    )
    correction = jnp.stack(
        [
            0.5 * (forward_x + backward_x),
            0.5 * (forward_y + backward_y),
            0.5 * (forward_z + backward_z),
        ]
    )
    return (provisional - correction, solution[1:-1, 1:-1])


def solution(mesh):
    in_specs = (P(None, "py", "pz", None), P("py", "pz", None), P(None, "py", "pz"))
    out_specs = (P(None, "py", "pz", None), P("py", "pz", None))
    return jax.shard_map(
        on_device, mesh=mesh, in_specs=in_specs, out_specs=out_specs, check_vma=False
    )
```

```python
import math

import jax
import jax.numpy as jnp
import numpy as np
from jax import lax
from jax.experimental import pallas as pl
from jax.experimental.pallas import tpu as pltpu
from jax.sharding import PartitionSpec as P

NX = 512
ITERS = 2


time_step = 0.05
heavy_density = 8.0
light_viscosity = 0.3
heavy_viscosity = 0.6
compressibility = 0.001
mean_inverse = 0.5
weno_epsilon = 1e-06
highest = lax.Precision.HIGHEST


def weno_blend(slope_one, slope_two, slope_three, slope_four, slope_five):
    smooth_one = (
        13.0 / 12.0 * (slope_one - 2.0 * slope_two + slope_three) ** 2
        + 0.25 * (slope_one - 4.0 * slope_two + 3.0 * slope_three) ** 2
    )
    smooth_two = (
        13.0 / 12.0 * (slope_two - 2.0 * slope_three + slope_four) ** 2
        + 0.25 * (slope_two - slope_four) ** 2
    )
    smooth_three = (
        13.0 / 12.0 * (slope_three - 2.0 * slope_four + slope_five) ** 2
        + 0.25 * (3.0 * slope_three - 4.0 * slope_four + slope_five) ** 2
    )
    alpha_one = 0.1 / (weno_epsilon + smooth_one) ** 2
    alpha_two = 0.6 / (weno_epsilon + smooth_two) ** 2
    alpha_three = 0.3 / (weno_epsilon + smooth_three) ** 2
    weight_sum = alpha_one + alpha_two + alpha_three
    blended = alpha_one * (slope_one / 3.0 - 7.0 * slope_two / 6.0 + 11.0 * slope_three / 6.0)
    blended = blended + alpha_two * (-slope_two / 6.0 + 5.0 * slope_three / 6.0 + slope_four / 3.0)
    blended = blended + alpha_three * (
        slope_three / 3.0 + 5.0 * slope_four / 6.0 - slope_five / 6.0
    )
    return blended / weight_sum


def upwind_derivative(padded, direction_axis, advecting):
    length = padded.shape[direction_axis] - 6
    differences = jnp.diff(padded, axis=direction_axis)

    def window(offset):
        return lax.slice_in_dim(differences, offset, offset + length, axis=direction_axis)

    lower_side = weno_blend(window(0), window(1), window(2), window(3), window(4))
    upper_side = weno_blend(window(5), window(4), window(3), window(2), window(1))
    return jnp.where(advecting > 0, lower_side, upper_side)


def predicted(center, along_x, along_y, along_z, fraction):
    slope_x = upwind_derivative(along_x, 3, center[0][None])
    slope_y = upwind_derivative(along_y, 1, center[1][None])
    slope_z = upwind_derivative(along_z, 2, center[2][None])
    transport = center[0] * slope_x + center[1] * slope_y + center[2] * slope_z
    spread = along_x[..., 4:-2] + along_x[..., 2:-4] - 2.0 * center
    spread = spread + (along_y[:, 4:-2] + along_y[:, 2:-4] - 2.0 * center)
    spread = spread + (along_z[:, :, 4:-2] + along_z[:, :, 2:-4] - 2.0 * center)
    density = 1.0 + (heavy_density - 1.0) * fraction
    kinematic = (light_viscosity + (heavy_viscosity - light_viscosity) * fraction) / density
    return center + time_step * (kinematic * spread - transport)


def wall_ghosts(velocity, wall_flags):
    tangential = 2.0 * wall_flags.astype(jnp.float32) - 1.0
    normal = -jnp.ones_like(tangential)
    mirror_signs = jnp.stack([normal, tangential, tangential])
    lower_ghost = velocity[..., :3][..., ::-1] * mirror_signs[:, 0, :, :, None]
    upper_ghost = velocity[..., -3:][..., ::-1] * mirror_signs[:, 1, :, :, None]
    return jnp.concatenate([lower_ghost, velocity, upper_ghost], axis=-1)


def shifted_pair(head, tail, axis):
    count = lax.axis_size(axis)
    up = [(i, i + 1) for i in range(count - 1)]
    down = [(i + 1, i) for i in range(count - 1)]
    return lax.ppermute(tail, axis, up), lax.ppermute(head, axis, down)


def cosine_table(length):
    wave_index = np.arange(length)[:, None]
    position = np.arange(length)[None, :]
    angle = np.pi / (2 * length) * (wave_index * (2 * position + 1) % (4 * length))
    weight = np.where(wave_index == 0, np.sqrt(1.0 / length), np.sqrt(2.0 / length))
    return weight * np.cos(angle)


def half_eigenvalue(length):
    return mean_inverse * 4.0 * np.sin(np.pi * np.arange(length) / (2 * length)) ** 2


def exchange(message, axis):
    return lax.all_to_all(message, axis, split_axis=0, concat_axis=0, tiled=True)


def dot(left, right):
    return lax.dot_general(
        left, right, (((1,), (0,)), ((), ())), precision=highest, preferred_element_type=jnp.float32
    )


def dot_nt(left, right):
    return lax.dot_general(
        left, right, (((1,), (1,)), ((), ())), precision=highest, preferred_element_type=jnp.float32
    )


def rolled(values, shift, axis):
    return pltpu.roll(values, shift % values.shape[axis], axis)


def moved(values, step):
    row = lax.broadcasted_iota(jnp.int32, values.shape, 0)
    edge = 0 if step == 1 else values.shape[0] - 1
    return jnp.where(row == edge, 0.0, rolled(values, step, 0))


def picked(values, source):
    lane = lax.broadcasted_iota(jnp.int32, (values.shape[1], source.shape[1]), 0)
    chosen = jnp.where(lane == source, 1.0, 0.0).astype(jnp.bfloat16)
    total = None
    rest = values
    for _ in range(3):
        piece = rest.astype(jnp.bfloat16)
        rest = rest - piece.astype(jnp.float32)
        term = jnp.dot(piece, chosen, preferred_element_type=jnp.float32)
        total = term if total is None else total + term
    return total


def from_tiles(tiles, count):
    return jnp.concatenate([tiles[:, t, :] for t in range(count)], axis=1)


def into_tiles(ref, values):
    for t in range(values.shape[1] // 128):
        ref[:, t, :] = values[:, 128 * t : 128 * t + 128]


def to_message(rows, table_x):
    spectral = dot_nt(table_x, rows)
    devices = spectral.shape[0] // 8
    return jnp.concatenate([spectral[devices * k : devices * k + devices] for k in range(8)], axis=1)


def row_blocks(message, source):
    ordered = picked(message, source)
    return [ordered[:, 64 * y : 64 * y + 64] for y in range(4)]


def to_modes(blocks, table_y):
    return dot(jnp.concatenate(blocks, axis=0).T, table_y)


def moments(rows, rho):
    upward = rows[0:8]
    for z in range(1, 8):
        upward = rho * upward + rows[8 * z : 8 * z + 8]
    downward = rows[56:64]
    for z in range(6, -1, -1):
        downward = rho * downward + rows[8 * z : 8 * z + 8]
    return upward, downward


def incoming(upward, downward, weights):
    low = jnp.sum(weights[0] * upward + weights[1] * downward, axis=0)
    high = jnp.sum(weights[2] * upward + weights[3] * downward, axis=0)
    return low, high


def solved(rows, low, high, rho, scale):
    inverse = 1.0 / rho
    cells = [rows[8 * z : 8 * z + 8] for z in range(8)]
    wave = low * inverse
    forward = [wave]
    for z in range(8):
        wave = rho * wave + cells[z]
        forward.append(wave)
    forward.append(rho * wave)
    wave = high
    backward = [high * inverse, high]
    for z in range(7, -1, -1):
        wave = rho * (wave + cells[z])
        backward.append(wave)
    backward = backward[::-1]
    return jnp.concatenate([scale * (f + b) for f, b in zip(forward, backward)], axis=0)


def to_rims(modes, table_y, source):
    rows = dot_nt(table_y, modes)
    devices = rows.shape[0] // 4
    blocks = [rows[devices * y : devices * y + devices] for y in range(4)]
    blocks = [moved(blocks[3], 1), *blocks, moved(blocks[0], -1)]
    return picked(jnp.concatenate(blocks, axis=1), source)


def from_rims(message, table_x):
    stacked = jnp.concatenate([message[:, 64 * k : 64 * k + 64] for k in range(8)], axis=0)
    return dot(stacked.T, table_x)


def fluxes(slots, beta_x, beta_y, beta_z):
    tiles = [slots[8 * y : 8 * y + 8] for y in range(6)]
    flux_y = [beta_y[y] * (tiles[y + 1] - tiles[y]) for y in range(5)]
    layer = lax.broadcasted_iota(jnp.int32, tiles[0].shape, 0)
    results = []
    for y in range(4):
        cells = tiles[y + 1]
        forward_x = beta_x[y] * (rolled(cells, -1, 1) - cells)
        above = jnp.where(layer == 7, slots[52 + y : 53 + y], rolled(cells, -1, 0))
        below = jnp.where(layer == 0, slots[48 + y : 49 + y], rolled(cells, 1, 0))
        results.append(
            (
                cells,
                forward_x,
                rolled(forward_x, 1, 1),
                flux_y[y + 1],
                flux_y[y],
                beta_z[0, y] * (above - cells),
                beta_z[1, y] * (cells - below),
            )
        )
    return results


def applied_rows(slots, beta_x, beta_y, beta_z):
    rows = []
    for cells, fx, bx, fy, by, fz, bz in fluxes(slots, beta_x, beta_y, beta_z):
        rows.append(compressibility * cells - (fx - bx + (fy - by) + (fz - bz)))
    return jnp.concatenate(rows, axis=0)


def total(values):
    return jnp.sum(jnp.sum(values, axis=0, keepdims=True), axis=1, keepdims=True)


def lane_row(values):
    lane = lax.broadcasted_iota(jnp.int32, (1, 128), 1)
    row = jnp.zeros((1, 128), jnp.float32)
    for index, value in enumerate(values):
        row = jnp.where(lane == index, value, row)
    return row


def send_fields(fields_ref, table_ref, out_ref):
    table = table_ref[...]
    for c in range(3):
        message = to_message(fields_ref[c].reshape(32, NX), table)
        out_ref[:, 2 * c, :] = message[:, :128]
        out_ref[:, 2 * c + 1, :] = message[:, 128:]


def read_fields(message_ref, table_ref, source_ref, rho_ref, gather_ref, rows_ref):
    tiles = message_ref[...]
    source = source_ref[...]
    parts = []
    for c in range(3):
        pair = jnp.concatenate([tiles[:, 2 * c, :], tiles[:, 2 * c + 1, :]], axis=1)
        parts.append(row_blocks(pair, source))
    across, along_y, along_z = parts
    after = [*along_y[1:], moved(along_y[0], -1)]
    before = [moved(along_y[3], 1), *along_y[:3]]
    table = table_ref[...]
    joined = to_modes([s - 0.5 * (a - b) for s, a, b in zip(across, after, before)], table)
    third = to_modes(along_z, table)
    zero = jnp.zeros_like(third[:8])
    above = jnp.concatenate([third[8:], zero], axis=0)
    below = jnp.concatenate([zero, third[:-8]], axis=0)
    rows = joined - 0.5 * (above - below)
    rho = rho_ref[...]
    upward, downward = moments(rows, rho)
    gather_ref[0:8] = upward
    gather_ref[8:16] = downward
    gather_ref[16:24] = third[0:8]
    gather_ref[24:32] = third[56:64]
    rows_ref[...] = rows


def first_solve(gather_ref, rows_ref, edge_ref, rho_ref, scale_ref, weights_ref, table_ref, source_ref,
                out_ref, residual_ref, waves_ref, aligned_ref):
    rho = rho_ref[...]
    power = rho * rho
    power = power * power * power * rho
    gathered = gather_ref[...]
    first, last = gathered[:, 16:24], gathered[:, 24:32]
    zero = jnp.zeros_like(first[:1])
    under = 0.5 * jnp.concatenate([zero, last[:-1]], axis=0)
    over = -0.5 * jnp.concatenate([first[1:], zero], axis=0)
    upward = gathered[:, 0:8] + power * under + over
    downward = gathered[:, 8:16] + under + power * over
    low, high = incoming(upward, downward, weights_ref[...])
    mine = edge_ref[...]
    rows = rows_ref[...]
    rows = jnp.concatenate(
        [
            rows[:8] + jnp.sum(mine * under, axis=0),
            rows[8:56],
            rows[56:] + jnp.sum(mine * over, axis=0),
        ],
        axis=0,
    )
    modes = solved(rows, low, high, rho, scale_ref[...])
    aligned_ref[...] = lane_row([total(rows * modes[8:72])])
    residual_ref[...] = rows
    waves_ref[0:8] = low
    waves_ref[8:16] = high
    into_tiles(out_ref, to_rims(modes, table_ref[...], source_ref[...]))


def first_image(message_ref, aligned_ref, table_ref, beta_x_ref, beta_y_ref, beta_z_ref, out_ref, slots_ref, applied_ref):
    table = table_ref[...]
    slots = from_rims(from_tiles(message_ref[...], 4), table)
    applied = applied_rows(slots, beta_x_ref[...], beta_y_ref[...], beta_z_ref[...])
    slots_ref[...] = slots
    applied_ref[...] = applied
    message = to_message(applied, table)
    curvature = total(slots[8:40] * applied)
    out_ref[:, 0, :] = message[:, :128]
    out_ref[:, 1, :] = message[:, 128:]
    row = lane_row([aligned_ref[...][:, :1], curvature])
    out_ref[:, 2, :] = jnp.broadcast_to(row, (message.shape[0], 128))
    out_ref[:, 3, :] = jnp.zeros((message.shape[0], 128), jnp.float32)


def read_image(message_ref, table_ref, source_ref, rho_ref, gather_ref, rows_ref):
    tiles = message_ref[...]
    rows = to_modes(row_blocks(from_tiles(tiles, 2), source_ref[...]), table_ref[...])
    sums = jnp.sum(tiles[:, 2, :], axis=0, keepdims=True)
    upward, downward = moments(rows, rho_ref[...])
    gather_ref[0:8] = upward
    gather_ref[8:16] = downward
    gather_ref[16:24] = jnp.broadcast_to(jnp.concatenate([sums, sums], axis=1), (8, 256))
    rows_ref[...] = rows


def second_solve(gather_ref, rows_ref, residual_ref, waves_ref, rho_ref, scale_ref, weights_ref, table_ref, source_ref,
                 out_ref, scalars_ref):
    gathered = gather_ref[...]
    sums = jnp.sum(gathered[:, 16:17, :128], axis=0)
    aligned, curvature = sums[:, 0:1], sums[:, 1:2]
    step = aligned / curvature
    low, high = incoming(gathered[:, 0:8], gathered[:, 8:16], weights_ref[...])
    waves = waves_ref[...]
    rows = residual_ref[...] - step * rows_ref[...]
    modes = solved(rows, waves[0:8] - step * low, waves[8:16] - step * high, rho_ref[...], scale_ref[...])
    scalars_ref[...] = lane_row([total(rows * modes[8:72]), aligned, curvature])
    into_tiles(out_ref, to_rims(modes, table_ref[...], source_ref[...]))


def second_image(message_ref, scalars_ref, applied_ref, table_ref, beta_x_ref, beta_y_ref, beta_z_ref, slots_ref, out_ref):
    slots = from_rims(from_tiles(message_ref[...], 4), table_ref[...])
    slots_ref[...] = slots
    bent = total(slots[8:40] * applied_rows(slots, beta_x_ref[...], beta_y_ref[...], beta_z_ref[...]))
    crossed = total(slots[8:40] * applied_ref[...])
    row = lane_row([scalars_ref[...][:, 0:1], bent, crossed])
    out_ref[...] = jnp.broadcast_to(row[None], out_ref.shape)


def add_parts(parts_ref, out_ref):
    row = jnp.sum(parts_ref[...], axis=0)
    out_ref[...] = jnp.broadcast_to(row[None], out_ref.shape)


def finish(parts_ref, scalars_ref, first_ref, second_ref, beta_x_ref, beta_y_ref, beta_z_ref, provisional_ref, next_ref, pressure_ref):
    sums = jnp.sum(parts_ref[...], axis=0)
    renewed, bent, crossed = sums[:, 0:1], sums[:, 1:2], sums[:, 2:3]
    scalars = scalars_ref[...]
    aligned, curvature = scalars[:, 1:2], scalars[:, 2:3]
    ratio = renewed / aligned
    second_step = renewed / (bent + 2.0 * ratio * crossed + ratio * ratio * curvature)
    first = first_ref[...]
    slots = (aligned / curvature) * first + second_step * (second_ref[...] + ratio * first)
    parts = fluxes(slots, beta_x_ref[...], beta_y_ref[...], beta_z_ref[...])
    for y, (cells, fx, bx, fy, by, fz, bz) in enumerate(parts):
        pressure_ref[y] = cells
        next_ref[0, y] = provisional_ref[0, y] - 0.5 * (fx + bx)
        next_ref[1, y] = provisional_ref[1, y] - 0.5 * (fy + by)
        next_ref[2, y] = provisional_ref[2, y] - 0.5 * (fz + bz)


def run(kernel, outs, *arrays):
    shapes = [jax.ShapeDtypeStruct(shape, jnp.float32) for shape in outs]
    whole = pl.BlockSpec(memory_space=pltpu.VMEM)
    return pl.pallas_call(
        kernel,
        out_shape=shapes,
        in_specs=[whole] * len(arrays),
        out_specs=[whole] * len(outs),
        name=kernel.__name__,
    )(*arrays)


def rim_slots():
    places = [(0, z + 1) for z in range(8)]
    places += [(y + 1, z + 1) for y in range(4) for z in range(8)]
    places += [(5, z + 1) for z in range(8)]
    places += [(y + 1, 0) for y in range(4)] + [(y + 1, 9) for y in range(4)]
    lanes = [[(y * 10 + z) * 8 + k for y, z in places] + [-1] * (64 - len(places)) for k in range(8)]
    return np.array(lanes, np.int32).reshape(1, -1)


def wave_weights(index, rho, count):
    block = jnp.arange(count, dtype=jnp.int32)
    period = 16 * count
    behind = 8 * (index - block) - 7 + jnp.where(block < index, 0, period)
    ahead = 8 * (block - index) - 7 + jnp.where(block > index, 0, period)
    mirrored_low = 8 * (index + block) + 1
    mirrored_high = period - 15 - 8 * (index + block)
    exponents = jnp.stack([behind, mirrored_low, mirrored_high, ahead]).astype(jnp.float32)
    log_rho = jnp.log(rho)
    powers = jnp.exp(exponents[:, :, None, None] * log_rho)
    return powers / (1.0 - jnp.exp(period * log_rho))


def on_device(velocity, fraction, wall_flags):
    rows, cols = (fraction.shape[0], fraction.shape[1])
    rows_devices = lax.axis_size("py")
    cols_devices = lax.axis_size("pz")
    total_rows = rows * rows_devices
    row_index = lax.axis_index("py")
    col_index = lax.axis_index("pz")

    def y_layers(part):
        return part.reshape(9, cols, NX)

    y_head = jnp.concatenate([y_layers(velocity[:, :3]), fraction[:1]], axis=0)
    y_tail = jnp.concatenate([y_layers(velocity[:, -3:]), fraction[-1:]], axis=0)
    y_low, y_high = shifted_pair(y_head, y_tail, "py")

    def z_layers(first, only):
        lanes = jnp.transpose(velocity[:, :, first : first + 3], (0, 2, 1, 3)).reshape(9, rows, NX)
        return jnp.concatenate([lanes, fraction[:, only][None]], axis=0)

    z_low, z_high = shifted_pair(z_layers(0, 0), z_layers(cols - 3, cols - 1), "pz")

    def unlayered(z_rim):
        return jnp.transpose(z_rim[:9].reshape(3, 3, rows, NX), (0, 2, 1, 3))

    provisional = predicted(
        velocity,
        wall_ghosts(velocity, wall_flags),
        jnp.concatenate([y_low[:9].reshape(3, 3, cols, NX), velocity, y_high[:9].reshape(3, 3, cols, NX)], axis=1),
        jnp.concatenate([unlayered(z_low), velocity, unlayered(z_high)], axis=2),
        fraction,
    )

    def density_of(part):
        return 1.0 + (heavy_density - 1.0) * part

    density = density_of(fraction)
    inner_x = 2.0 / (density[:, :, 1:] + density[:, :, :-1])
    beta_x = jnp.concatenate([inner_x, jnp.zeros_like(density[:, :, :1])], axis=2)
    along_y = jnp.concatenate([density_of(y_low[9:]), density, density_of(y_high[9:])], axis=0)
    face = row_index * rows + jnp.arange(rows + 1, dtype=jnp.int32)[:, None, None]
    wall = (face == 0) | (face == total_rows)
    beta_y = jnp.where(wall, 0.0, 2.0 / (along_y[1:] + along_y[:-1]))
    over = jnp.concatenate([density[:, 1:], density_of(z_high[9][:, None])], axis=1)
    under = jnp.concatenate([density_of(z_low[9][:, None]), density[:, :-1]], axis=1)
    layer = col_index * cols + jnp.arange(cols, dtype=jnp.int32)[None, :, None]
    plus_z = jnp.where(layer == cols_devices * cols - 1, 0.0, 2.0 / (density + over))
    minus_z = jnp.where(layer == 0, 0.0, 2.0 / (density + under))
    betas = (beta_x, beta_y, jnp.stack([plus_z, minus_z]))

    normal_x = provisional[0]
    forward_x = jnp.concatenate([normal_x[:, :, 1:], -normal_x[:, :, -1:]], axis=2)
    backward_x = jnp.concatenate([-normal_x[:, :, :1], normal_x[:, :, :-1]], axis=2)
    source_x = -0.5 * (forward_x - backward_x)
    fields = jnp.stack([source_x, provisional[1], provisional[2]])

    part_x = NX // rows_devices
    plain_x = cosine_table(NX).reshape(rows_devices, part_x, NX).transpose(1, 0, 2).reshape(NX, NX)
    plain_y = cosine_table(total_rows).T.reshape(rows_devices, rows, total_rows)
    plain_y = plain_y.transpose(1, 0, 2).reshape(total_rows, total_rows)
    table_x = jnp.asarray(plain_x, dtype=jnp.float32)
    table_y = jnp.asarray(plain_y, dtype=jnp.float32)
    inner = np.arange(256)
    row_source = jnp.asarray((inner % 8 * 32 + inner // 64 * 8 + inner // 8 % 8)[None].astype(np.int32))
    rim_source = jnp.asarray(rim_slots())

    half_x = lax.dynamic_slice(
        jnp.asarray(half_eigenvalue(NX), dtype=jnp.float32), (row_index * part_x,), (part_x,)
    )
    half_y = jnp.asarray(half_eigenvalue(total_rows), dtype=jnp.float32)
    shift = compressibility + half_x[:, None] + half_y[None, :]
    root = jnp.sqrt(shift * (shift + 2.0))
    rho = 1.0 / (1.0 + shift + root)
    scale = 1.0 / root
    weights = wave_weights(col_index, rho, cols_devices)
    here = jnp.arange(cols_devices, dtype=jnp.int32) == col_index
    edge = jnp.broadcast_to(here.astype(jnp.float32)[:, None, None], (cols_devices, part_x, total_rows))

    modes_shape = (64, total_rows)
    wide = (rows_devices, 8, 128)
    narrow = (rows_devices, 4, 128)
    (message,) = run(send_fields, [wide], fields, table_x)
    message = exchange(message, "py")
    gather, modes = run(
        read_fields, [(32, total_rows), modes_shape], message, table_y, row_source, rho
    )
    gather = lax.all_gather(gather, "pz")
    message, residual, waves, aligned = run(
        first_solve,
        [narrow, modes_shape, (16, total_rows), (1, 128)],
        gather, modes, edge, rho, scale, weights, table_y, rim_source,
    )
    message = exchange(message, "py")
    message, first, applied = run(
        first_image, [narrow, (64, NX), (32, NX)], message, aligned, table_x, *betas
    )
    message = exchange(message, "py")
    gather, modes = run(
        read_image, [(24, total_rows), modes_shape], message, table_y, row_source, rho
    )
    gather = lax.all_gather(gather, "pz")
    message, scalars = run(
        second_solve,
        [narrow, (1, 128)],
        gather, modes, residual, waves, rho, scale, weights, table_y, rim_source,
    )
    message = exchange(message, "py")
    second, parts = run(
        second_image, [(64, NX), (rows_devices, 1, 128)], message, scalars, applied, table_x, *betas
    )
    (parts,) = run(add_parts, [(cols_devices, 1, 128)], exchange(parts, "py"))
    parts = exchange(parts, "pz")
    next_velocity, pressure = run(
        finish,
        [velocity.shape, fraction.shape],
        parts, scalars, first, second, *betas, provisional,
    )
    return next_velocity, pressure


def solution(mesh):
    in_specs = (P(None, "py", "pz", None), P("py", "pz", None), P(None, "py", "pz"))
    out_specs = (P(None, "py", "pz", None), P("py", "pz", None))
    return jax.shard_map(
        on_device, mesh=mesh, in_specs=in_specs, out_specs=out_specs, check_vma=False
    )
```

```python
import jax
import jax.numpy as jnp
import numpy as np
from jax import lax
from jax.experimental import pallas as pl
from jax.experimental.pallas import tpu as pltpu
from jax.sharding import PartitionSpec as P

NX = 512


time_step = 0.05
heavy_density = 8.0
light_viscosity = 0.3
heavy_viscosity = 0.6
compressibility = 0.001
mean_inverse = 0.5
weno_epsilon = 1e-06
highest = lax.Precision.HIGHEST


def weno_blend(slope_one, slope_two, slope_three, slope_four, slope_five):
    smooth_one = (
        13.0 / 12.0 * (slope_one - 2.0 * slope_two + slope_three) ** 2
        + 0.25 * (slope_one - 4.0 * slope_two + 3.0 * slope_three) ** 2
    )
    smooth_two = (
        13.0 / 12.0 * (slope_two - 2.0 * slope_three + slope_four) ** 2
        + 0.25 * (slope_two - slope_four) ** 2
    )
    smooth_three = (
        13.0 / 12.0 * (slope_three - 2.0 * slope_four + slope_five) ** 2
        + 0.25 * (3.0 * slope_three - 4.0 * slope_four + slope_five) ** 2
    )
    alpha_one = 0.1 / (weno_epsilon + smooth_one) ** 2
    alpha_two = 0.6 / (weno_epsilon + smooth_two) ** 2
    alpha_three = 0.3 / (weno_epsilon + smooth_three) ** 2
    weight_sum = alpha_one + alpha_two + alpha_three
    blended = alpha_one * (slope_one / 3.0 - 7.0 * slope_two / 6.0 + 11.0 * slope_three / 6.0)
    blended = blended + alpha_two * (-slope_two / 6.0 + 5.0 * slope_three / 6.0 + slope_four / 3.0)
    blended = blended + alpha_three * (
        slope_three / 3.0 + 5.0 * slope_four / 6.0 - slope_five / 6.0
    )
    return blended / weight_sum


def upwind_derivative(padded, direction_axis, advecting):
    length = padded.shape[direction_axis] - 6
    differences = jnp.diff(padded, axis=direction_axis)

    def window(offset):
        return lax.slice_in_dim(differences, offset, offset + length, axis=direction_axis)

    lower_side = weno_blend(window(0), window(1), window(2), window(3), window(4))
    upper_side = weno_blend(window(5), window(4), window(3), window(2), window(1))
    return jnp.where(advecting > 0, lower_side, upper_side)


def predicted(center, along_x, along_y, along_z, fraction):
    slope_x = upwind_derivative(along_x, 3, center[0][None])
    slope_y = upwind_derivative(along_y, 1, center[1][None])
    slope_z = upwind_derivative(along_z, 2, center[2][None])
    transport = center[0] * slope_x + center[1] * slope_y + center[2] * slope_z
    spread = along_x[..., 4:-2] + along_x[..., 2:-4] - 2.0 * center
    spread = spread + (along_y[:, 4:-2] + along_y[:, 2:-4] - 2.0 * center)
    spread = spread + (along_z[:, :, 4:-2] + along_z[:, :, 2:-4] - 2.0 * center)
    density = 1.0 + (heavy_density - 1.0) * fraction
    kinematic = (light_viscosity + (heavy_viscosity - light_viscosity) * fraction) / density
    return center + time_step * (kinematic * spread - transport)


def wall_ghosts(velocity, wall_flags):
    tangential = 2.0 * wall_flags.astype(jnp.float32) - 1.0
    normal = -jnp.ones_like(tangential)
    mirror_signs = jnp.stack([normal, tangential, tangential])
    lower_ghost = velocity[..., :3][..., ::-1] * mirror_signs[:, 0, :, :, None]
    upper_ghost = velocity[..., -3:][..., ::-1] * mirror_signs[:, 1, :, :, None]
    return jnp.concatenate([lower_ghost, velocity, upper_ghost], axis=-1)


def shifted_pair(head, tail, axis):
    count = lax.axis_size(axis)
    up = [(i, i + 1) for i in range(count - 1)]
    down = [(i + 1, i) for i in range(count - 1)]
    return lax.ppermute(tail, axis, up), lax.ppermute(head, axis, down)


def cosine_table(length):
    wave_index = np.arange(length)[:, None]
    position = np.arange(length)[None, :]
    angle = np.pi / (2 * length) * (wave_index * (2 * position + 1) % (4 * length))
    weight = np.where(wave_index == 0, np.sqrt(1.0 / length), np.sqrt(2.0 / length))
    return weight * np.cos(angle)


def half_eigenvalue(length):
    return mean_inverse * 4.0 * np.sin(np.pi * np.arange(length) / (2 * length)) ** 2


def exchange(message, axis):
    return lax.all_to_all(message, axis, split_axis=0, concat_axis=0, tiled=True)


def dot(left, right):
    return lax.dot_general(
        left, right, (((1,), (0,)), ((), ())), precision=highest, preferred_element_type=jnp.float32
    )


def dot_nt(left, right):
    return lax.dot_general(
        left, right, (((1,), (1,)), ((), ())), precision=highest, preferred_element_type=jnp.float32
    )


def rolled(values, shift, axis):
    return pltpu.roll(values, shift % values.shape[axis], axis)


def moved(values, step):
    row = lax.broadcasted_iota(jnp.int32, values.shape, 0)
    edge = 0 if step == 1 else values.shape[0] - 1
    return jnp.where(row == edge, 0.0, rolled(values, step, 0))


def picked(values, source):
    lane = lax.broadcasted_iota(jnp.int32, (values.shape[1], source.shape[1]), 0)
    chosen = jnp.where(lane == source, 1.0, 0.0).astype(jnp.bfloat16)
    total = None
    rest = values
    for _ in range(3):
        piece = rest.astype(jnp.bfloat16)
        rest = rest - piece.astype(jnp.float32)
        term = jnp.dot(piece, chosen, preferred_element_type=jnp.float32)
        total = term if total is None else total + term
    return total


def from_tiles(tiles, count):
    return jnp.concatenate([tiles[:, t, :] for t in range(count)], axis=1)


def into_tiles(ref, values):
    for t in range(values.shape[1] // 128):
        ref[:, t, :] = values[:, 128 * t : 128 * t + 128]


def to_messages(rows, table_x):
    spectral = dot_nt(table_x, rows)
    devices = spectral.shape[0] // 8
    blocks = [spectral[devices * k : devices * k + devices] for k in range(8)]
    return [
        jnp.concatenate([block[:, 32 * c : 32 * c + 32] for block in blocks], axis=1)
        for c in range(rows.shape[0] // 32)
    ]


def row_blocks(messages, source):
    ordered = picked(jnp.concatenate(messages, axis=0), source)
    devices = messages[0].shape[0]
    return [
        [ordered[devices * c : devices * c + devices, 64 * y : 64 * y + 64] for y in range(4)]
        for c in range(len(messages))
    ]


def to_modes(fields, table_y):
    cells = [jnp.concatenate(blocks, axis=0).T for blocks in fields]
    modes = dot(jnp.concatenate(cells, axis=0), table_y)
    return [modes[64 * c : 64 * c + 64] for c in range(len(fields))]


def moments(rows, rho):
    upward = rows[0:8]
    for z in range(1, 8):
        upward = rho * upward + rows[8 * z : 8 * z + 8]
    downward = rows[56:64]
    for z in range(6, -1, -1):
        downward = rho * downward + rows[8 * z : 8 * z + 8]
    return upward, downward


def incoming(upward, downward, weights):
    low = jnp.sum(weights[0] * upward + weights[1] * downward, axis=0)
    high = jnp.sum(weights[2] * upward + weights[3] * downward, axis=0)
    return low, high


def solved(rows, low, high, rho, scale):
    inverse = 1.0 / rho
    cells = [rows[8 * z : 8 * z + 8] for z in range(8)]
    wave = low * inverse
    forward = [wave]
    for z in range(8):
        wave = rho * wave + cells[z]
        forward.append(wave)
    forward.append(rho * wave)
    wave = high
    backward = [high * inverse, high]
    for z in range(7, -1, -1):
        wave = rho * (wave + cells[z])
        backward.append(wave)
    backward = backward[::-1]
    return jnp.concatenate([scale * (f + b) for f, b in zip(forward, backward)], axis=0)


def to_rims(modes, table_y, source):
    rows = dot_nt(table_y, modes)
    devices = rows.shape[0] // 4
    blocks = [rows[devices * y : devices * y + devices] for y in range(4)]
    blocks = [moved(blocks[3], 1), *blocks, moved(blocks[0], -1)]
    return picked(jnp.concatenate(blocks, axis=1), source)


def from_rims(message, table_x):
    stacked = jnp.concatenate([message[:, 64 * k : 64 * k + 64] for k in range(8)], axis=0)
    return dot(stacked.T, table_x)


def fluxes(slots, beta_x, beta_y, beta_z):
    tiles = [slots[8 * y : 8 * y + 8] for y in range(6)]
    flux_y = [beta_y[y] * (tiles[y + 1] - tiles[y]) for y in range(5)]
    layer = lax.broadcasted_iota(jnp.int32, tiles[0].shape, 0)
    results = []
    for y in range(4):
        cells = tiles[y + 1]
        forward_x = beta_x[y] * (rolled(cells, -1, 1) - cells)
        above = jnp.where(layer == 7, slots[52 + y : 53 + y], rolled(cells, -1, 0))
        below = jnp.where(layer == 0, slots[48 + y : 49 + y], rolled(cells, 1, 0))
        results.append(
            (
                cells,
                forward_x,
                rolled(forward_x, 1, 1),
                flux_y[y + 1],
                flux_y[y],
                beta_z[0, y] * (above - cells),
                beta_z[1, y] * (cells - below),
            )
        )
    return results


def applied_rows(slots, beta_x, beta_y, beta_z):
    rows = []
    for cells, fx, bx, fy, by, fz, bz in fluxes(slots, beta_x, beta_y, beta_z):
        rows.append(compressibility * cells - (fx - bx + (fy - by) + (fz - bz)))
    return jnp.concatenate(rows, axis=0)


def total(values):
    return jnp.sum(jnp.sum(values, axis=0, keepdims=True), axis=1, keepdims=True)


def lane_row(values):
    lane = lax.broadcasted_iota(jnp.int32, (1, 128), 1)
    row = jnp.zeros((1, 128), jnp.float32)
    for index, value in enumerate(values):
        row = jnp.where(lane == index, value, row)
    return row


def send_fields(provisional_ref, table_ref, out_ref):
    normal = provisional_ref[0].reshape(32, NX)
    lane = lax.broadcasted_iota(jnp.int32, normal.shape, 1)
    after = jnp.where(lane == NX - 1, -normal, rolled(normal, -1, 1))
    before = jnp.where(lane == 0, -normal, rolled(normal, 1, 1))
    rows = [-0.5 * (after - before)]
    rows += [provisional_ref[c].reshape(32, NX) for c in (1, 2)]
    for c, message in enumerate(to_messages(jnp.concatenate(rows, axis=0), table_ref[...])):
        out_ref[:, 2 * c, :] = message[:, :128]
        out_ref[:, 2 * c + 1, :] = message[:, 128:]


def read_fields(message_ref, table_ref, source_ref, rho_ref, gather_ref, rows_ref):
    tiles = message_ref[...]
    pairs = [
        jnp.concatenate([tiles[:, 2 * c, :], tiles[:, 2 * c + 1, :]], axis=1) for c in range(3)
    ]
    across, along_y, along_z = row_blocks(pairs, source_ref[...])
    after = [*along_y[1:], moved(along_y[0], -1)]
    before = [moved(along_y[3], 1), *along_y[:3]]
    across = [s - 0.5 * (a - b) for s, a, b in zip(across, after, before)]
    joined, third = to_modes([across, along_z], table_ref[...])
    zero = jnp.zeros_like(third[:8])
    above = jnp.concatenate([third[8:], zero], axis=0)
    below = jnp.concatenate([zero, third[:-8]], axis=0)
    rows = joined - 0.5 * (above - below)
    rho = rho_ref[...]
    upward, downward = moments(rows, rho)
    gather_ref[0:8] = upward
    gather_ref[8:16] = downward
    gather_ref[16:24] = third[0:8]
    gather_ref[24:32] = third[56:64]
    rows_ref[...] = rows


def first_solve(place_ref, gather_ref, rows_ref, rho_ref, scale_ref, weights_ref, table_ref, source_ref,
                out_ref, residual_ref, waves_ref, aligned_ref):
    rho = rho_ref[...]
    power = rho * rho
    power = power * power * power * rho
    gathered = gather_ref[...]
    first, last = gathered[:, 16:24], gathered[:, 24:32]
    zero = jnp.zeros_like(first[:1])
    under = 0.5 * jnp.concatenate([zero, last[:-1]], axis=0)
    over = -0.5 * jnp.concatenate([first[1:], zero], axis=0)
    upward = gathered[:, 0:8] + power * under + over
    downward = gathered[:, 8:16] + under + power * over
    low, high = incoming(upward, downward, weights_ref[...])
    mine = lax.broadcasted_iota(jnp.int32, under.shape, 0) == place_ref[0]
    rows = rows_ref[...]
    rows = jnp.concatenate(
        [
            rows[:8] + jnp.sum(jnp.where(mine, under, 0.0), axis=0),
            rows[8:56],
            rows[56:] + jnp.sum(jnp.where(mine, over, 0.0), axis=0),
        ],
        axis=0,
    )
    modes = solved(rows, low, high, rho, scale_ref[...])
    aligned_ref[...] = lane_row([total(rows * modes[8:72])])
    residual_ref[...] = rows
    waves_ref[0:8] = low
    waves_ref[8:16] = high
    into_tiles(out_ref, to_rims(modes, table_ref[...], source_ref[...]))


def first_image(message_ref, aligned_ref, table_ref, beta_x_ref, beta_y_ref, beta_z_ref, out_ref, slots_ref, applied_ref):
    table = table_ref[...]
    slots = from_rims(from_tiles(message_ref[...], 4), table)
    applied = applied_rows(slots, beta_x_ref[...], beta_y_ref[...], beta_z_ref[...])
    slots_ref[...] = slots
    applied_ref[...] = applied
    (message,) = to_messages(applied, table)
    curvature = total(slots[8:40] * applied)
    out_ref[:, 0, :] = message[:, :128]
    out_ref[:, 1, :] = message[:, 128:]
    row = lane_row([aligned_ref[...][:, :1], curvature])
    out_ref[:, 2, :] = jnp.broadcast_to(row, (message.shape[0], 128))
    out_ref[:, 3, :] = jnp.zeros((message.shape[0], 128), jnp.float32)


def read_image(message_ref, table_ref, source_ref, rho_ref, gather_ref, rows_ref):
    tiles = message_ref[...]
    (rows,) = to_modes(row_blocks([from_tiles(tiles, 2)], source_ref[...]), table_ref[...])
    sums = jnp.sum(tiles[:, 2, :], axis=0, keepdims=True)
    upward, downward = moments(rows, rho_ref[...])
    gather_ref[0:8] = upward
    gather_ref[8:16] = downward
    gather_ref[16:24] = jnp.broadcast_to(jnp.concatenate([sums, sums], axis=1), (8, 256))
    rows_ref[...] = rows


def second_solve(gather_ref, rows_ref, residual_ref, waves_ref, rho_ref, scale_ref, weights_ref, table_ref, source_ref,
                 out_ref, scalars_ref):
    gathered = gather_ref[...]
    sums = jnp.sum(gathered[:, 16:17, :128], axis=0)
    aligned, curvature = sums[:, 0:1], sums[:, 1:2]
    step = aligned / curvature
    low, high = incoming(gathered[:, 0:8], gathered[:, 8:16], weights_ref[...])
    waves = waves_ref[...]
    rows = residual_ref[...] - step * rows_ref[...]
    modes = solved(rows, waves[0:8] - step * low, waves[8:16] - step * high, rho_ref[...], scale_ref[...])
    scalars_ref[...] = lane_row([total(rows * modes[8:72]), aligned, curvature])
    into_tiles(out_ref, to_rims(modes, table_ref[...], source_ref[...]))


def second_image(message_ref, scalars_ref, applied_ref, table_ref, beta_x_ref, beta_y_ref, beta_z_ref, slots_ref, out_ref):
    slots = from_rims(from_tiles(message_ref[...], 4), table_ref[...])
    slots_ref[...] = slots
    bent = total(slots[8:40] * applied_rows(slots, beta_x_ref[...], beta_y_ref[...], beta_z_ref[...]))
    crossed = total(slots[8:40] * applied_ref[...])
    row = lane_row([scalars_ref[...][:, 0:1], bent, crossed])
    out_ref[...] = jnp.broadcast_to(row[None], out_ref.shape)


def add_parts(parts_ref, out_ref):
    row = jnp.sum(parts_ref[...], axis=0)
    out_ref[...] = jnp.broadcast_to(row[None], out_ref.shape)


def finish(parts_ref, scalars_ref, first_ref, second_ref, beta_x_ref, beta_y_ref, beta_z_ref, provisional_ref, next_ref, pressure_ref):
    sums = jnp.sum(parts_ref[...], axis=0)
    renewed, bent, crossed = sums[:, 0:1], sums[:, 1:2], sums[:, 2:3]
    scalars = scalars_ref[...]
    aligned, curvature = scalars[:, 1:2], scalars[:, 2:3]
    ratio = renewed / aligned
    second_step = renewed / (bent + 2.0 * ratio * crossed + ratio * ratio * curvature)
    first = first_ref[...]
    slots = (aligned / curvature) * first + second_step * (second_ref[...] + ratio * first)
    parts = fluxes(slots, beta_x_ref[...], beta_y_ref[...], beta_z_ref[...])
    for y, (cells, fx, bx, fy, by, fz, bz) in enumerate(parts):
        pressure_ref[y] = cells
        next_ref[0, y] = provisional_ref[0, y] - 0.5 * (fx + bx)
        next_ref[1, y] = provisional_ref[1, y] - 0.5 * (fy + by)
        next_ref[2, y] = provisional_ref[2, y] - 0.5 * (fz + bz)


def run(kernel, outs, *arrays, last=False):
    whole = pl.BlockSpec(memory_space=pltpu.VMEM)
    scalar = pl.BlockSpec(memory_space=pltpu.SMEM)
    scalars = [array.ndim == 1 for array in arrays]
    kept = jax.ShapeDtypeStruct if last else pltpu.VMEM
    return pl.pallas_call(
        kernel,
        out_shape=[kept(shape, jnp.float32) for shape in outs],
        in_specs=[scalar if small else whole for small in scalars],
        out_specs=[whole] * len(outs),
        compiler_params=pltpu.CompilerParams(vmem_limit_bytes=8 << 20),
    )(
        *[
            array if small else pltpu.with_memory_space_constraint(array, pltpu.VMEM)
            for array, small in zip(arrays, scalars)
        ]
    )


def rim_slots():
    places = [(0, z + 1) for z in range(8)]
    places += [(y + 1, z + 1) for y in range(4) for z in range(8)]
    places += [(5, z + 1) for z in range(8)]
    places += [(y + 1, 0) for y in range(4)] + [(y + 1, 9) for y in range(4)]
    lanes = [[(y * 10 + z) * 8 + k for y, z in places] + [-1] * (64 - len(places)) for k in range(8)]
    return np.array(lanes, np.int32).reshape(1, -1)


def wave_weights(index, rho, count):
    block = jnp.arange(count, dtype=jnp.int32)
    period = 16 * count
    behind = 8 * (index - block) - 7 + jnp.where(block < index, 0, period)
    ahead = 8 * (block - index) - 7 + jnp.where(block > index, 0, period)
    mirrored_low = 8 * (index + block) + 1
    mirrored_high = period - 15 - 8 * (index + block)
    exponents = jnp.stack([behind, mirrored_low, mirrored_high, ahead]).astype(jnp.float32)
    log_rho = jnp.log(rho)
    powers = jnp.exp(exponents[:, :, None, None] * log_rho)
    return powers / (1.0 - jnp.exp(period * log_rho))


def on_device(velocity, fraction, wall_flags):
    rows, cols = (fraction.shape[0], fraction.shape[1])
    rows_devices = lax.axis_size("py")
    cols_devices = lax.axis_size("pz")
    total_rows = rows * rows_devices
    row_index = lax.axis_index("py")
    col_index = lax.axis_index("pz")

    def y_layers(part):
        return part.reshape(9, cols, NX)

    y_head = jnp.concatenate([y_layers(velocity[:, :3]), fraction[:1]], axis=0)
    y_tail = jnp.concatenate([y_layers(velocity[:, -3:]), fraction[-1:]], axis=0)
    y_low, y_high = shifted_pair(y_head, y_tail, "py")

    def z_layers(first, only):
        lanes = jnp.transpose(velocity[:, :, first : first + 3], (0, 2, 1, 3)).reshape(9, rows, NX)
        return jnp.concatenate([lanes, fraction[:, only][None]], axis=0)

    z_low, z_high = shifted_pair(z_layers(0, 0), z_layers(cols - 3, cols - 1), "pz")

    def unlayered(z_rim):
        return jnp.transpose(z_rim[:9].reshape(3, 3, rows, NX), (0, 2, 1, 3))

    provisional = predicted(
        velocity,
        wall_ghosts(velocity, wall_flags),
        jnp.concatenate([y_low[:9].reshape(3, 3, cols, NX), velocity, y_high[:9].reshape(3, 3, cols, NX)], axis=1),
        jnp.concatenate([unlayered(z_low), velocity, unlayered(z_high)], axis=2),
        fraction,
    )

    def density_of(part):
        return 1.0 + (heavy_density - 1.0) * part

    density = density_of(fraction)
    inner_x = 2.0 / (density[:, :, 1:] + density[:, :, :-1])
    beta_x = jnp.concatenate([inner_x, jnp.zeros_like(density[:, :, :1])], axis=2)
    along_y = jnp.concatenate([density_of(y_low[9:]), density, density_of(y_high[9:])], axis=0)
    face = row_index * rows + jnp.arange(rows + 1, dtype=jnp.int32)[:, None, None]
    wall = (face == 0) | (face == total_rows)
    beta_y = jnp.where(wall, 0.0, 2.0 / (along_y[1:] + along_y[:-1]))
    over = jnp.concatenate([density[:, 1:], density_of(z_high[9][:, None])], axis=1)
    under = jnp.concatenate([density_of(z_low[9][:, None]), density[:, :-1]], axis=1)
    layer = col_index * cols + jnp.arange(cols, dtype=jnp.int32)[None, :, None]
    plus_z = jnp.where(layer == cols_devices * cols - 1, 0.0, 2.0 / (density + over))
    minus_z = jnp.where(layer == 0, 0.0, 2.0 / (density + under))
    betas = (beta_x, beta_y, jnp.stack([plus_z, minus_z]))

    part_x = NX // rows_devices
    plain_x = cosine_table(NX).reshape(rows_devices, part_x, NX).transpose(1, 0, 2).reshape(NX, NX)
    plain_y = cosine_table(total_rows).T.reshape(rows_devices, rows, total_rows)
    plain_y = plain_y.transpose(1, 0, 2).reshape(total_rows, total_rows)
    table_x = jnp.asarray(plain_x, dtype=jnp.float32)
    table_y = jnp.asarray(plain_y, dtype=jnp.float32)
    inner = np.arange(256)
    row_source = jnp.asarray((inner % 8 * 32 + inner // 64 * 8 + inner // 8 % 8)[None].astype(np.int32))
    rim_source = jnp.asarray(rim_slots())

    half_x = lax.dynamic_slice(
        jnp.asarray(half_eigenvalue(NX), dtype=jnp.float32), (row_index * part_x,), (part_x,)
    )
    half_y = jnp.asarray(half_eigenvalue(total_rows), dtype=jnp.float32)
    shift = compressibility + half_x[:, None] + half_y[None, :]
    root = jnp.sqrt(shift * (shift + 2.0))
    rho = 1.0 / (1.0 + shift + root)
    scale = 1.0 / root
    weights = wave_weights(col_index, rho, cols_devices)
    place = col_index.astype(jnp.int32).reshape(1)

    modes_shape = (64, total_rows)
    wide = (rows_devices, 8, 128)
    narrow = (rows_devices, 4, 128)
    (message,) = run(send_fields, [wide], provisional, table_x)
    message = exchange(message, "py")
    gather, modes = run(
        read_fields, [(32, total_rows), modes_shape], message, table_y, row_source, rho
    )
    gather = lax.all_gather(gather, "pz")
    message, residual, waves, aligned = run(
        first_solve,
        [narrow, modes_shape, (16, total_rows), (1, 128)],
        place, gather, modes, rho, scale, weights, table_y, rim_source,
    )
    message = exchange(message, "py")
    message, first, applied = run(
        first_image, [narrow, (64, NX), (32, NX)], message, aligned, table_x, *betas
    )
    message = exchange(message, "py")
    gather, modes = run(
        read_image, [(24, total_rows), modes_shape], message, table_y, row_source, rho
    )
    gather = lax.all_gather(gather, "pz")
    message, scalars = run(
        second_solve,
        [narrow, (1, 128)],
        gather, modes, residual, waves, rho, scale, weights, table_y, rim_source,
    )
    message = exchange(message, "py")
    second, parts = run(
        second_image, [(64, NX), (rows_devices, 1, 128)], message, scalars, applied, table_x, *betas
    )
    (parts,) = run(add_parts, [(cols_devices, 1, 128)], exchange(parts, "py"))
    parts = exchange(parts, "pz")
    next_velocity, pressure = run(
        finish,
        [velocity.shape, fraction.shape],
        parts, scalars, first, second, *betas, provisional,
        last=True,
    )
    return next_velocity, pressure


def solution(mesh):
    in_specs = (P(None, "py", "pz", None), P("py", "pz", None), P(None, "py", "pz"))
    out_specs = (P(None, "py", "pz", None), P("py", "pz", None))
    return jax.shard_map(
        on_device, mesh=mesh, in_specs=in_specs, out_specs=out_specs, check_vma=False
    )
```

```python
import jax
import jax.numpy as jnp
import numpy as np
from jax import lax
from jax.experimental import pallas as pl
from jax.experimental.pallas import tpu as pltpu
from jax.sharding import Mesh, PartitionSpec as P

NX = 512


time_step = 0.05
heavy_density = 8.0
light_viscosity = 0.3
heavy_viscosity = 0.6
compressibility = 0.001
mean_inverse = 0.5
weno_epsilon = 1e-06
highest = lax.Precision.HIGHEST


def weno_blend(slope_one, slope_two, slope_three, slope_four, slope_five):
    smooth_one = (
        13.0 / 12.0 * (slope_one - 2.0 * slope_two + slope_three) ** 2
        + 0.25 * (slope_one - 4.0 * slope_two + 3.0 * slope_three) ** 2
    )
    smooth_two = (
        13.0 / 12.0 * (slope_two - 2.0 * slope_three + slope_four) ** 2
        + 0.25 * (slope_two - slope_four) ** 2
    )
    smooth_three = (
        13.0 / 12.0 * (slope_three - 2.0 * slope_four + slope_five) ** 2
        + 0.25 * (3.0 * slope_three - 4.0 * slope_four + slope_five) ** 2
    )
    alpha_one = 0.1 / (weno_epsilon + smooth_one) ** 2
    alpha_two = 0.6 / (weno_epsilon + smooth_two) ** 2
    alpha_three = 0.3 / (weno_epsilon + smooth_three) ** 2
    weight_sum = alpha_one + alpha_two + alpha_three
    blended = alpha_one * (slope_one / 3.0 - 7.0 * slope_two / 6.0 + 11.0 * slope_three / 6.0)
    blended = blended + alpha_two * (-slope_two / 6.0 + 5.0 * slope_three / 6.0 + slope_four / 3.0)
    blended = blended + alpha_three * (
        slope_three / 3.0 + 5.0 * slope_four / 6.0 - slope_five / 6.0
    )
    return blended / weight_sum


def upwind_derivative(padded, direction_axis, advecting):
    length = padded.shape[direction_axis] - 6
    differences = jnp.diff(padded, axis=direction_axis)

    def window(offset):
        return lax.slice_in_dim(differences, offset, offset + length, axis=direction_axis)

    lower_side = weno_blend(window(0), window(1), window(2), window(3), window(4))
    upper_side = weno_blend(window(5), window(4), window(3), window(2), window(1))
    return jnp.where(advecting > 0, lower_side, upper_side)


def predicted(center, along_x, along_y, along_z, fraction):
    slope_x = upwind_derivative(along_x, 3, center[0][None])
    slope_y = upwind_derivative(along_y, 1, center[1][None])
    slope_z = upwind_derivative(along_z, 2, center[2][None])
    transport = center[0] * slope_x + center[1] * slope_y + center[2] * slope_z
    spread = along_x[..., 4:-2] + along_x[..., 2:-4] - 2.0 * center
    spread = spread + (along_y[:, 4:-2] + along_y[:, 2:-4] - 2.0 * center)
    spread = spread + (along_z[:, :, 4:-2] + along_z[:, :, 2:-4] - 2.0 * center)
    density = 1.0 + (heavy_density - 1.0) * fraction
    kinematic = (light_viscosity + (heavy_viscosity - light_viscosity) * fraction) / density
    return center + time_step * (kinematic * spread - transport)


def wall_ghosts(velocity, wall_flags):
    tangential = 2.0 * wall_flags.astype(jnp.float32) - 1.0
    normal = -jnp.ones_like(tangential)
    mirror_signs = jnp.stack([normal, tangential, tangential])
    lower_ghost = velocity[..., :3][..., ::-1] * mirror_signs[:, 0, :, :, None]
    upper_ghost = velocity[..., -3:][..., ::-1] * mirror_signs[:, 1, :, :, None]
    return jnp.concatenate([lower_ghost, velocity, upper_ghost], axis=-1)


def shifted_pair(head, tail, axis):
    count = lax.axis_size(axis)
    up = [(i, i + 1) for i in range(count - 1)]
    down = [(i + 1, i) for i in range(count - 1)]
    return lax.ppermute(tail, axis, up), lax.ppermute(head, axis, down)


def cosine_table(length):
    wave_index = np.arange(length)[:, None]
    position = np.arange(length)[None, :]
    angle = np.pi / (2 * length) * (wave_index * (2 * position + 1) % (4 * length))
    weight = np.where(wave_index == 0, np.sqrt(1.0 / length), np.sqrt(2.0 / length))
    return weight * np.cos(angle)


def half_eigenvalue(length):
    return mean_inverse * 4.0 * np.sin(np.pi * np.arange(length) / (2 * length)) ** 2


def exchange(message, axis):
    return lax.all_to_all(message, axis, split_axis=0, concat_axis=0, tiled=True)


def dot(left, right):
    return lax.dot_general(
        left, right, (((1,), (0,)), ((), ())), precision=highest, preferred_element_type=jnp.float32
    )


def dot_nt(left, right):
    return lax.dot_general(
        left, right, (((1,), (1,)), ((), ())), precision=highest, preferred_element_type=jnp.float32
    )


def rolled(values, shift, axis):
    return pltpu.roll(values, shift % values.shape[axis], axis)


def moved(values, step):
    row = lax.broadcasted_iota(jnp.int32, values.shape, 0)
    edge = 0 if step == 1 else values.shape[0] - 1
    return jnp.where(row == edge, 0.0, rolled(values, step, 0))


def picked(values, source):
    lane = lax.broadcasted_iota(jnp.int32, (values.shape[1], source.shape[1]), 0)
    chosen = jnp.where(lane == source, 1.0, 0.0).astype(jnp.bfloat16)
    total = None
    rest = values
    for _ in range(3):
        piece = rest.astype(jnp.bfloat16)
        rest = rest - piece.astype(jnp.float32)
        term = jnp.dot(piece, chosen, preferred_element_type=jnp.float32)
        total = term if total is None else total + term
    return total


def from_tiles(tiles, count):
    return jnp.concatenate([tiles[:, t, :] for t in range(count)], axis=1)


def into_tiles(ref, values):
    for t in range(values.shape[1] // 128):
        ref[:, t, :] = values[:, 128 * t : 128 * t + 128]


def to_messages(rows, table_x):
    spectral = dot_nt(table_x, rows)
    devices = spectral.shape[0] // 4
    blocks = [spectral[devices * k : devices * k + devices] for k in range(4)]
    return [
        jnp.concatenate([block[:, 32 * c : 32 * c + 32] for block in blocks], axis=1)
        for c in range(rows.shape[0] // 32)
    ]


def row_blocks(messages, source):
    ordered = picked(jnp.concatenate(messages, axis=0), source)
    devices = messages[0].shape[0]
    return [
        [ordered[devices * c : devices * c + devices, 64 * y : 64 * y + 64] for y in range(4)]
        for c in range(len(messages))
    ]


def to_modes(fields, table_y):
    cells = [jnp.concatenate(blocks, axis=0).T for blocks in fields]
    modes = dot(jnp.concatenate(cells, axis=0), table_y)
    layers = [
        jnp.concatenate([modes[4 * r : 4 * r + 4, :128], modes[4 * r : 4 * r + 4, 128:]], axis=0)
        for r in range(16 * len(fields))
    ]
    return [layers[16 * c : 16 * c + 16] for c in range(len(fields))]


def from_layers(layers):
    return jnp.concatenate(
        [jnp.concatenate([layer[:4], layer[4:]], axis=1) for layer in layers], axis=0
    )


def moments(layers, rho):
    upward = layers[0]
    for layer in layers[1:]:
        upward = rho * upward + layer
    downward = layers[-1]
    for layer in layers[-2::-1]:
        downward = rho * downward + layer
    return upward, downward


def incoming(upward, downward, weights):
    low = jnp.sum(weights[0] * upward + weights[1] * downward, axis=0)
    high = jnp.sum(weights[2] * upward + weights[3] * downward, axis=0)
    return low, high


def solved(layers, low, high, rho, scale):
    inverse = 1.0 / rho
    wave = low * inverse
    forward = [wave]
    for layer in layers:
        wave = rho * wave + layer
        forward.append(wave)
    forward.append(rho * wave)
    wave = high
    backward = [high * inverse, high]
    for layer in layers[::-1]:
        wave = rho * (wave + layer)
        backward.append(wave)
    backward = backward[::-1]
    return [scale * (f + b) for f, b in zip(forward, backward)]


def layers_total(left, right):
    product = left[0] * right[0]
    for one, other in zip(left[1:], right[1:]):
        product = product + one * other
    return total(product)


def send_rims(out_ref, layers, table_y, source):
    rows = dot_nt(table_y, from_layers(layers))
    devices = rows.shape[0] // 4
    blocks = [rows[devices * y : devices * y + devices] for y in range(4)]
    blocks = [moved(blocks[3], 1), *blocks, moved(blocks[0], -1)]
    into_tiles(out_ref, picked(jnp.concatenate(blocks, axis=1), source))


def from_rims(message, table_x):
    stacked = jnp.concatenate([message[:, 64 * k : 64 * k + 64] for k in range(4)], axis=0)
    return dot(stacked.T, table_x)


def fluxes(slots, beta_x, beta_y, beta_z):
    tiles = [slots[8 * y : 8 * y + 8] for y in range(6)]
    flux_y = [beta_y[y] * (tiles[y + 1] - tiles[y]) for y in range(5)]
    layer = lax.broadcasted_iota(jnp.int32, tiles[0].shape, 0)
    results = []
    for y in range(4):
        cells = tiles[y + 1]
        forward_x = beta_x[y] * (rolled(cells, -1, 1) - cells)
        above = jnp.where(layer == 7, slots[52 + y : 53 + y], rolled(cells, -1, 0))
        below = jnp.where(layer == 0, slots[48 + y : 49 + y], rolled(cells, 1, 0))
        results.append(
            (
                cells,
                forward_x,
                rolled(forward_x, 1, 1),
                flux_y[y + 1],
                flux_y[y],
                beta_z[0, y] * (above - cells),
                beta_z[1, y] * (cells - below),
            )
        )
    return results


def applied_rows(slots, beta_x, beta_y, beta_z):
    rows = []
    for cells, fx, bx, fy, by, fz, bz in fluxes(slots, beta_x, beta_y, beta_z):
        rows.append(compressibility * cells - (fx - bx + (fy - by) + (fz - bz)))
    return jnp.concatenate(rows, axis=0)


def total(values):
    return jnp.sum(jnp.sum(values, axis=0, keepdims=True), axis=1, keepdims=True)


def lane_row(values):
    lane = lax.broadcasted_iota(jnp.int32, (1, 128), 1)
    row = jnp.zeros((1, 128), jnp.float32)
    for index, value in enumerate(values):
        row = jnp.where(lane == index, value, row)
    return row


def send_fields(provisional_ref, table_ref, out_ref):
    normal = provisional_ref[0].reshape(32, NX)
    lane = lax.broadcasted_iota(jnp.int32, normal.shape, 1)
    after = jnp.where(lane == NX - 1, -normal, rolled(normal, -1, 1))
    before = jnp.where(lane == 0, -normal, rolled(normal, 1, 1))
    rows = [-0.5 * (after - before)]
    rows += [provisional_ref[c].reshape(32, NX) for c in (1, 2)]
    for c, message in enumerate(to_messages(jnp.concatenate(rows, axis=0), table_ref[...])):
        out_ref[:, c, :] = message
    out_ref[:, 3, :] = jnp.zeros_like(message)


def read_fields(message_ref, table_ref, source_ref, rho_ref, gather_ref, layers_ref):
    tiles = message_ref[...]
    pairs = [jnp.concatenate([tiles[:, c, :], tiles[:, c + 4, :]], axis=1) for c in range(3)]
    across, along_y, along_z = row_blocks(pairs, source_ref[...])
    after = [*along_y[1:], moved(along_y[0], -1)]
    before = [moved(along_y[3], 1), *along_y[:3]]
    across = [s - 0.5 * (a - b) for s, a, b in zip(across, after, before)]
    joined, third = to_modes([across, along_z], table_ref[...])
    zero = jnp.zeros_like(third[0])
    above = [*third[1:], zero]
    below = [zero, *third[:-1]]
    layers = [j - 0.5 * (a - b) for j, a, b in zip(joined, above, below)]
    upward, downward = moments(layers, rho_ref[...])
    for device in range(gather_ref.shape[0]):
        gather_ref[device, 0:8] = upward
        gather_ref[device, 8:16] = downward
        gather_ref[device, 16:24] = third[0]
        gather_ref[device, 24:32] = third[-1]
    for z, layer in enumerate(layers):
        layers_ref[z] = layer


def first_solve(place_ref, gather_ref, layers_ref, rho_ref, scale_ref, weights_ref, table_ref, source_ref,
                out_ref, residual_ref, waves_ref, aligned_ref):
    rho = rho_ref[...]
    square = rho * rho
    fourth = square * square
    power = fourth * fourth * fourth * square * rho
    gathered = gather_ref[...]
    first, last = gathered[:, 16:24], gathered[:, 24:32]
    zero = jnp.zeros_like(first[:1])
    under = 0.5 * jnp.concatenate([zero, last[:-1]], axis=0)
    over = -0.5 * jnp.concatenate([first[1:], zero], axis=0)
    upward = gathered[:, 0:8] + power * under + over
    downward = gathered[:, 8:16] + under + power * over
    low, high = incoming(upward, downward, weights_ref[...])
    mine = lax.broadcasted_iota(jnp.int32, under.shape, 0) == place_ref[0]
    layers = [layers_ref[z] for z in range(16)]
    layers[0] = layers[0] + jnp.sum(jnp.where(mine, under, 0.0), axis=0)
    layers[15] = layers[15] + jnp.sum(jnp.where(mine, over, 0.0), axis=0)
    modes = solved(layers, low, high, rho, scale_ref[...])
    aligned_ref[...] = lane_row([layers_total(layers, modes[1:-1])])
    for z, layer in enumerate(layers):
        residual_ref[z] = layer
    waves_ref[0] = low
    waves_ref[1] = high
    send_rims(out_ref, modes, table_ref[...], source_ref[...])


def first_image(message_ref, aligned_ref, table_ref, beta_x_ref, beta_y_ref, beta_z_ref, out_ref, slots_ref, applied_ref):
    table = table_ref[...]
    slots = from_rims(from_tiles(message_ref[...], 2), table)
    applied = applied_rows(slots, beta_x_ref[...], beta_y_ref[...], beta_z_ref[...])
    slots_ref[...] = slots
    applied_ref[...] = applied
    (message,) = to_messages(applied, table)
    curvature = total(slots[8:40] * applied)
    out_ref[:, 0, :] = message
    row = lane_row([aligned_ref[...][:, :1], curvature])
    out_ref[:, 1, :] = jnp.broadcast_to(row, message.shape)


def read_image(message_ref, table_ref, source_ref, rho_ref, gather_ref, layers_ref):
    tiles = message_ref[...]
    pair = jnp.concatenate([tiles[:, 0, :], tiles[:, 2, :]], axis=1)
    (layers,) = to_modes(row_blocks([pair], source_ref[...]), table_ref[...])
    sums = jnp.sum(tiles[:, 1, :] + tiles[:, 3, :], axis=0, keepdims=True)
    upward, downward = moments(layers, rho_ref[...])
    sums = jnp.broadcast_to(sums, upward.shape)
    for device in range(gather_ref.shape[0]):
        gather_ref[device, 0:8] = upward
        gather_ref[device, 8:16] = downward
        gather_ref[device, 16:24] = sums
    for z, layer in enumerate(layers):
        layers_ref[z] = layer


def second_solve(gather_ref, layers_ref, residual_ref, waves_ref, rho_ref, scale_ref, weights_ref, table_ref, source_ref,
                 out_ref, scalars_ref):
    gathered = gather_ref[...]
    sums = jnp.sum(gathered[:, 16:24], axis=0)[:1]
    aligned, curvature = sums[:, 0:1], sums[:, 1:2]
    step = aligned / curvature
    low, high = incoming(gathered[:, 0:8], gathered[:, 8:16], weights_ref[...])
    layers = [residual_ref[z] - step * layers_ref[z] for z in range(16)]
    modes = solved(layers, waves_ref[0] - step * low, waves_ref[1] - step * high, rho_ref[...], scale_ref[...])
    scalars_ref[...] = lane_row([layers_total(layers, modes[1:-1]), aligned, curvature])
    send_rims(out_ref, modes, table_ref[...], source_ref[...])


def second_image(message_ref, scalars_ref, applied_ref, table_ref, beta_x_ref, beta_y_ref, beta_z_ref, slots_ref, out_ref):
    slots = from_rims(from_tiles(message_ref[...], 2), table_ref[...])
    slots_ref[...] = slots
    bent = total(slots[8:40] * applied_rows(slots, beta_x_ref[...], beta_y_ref[...], beta_z_ref[...]))
    crossed = total(slots[8:40] * applied_ref[...])
    row = lane_row([scalars_ref[...][:, 0:1], bent, crossed])
    out_ref[...] = jnp.broadcast_to(row[None], out_ref.shape)


def add_parts(parts_ref, out_ref):
    row = jnp.sum(parts_ref[...], axis=0)
    out_ref[...] = jnp.broadcast_to(row[None], out_ref.shape)


def finish(parts_ref, scalars_ref, first_ref, second_ref, beta_x_ref, beta_y_ref, beta_z_ref, provisional_ref, next_ref, pressure_ref):
    sums = jnp.sum(parts_ref[...], axis=0)
    renewed, bent, crossed = sums[:, 0:1], sums[:, 1:2], sums[:, 2:3]
    scalars = scalars_ref[...]
    aligned, curvature = scalars[:, 1:2], scalars[:, 2:3]
    ratio = renewed / aligned
    second_step = renewed / (bent + 2.0 * ratio * crossed + ratio * ratio * curvature)
    first = first_ref[...]
    slots = (aligned / curvature) * first + second_step * (second_ref[...] + ratio * first)
    parts = fluxes(slots, beta_x_ref[...], beta_y_ref[...], beta_z_ref[...])
    for y, (cells, fx, bx, fy, by, fz, bz) in enumerate(parts):
        pressure_ref[y] = cells
        next_ref[0, y] = provisional_ref[0, y] - 0.5 * (fx + bx)
        next_ref[1, y] = provisional_ref[1, y] - 0.5 * (fy + by)
        next_ref[2, y] = provisional_ref[2, y] - 0.5 * (fz + bz)


def run(kernel, outs, *arrays, last=False):
    whole = pl.BlockSpec(memory_space=pltpu.VMEM)
    scalar = pl.BlockSpec(memory_space=pltpu.SMEM)
    scalars = [array.ndim == 1 for array in arrays]
    kept = jax.ShapeDtypeStruct if last else pltpu.VMEM
    return pl.pallas_call(
        kernel,
        out_shape=[kept(shape, jnp.float32) for shape in outs],
        in_specs=[scalar if small else whole for small in scalars],
        out_specs=[whole] * len(outs),
        compiler_params=pltpu.CompilerParams(vmem_limit_bytes=8 << 20),
    )(
        *[
            array if small else pltpu.with_memory_space_constraint(array, pltpu.VMEM)
            for array, small in zip(arrays, scalars)
        ]
    )


def rim_slots():
    places = [(0, z + 1) for z in range(8)]
    places += [(y + 1, z + 1) for y in range(4) for z in range(8)]
    places += [(5, z + 1) for z in range(8)]
    places += [(y + 1, 0) for y in range(4)] + [(y + 1, 9) for y in range(4)]
    lanes = [
        [(y * 18 + 8 * core + z) * 4 + k for y, z in places] + [-1] * (64 - len(places))
        for core in range(2)
        for k in range(4)
    ]
    return np.array(lanes, np.int32).reshape(1, -1)


def wave_weights(index, rho, count, size):
    block = jnp.arange(count, dtype=jnp.int32)
    period = 2 * size * count
    behind = size * (index - block) - size + 1 + jnp.where(block < index, 0, period)
    ahead = size * (block - index) - size + 1 + jnp.where(block > index, 0, period)
    mirrored_low = size * (index + block) + 1
    mirrored_high = period - 2 * size + 1 - size * (index + block)
    exponents = jnp.stack([behind, mirrored_low, mirrored_high, ahead]).astype(jnp.float32)
    log_rho = jnp.log(rho)
    powers = jnp.exp(exponents[:, :, None, None] * log_rho)
    return powers / (1.0 - jnp.exp(period * log_rho))


def on_device(velocity, fraction, wall_flags):
    rows, cols = (fraction.shape[0], fraction.shape[1])
    rows_devices = lax.axis_size("py")
    chips = lax.axis_size("px")
    cores = lax.axis_size("core")
    cols_devices = chips * cores
    total_rows = rows * rows_devices
    row_index = lax.axis_index("py")
    chip_index = lax.axis_index("px")
    core_index = lax.axis_index("core")
    col_index = chip_index * cores + core_index

    def y_layers(part):
        return part.reshape(9, cols, NX)

    y_head = jnp.concatenate([y_layers(velocity[:, :3]), fraction[:1]], axis=0)
    y_tail = jnp.concatenate([y_layers(velocity[:, -3:]), fraction[-1:]], axis=0)
    y_low, y_high = shifted_pair(y_head, y_tail, "py")

    def z_layers(first, only):
        lanes = jnp.transpose(velocity[:, :, first : first + 3], (0, 2, 1, 3)).reshape(9, rows, NX)
        return jnp.concatenate([lanes, fraction[:, only][None]], axis=0)

    z_low, z_high = shifted_pair(z_layers(0, 0), z_layers(cols - 3, cols - 1), ("px", "core"))

    def unlayered(z_rim):
        return jnp.transpose(z_rim[:9].reshape(3, 3, rows, NX), (0, 2, 1, 3))

    provisional = predicted(
        velocity,
        wall_ghosts(velocity, wall_flags),
        jnp.concatenate([y_low[:9].reshape(3, 3, cols, NX), velocity, y_high[:9].reshape(3, 3, cols, NX)], axis=1),
        jnp.concatenate([unlayered(z_low), velocity, unlayered(z_high)], axis=2),
        fraction,
    )

    def density_of(part):
        return 1.0 + (heavy_density - 1.0) * part

    density = density_of(fraction)
    inner_x = 2.0 / (density[:, :, 1:] + density[:, :, :-1])
    beta_x = jnp.concatenate([inner_x, jnp.zeros_like(density[:, :, :1])], axis=2)
    along_y = jnp.concatenate([density_of(y_low[9:]), density, density_of(y_high[9:])], axis=0)
    face = row_index * rows + jnp.arange(rows + 1, dtype=jnp.int32)[:, None, None]
    wall = (face == 0) | (face == total_rows)
    beta_y = jnp.where(wall, 0.0, 2.0 / (along_y[1:] + along_y[:-1]))
    over = jnp.concatenate([density[:, 1:], density_of(z_high[9][:, None])], axis=1)
    under = jnp.concatenate([density_of(z_low[9][:, None]), density[:, :-1]], axis=1)
    layer = col_index * cols + jnp.arange(cols, dtype=jnp.int32)[None, :, None]
    plus_z = jnp.where(layer == cols_devices * cols - 1, 0.0, 2.0 / (density + over))
    minus_z = jnp.where(layer == 0, 0.0, 2.0 / (density + under))
    betas = (beta_x, beta_y, jnp.stack([plus_z, minus_z]))

    peers = rows_devices * cores
    part_x = NX // peers
    plain_x = cosine_table(NX).reshape(peers, part_x, NX).transpose(1, 0, 2).reshape(NX, NX)
    plain_y = cosine_table(total_rows).T.reshape(rows_devices, rows, total_rows)
    plain_y = plain_y.transpose(1, 0, 2).reshape(total_rows, total_rows)
    table_x = jnp.asarray(plain_x, dtype=jnp.float32)
    table_y = jnp.asarray(plain_y, dtype=jnp.float32)
    inner = np.arange(256)
    row_source = jnp.asarray(
        (inner // 32 % 2 * 128 + inner % 4 * 32 + inner // 64 * 8 + inner // 4 % 8)[None].astype(np.int32)
    )
    rim_source = jnp.asarray(rim_slots())

    half_x = lax.dynamic_slice(
        jnp.asarray(half_eigenvalue(NX), dtype=jnp.float32), ((row_index * cores + core_index) * part_x,), (part_x,)
    )
    half_y = jnp.asarray(half_eigenvalue(total_rows), dtype=jnp.float32)
    shift = compressibility + half_x[None, :, None] + half_y.reshape(2, 1, 128)
    shift = shift.reshape(8, 128)
    root = jnp.sqrt(shift * (shift + 2.0))
    rho = 1.0 / (1.0 + shift + root)
    scale = 1.0 / root
    size = cols * cores
    weights = wave_weights(chip_index, rho, chips, size)
    place = chip_index.astype(jnp.int32).reshape(1)

    across = ("py", "core")
    layers_shape = (size, 8, 128)
    rims_shape = (rows_devices, 4, 128)
    (message,) = run(send_fields, [(peers, 4, 128)], provisional, table_x)
    message = exchange(message, across).reshape(rows_devices, 8, 128)
    gather, layers = run(
        read_fields, [(chips, 32, 128), layers_shape], message, table_y, row_source, rho
    )
    gather = exchange(gather, "px")
    message, residual, waves, aligned = run(
        first_solve,
        [rims_shape, layers_shape, (2, 8, 128), (1, 128)],
        place, gather, layers, rho, scale, weights, table_y, rim_source,
    )
    message = exchange(message.reshape(peers, 2, 128), across)
    message, first, applied = run(
        first_image, [(peers, 2, 128), (64, NX), (32, NX)], message, aligned, table_x, *betas
    )
    message = exchange(message, across).reshape(rows_devices, 4, 128)
    gather, layers = run(
        read_image, [(chips, 24, 128), layers_shape], message, table_y, row_source, rho
    )
    gather = exchange(gather, "px")
    message, scalars = run(
        second_solve,
        [rims_shape, (1, 128)],
        gather, layers, residual, waves, rho, scale, weights, table_y, rim_source,
    )
    message = exchange(message.reshape(peers, 2, 128), across)
    second, parts = run(
        second_image, [(64, NX), (peers, 1, 128)], message, scalars, applied, table_x, *betas
    )
    (parts,) = run(add_parts, [(chips, 1, 128)], exchange(parts, across))
    parts = exchange(parts, "px")
    next_velocity, pressure = run(
        finish,
        [velocity.shape, fraction.shape],
        parts, scalars, first, second, *betas, provisional,
        last=True,
    )
    return next_velocity, pressure


def solution(mesh):
    rows = mesh.shape["py"]
    split = Mesh(mesh.devices.reshape(rows, -1, 2), ("py", "px", "core"))
    wide = P(None, "py", ("px", "core"), None)
    flat = P("py", ("px", "core"), None)
    return jax.shard_map(
        on_device,
        mesh=split,
        in_specs=(wide, flat, P(None, "py", ("px", "core"))),
        out_specs=(wide, flat),
        check_vma=False,
    )
```

```python
import jax
import jax.numpy as jnp
import numpy as np
from jax import lax
from jax.experimental import pallas as pl
from jax.experimental.pallas import tpu as pltpu
from jax.sharding import Mesh, PartitionSpec as P

NX = 512


time_step = 0.05
heavy_density = 8.0
light_viscosity = 0.3
heavy_viscosity = 0.6
compressibility = 0.001
mean_inverse = 0.5
weno_epsilon = 1e-06
highest = lax.Precision.HIGHEST


def weno_blend(slope_one, slope_two, slope_three, slope_four, slope_five):
    smooth_one = (
        13.0 / 12.0 * (slope_one - 2.0 * slope_two + slope_three) ** 2
        + 0.25 * (slope_one - 4.0 * slope_two + 3.0 * slope_three) ** 2
    )
    smooth_two = (
        13.0 / 12.0 * (slope_two - 2.0 * slope_three + slope_four) ** 2
        + 0.25 * (slope_two - slope_four) ** 2
    )
    smooth_three = (
        13.0 / 12.0 * (slope_three - 2.0 * slope_four + slope_five) ** 2
        + 0.25 * (3.0 * slope_three - 4.0 * slope_four + slope_five) ** 2
    )
    scale_one = weno_epsilon + smooth_one
    scale_two = weno_epsilon + smooth_two
    scale_three = weno_epsilon + smooth_three
    alpha_one = 0.1 * (scale_two * scale_three) ** 2
    alpha_two = 0.6 * (scale_one * scale_three) ** 2
    alpha_three = 0.3 * (scale_one * scale_two) ** 2
    weight_sum = alpha_one + alpha_two + alpha_three
    blended = alpha_one * (slope_one / 3.0 - 7.0 * slope_two / 6.0 + 11.0 * slope_three / 6.0)
    blended = blended + alpha_two * (-slope_two / 6.0 + 5.0 * slope_three / 6.0 + slope_four / 3.0)
    blended = blended + alpha_three * (
        slope_three / 3.0 + 5.0 * slope_four / 6.0 - slope_five / 6.0
    )
    return blended / weight_sum


def upwind_derivative(padded, direction_axis, advecting):
    length = padded.shape[direction_axis] - 6
    differences = jnp.diff(padded, axis=direction_axis)
    rightward = advecting > 0

    def window(offset):
        return lax.slice_in_dim(differences, offset, offset + length, axis=direction_axis)

    return weno_blend(*[jnp.where(rightward, window(k), window(5 - k)) for k in range(5)])


def predicted(center, along_x, along_y, along_z, fraction):
    slope_x = upwind_derivative(along_x, 3, center[0][None])
    slope_y = upwind_derivative(along_y, 1, center[1][None])
    slope_z = upwind_derivative(along_z, 2, center[2][None])
    transport = center[0] * slope_x + center[1] * slope_y + center[2] * slope_z
    spread = along_x[..., 4:-2] + along_x[..., 2:-4] - 2.0 * center
    spread = spread + (along_y[:, 4:-2] + along_y[:, 2:-4] - 2.0 * center)
    spread = spread + (along_z[:, :, 4:-2] + along_z[:, :, 2:-4] - 2.0 * center)
    density = 1.0 + (heavy_density - 1.0) * fraction
    kinematic = (light_viscosity + (heavy_viscosity - light_viscosity) * fraction) / density
    return center + time_step * (kinematic * spread - transport)


def wall_ghosts(velocity, wall_flags):
    component = lax.broadcasted_iota(jnp.int32, (3, *wall_flags.shape), 0)
    mirror_signs = jnp.where((component == 0) | (wall_flags[None] == 0), -1.0, 1.0)
    lower_ghost = velocity[..., :3][..., ::-1] * mirror_signs[:, 0, :, :, None]
    upper_ghost = velocity[..., -3:][..., ::-1] * mirror_signs[:, 1, :, :, None]
    return jnp.concatenate([lower_ghost, velocity, upper_ghost], axis=-1)


def shifted_pair(head, tail, axis):
    count = lax.axis_size(axis)
    up = [(i, i + 1) for i in range(count - 1)]
    down = [(i + 1, i) for i in range(count - 1)]
    return lax.ppermute(tail, axis, up), lax.ppermute(head, axis, down)


def cosine_table(length):
    wave_index = np.arange(length)[:, None]
    position = np.arange(length)[None, :]
    angle = np.pi / (2 * length) * (wave_index * (2 * position + 1) % (4 * length))
    weight = np.where(wave_index == 0, np.sqrt(1.0 / length), np.sqrt(2.0 / length))
    return weight * np.cos(angle)


def half_eigenvalue(length):
    return mean_inverse * 4.0 * np.sin(np.pi * np.arange(length) / (2 * length)) ** 2


def exchange(message, axis):
    return lax.all_to_all(message, axis, split_axis=0, concat_axis=0, tiled=True)


def dot(left, right):
    return lax.dot_general(
        left, right, (((1,), (0,)), ((), ())), precision=highest, preferred_element_type=jnp.float32
    )


def dot_nt(left, right):
    return lax.dot_general(
        left, right, (((1,), (1,)), ((), ())), precision=highest, preferred_element_type=jnp.float32
    )


def rolled(values, shift, axis):
    return pltpu.roll(values, shift % values.shape[axis], axis)


def moved(values, step):
    row = lax.broadcasted_iota(jnp.int32, values.shape, 0)
    edge = 0 if step == 1 else values.shape[0] - 1
    return jnp.where(row == edge, 0.0, rolled(values, step, 0))


def picked(values, source):
    lane = lax.broadcasted_iota(jnp.int32, (values.shape[1], source.shape[1]), 0)
    chosen = jnp.where(lane == source, 1.0, 0.0).astype(jnp.bfloat16)
    total = None
    rest = values
    for _ in range(3):
        piece = rest.astype(jnp.bfloat16)
        rest = rest - piece.astype(jnp.float32)
        term = jnp.dot(piece, chosen, preferred_element_type=jnp.float32)
        total = term if total is None else total + term
    return total


def from_tiles(tiles, count):
    return jnp.concatenate([tiles[:, t, :] for t in range(count)], axis=1)


def into_tiles(ref, values):
    for t in range(values.shape[1] // 128):
        ref[:, t, :] = values[:, 128 * t : 128 * t + 128]


def to_messages(rows, table_x):
    spectral = dot_nt(table_x, rows)
    devices = spectral.shape[0] // 4
    blocks = [spectral[devices * k : devices * k + devices] for k in range(4)]
    return [
        jnp.concatenate([block[:, 32 * c : 32 * c + 32] for block in blocks], axis=1)
        for c in range(rows.shape[0] // 32)
    ]


def row_blocks(messages, source):
    ordered = picked(jnp.concatenate(messages, axis=0), source)
    devices = messages[0].shape[0]
    return [
        [ordered[devices * c : devices * c + devices, 64 * y : 64 * y + 64] for y in range(4)]
        for c in range(len(messages))
    ]


def to_modes(fields, table_y):
    cells = [jnp.concatenate(blocks, axis=0).T for blocks in fields]
    modes = dot(jnp.concatenate(cells, axis=0), table_y)
    layers = [
        jnp.concatenate([modes[4 * r : 4 * r + 4, :128], modes[4 * r : 4 * r + 4, 128:]], axis=0)
        for r in range(16 * len(fields))
    ]
    return [layers[16 * c : 16 * c + 16] for c in range(len(fields))]


def from_layers(layers):
    return jnp.concatenate(
        [jnp.concatenate([layer[:4], layer[4:]], axis=1) for layer in layers], axis=0
    )


def moments(layers, rho):
    upward = layers[0]
    for layer in layers[1:]:
        upward = rho * upward + layer
    downward = layers[-1]
    for layer in layers[-2::-1]:
        downward = rho * downward + layer
    return upward, downward


def incoming(upward, downward, weights):
    low = jnp.sum(weights[0] * upward + weights[1] * downward, axis=0)
    high = jnp.sum(weights[2] * upward + weights[3] * downward, axis=0)
    return low, high


def solved(layers, low, high, rho, scale):
    inverse = 1.0 / rho
    wave = low * inverse
    forward = [wave]
    for layer in layers:
        wave = rho * wave + layer
        forward.append(wave)
    forward.append(rho * wave)
    wave = high
    backward = [high * inverse, high]
    for layer in layers[::-1]:
        wave = rho * (wave + layer)
        backward.append(wave)
    backward = backward[::-1]
    return [scale * (f + b) for f, b in zip(forward, backward)]


def layers_total(left, right):
    product = left[0] * right[0]
    for one, other in zip(left[1:], right[1:]):
        product = product + one * other
    return total(product)


def send_rims(out_ref, layers, table_y, source):
    rows = dot_nt(table_y, from_layers(layers))
    devices = rows.shape[0] // 4
    blocks = [rows[devices * y : devices * y + devices] for y in range(4)]
    blocks = [moved(blocks[3], 1), *blocks, moved(blocks[0], -1)]
    into_tiles(out_ref, picked(jnp.concatenate(blocks, axis=1), source))


def from_rims(message, table_x):
    stacked = jnp.concatenate([message[:, 64 * k : 64 * k + 64] for k in range(4)], axis=0)
    return dot(stacked.T, table_x)


def fluxes(slots, beta_x, beta_y, beta_z):
    tiles = [slots[8 * y : 8 * y + 8] for y in range(6)]
    flux_y = [beta_y[y] * (tiles[y + 1] - tiles[y]) for y in range(5)]
    layer = lax.broadcasted_iota(jnp.int32, tiles[0].shape, 0)
    results = []
    for y in range(4):
        cells = tiles[y + 1]
        forward_x = beta_x[y] * (rolled(cells, -1, 1) - cells)
        above = jnp.where(layer == 7, slots[52 + y : 53 + y], rolled(cells, -1, 0))
        below = jnp.where(layer == 0, slots[48 + y : 49 + y], rolled(cells, 1, 0))
        results.append(
            (
                cells,
                forward_x,
                rolled(forward_x, 1, 1),
                flux_y[y + 1],
                flux_y[y],
                beta_z[0, y] * (above - cells),
                beta_z[1, y] * (cells - below),
            )
        )
    return results


def applied_rows(slots, beta_x, beta_y, beta_z):
    rows = []
    for cells, fx, bx, fy, by, fz, bz in fluxes(slots, beta_x, beta_y, beta_z):
        rows.append(compressibility * cells - (fx - bx + (fy - by) + (fz - bz)))
    return jnp.concatenate(rows, axis=0)


def total(values):
    return jnp.sum(jnp.sum(values, axis=0, keepdims=True), axis=1, keepdims=True)


def lane_row(values):
    lane = lax.broadcasted_iota(jnp.int32, (1, 128), 1)
    row = jnp.zeros((1, 128), jnp.float32)
    for index, value in enumerate(values):
        row = jnp.where(lane == index, value, row)
    return row


def send_fields(provisional_ref, table_ref, out_ref):
    normal = provisional_ref[0].reshape(32, NX)
    lane = lax.broadcasted_iota(jnp.int32, normal.shape, 1)
    after = jnp.where(lane == NX - 1, -normal, rolled(normal, -1, 1))
    before = jnp.where(lane == 0, -normal, rolled(normal, 1, 1))
    rows = [-0.5 * (after - before)]
    rows += [provisional_ref[c].reshape(32, NX) for c in (1, 2)]
    for c, message in enumerate(to_messages(jnp.concatenate(rows, axis=0), table_ref[...])):
        out_ref[:, c, :] = message
    out_ref[:, 3, :] = jnp.zeros_like(message)


def prepare(place_ref, half_x_ref, half_y_ref, fraction_ref, y_low_ref, y_high_ref, z_low_ref, z_high_ref,
            beta_x_ref, beta_y_ref, beta_z_ref, rho_ref, scale_ref, weights_ref):
    row, chip, core = place_ref[0], place_ref[1], place_ref[2]

    def density_of(part):
        return 1.0 + (heavy_density - 1.0) * part

    cells = [density_of(fraction_ref[y]) for y in range(4)]
    under, over = density_of(z_low_ref[...]), density_of(z_high_ref[...])
    lane = lax.broadcasted_iota(jnp.int32, cells[0].shape, 1)
    layer = lax.broadcasted_iota(jnp.int32, cells[0].shape, 0)
    first_z = (layer == 0) & (chip == 0) & (core == 0)
    last_z = (layer == 7) & (chip == weights_ref.shape[1] - 1) & (core == 1)
    for y, own in enumerate(cells):
        beta_x_ref[y] = jnp.where(lane == NX - 1, 0.0, 2.0 / (own + rolled(own, -1, 1)))
        above = jnp.where(layer == 7, over[y : y + 1], rolled(own, -1, 0))
        below = jnp.where(layer == 0, under[y : y + 1], rolled(own, 1, 0))
        beta_z_ref[0, y] = jnp.where(last_z, 0.0, 2.0 / (own + above))
        beta_z_ref[1, y] = jnp.where(first_z, 0.0, 2.0 / (own + below))
    column = [density_of(y_low_ref[...]), *cells, density_of(y_high_ref[...])]
    for y in range(5):
        wall = (lane >= 0) & (row == (0 if y == 0 else 63)) if y in (0, 4) else lane < 0
        beta_y_ref[y] = jnp.where(wall, 0.0, 2.0 / (column[y + 1] + column[y]))
    mode = lax.broadcasted_iota(jnp.int32, rho_ref.shape, 0) % 4
    half_x = jnp.zeros(rho_ref.shape, jnp.float32)
    for k in range(4):
        half_x = jnp.where(mode == k, half_x_ref[(row * 2 + core) * 4 + k], half_x)
    shift = compressibility + half_x + half_y_ref[...]
    root = jnp.sqrt(shift * (shift + 2.0))
    rho = 1.0 / (1.0 + shift + root)
    rho_ref[...] = rho
    scale_ref[...] = 1.0 / root
    log_rho = jnp.log(rho)
    count, size = weights_ref.shape[1], 16
    period = 2 * size * count
    norm = 1.0 / (1.0 - jnp.exp(period * log_rho))
    for block in range(count):
        behind = size * (chip - block) - size + 1 + jnp.where(block < chip, 0, period)
        ahead = size * (block - chip) - size + 1 + jnp.where(block > chip, 0, period)
        low = size * (chip + block) + 1
        high = period - 2 * size + 1 - size * (chip + block)
        for side, exponent in enumerate((behind, low, high, ahead)):
            weights_ref[side, block] = jnp.exp(exponent.astype(jnp.float32) * log_rho) * norm


def read_fields(message_ref, table_ref, source_ref, rho_ref, gather_ref, layers_ref):
    tiles = message_ref[...]
    pairs = [jnp.concatenate([tiles[:, c, :], tiles[:, c + 4, :]], axis=1) for c in range(3)]
    across, along_y, along_z = row_blocks(pairs, source_ref[:, :256])
    after = [*along_y[1:], moved(along_y[0], -1)]
    before = [moved(along_y[3], 1), *along_y[:3]]
    across = [s - 0.5 * (a - b) for s, a, b in zip(across, after, before)]
    joined, third = to_modes([across, along_z], table_ref[...])
    zero = jnp.zeros_like(third[0])
    above = [*third[1:], zero]
    below = [zero, *third[:-1]]
    layers = [j - 0.5 * (a - b) for j, a, b in zip(joined, above, below)]
    upward, downward = moments(layers, rho_ref[...])
    for device in range(gather_ref.shape[0]):
        gather_ref[device, 0:8] = upward
        gather_ref[device, 8:16] = downward
        gather_ref[device, 16:24] = third[0]
        gather_ref[device, 24:32] = third[-1]
    for z, layer in enumerate(layers):
        layers_ref[z] = layer


def first_solve(place_ref, gather_ref, layers_ref, rho_ref, scale_ref, weights_ref, table_ref, source_ref,
                out_ref, residual_ref, waves_ref, aligned_ref):
    rho = rho_ref[...]
    square = rho * rho
    fourth = square * square
    power = fourth * fourth * fourth * square * rho
    gathered = gather_ref[...]
    first, last = gathered[:, 16:24], gathered[:, 24:32]
    zero = jnp.zeros_like(first[:1])
    under = 0.5 * jnp.concatenate([zero, last[:-1]], axis=0)
    over = -0.5 * jnp.concatenate([first[1:], zero], axis=0)
    upward = gathered[:, 0:8] + power * under + over
    downward = gathered[:, 8:16] + under + power * over
    low, high = incoming(upward, downward, weights_ref[...])
    mine = lax.broadcasted_iota(jnp.int32, under.shape, 0) == place_ref[0]
    layers = [layers_ref[z] for z in range(16)]
    layers[0] = layers[0] + jnp.sum(jnp.where(mine, under, 0.0), axis=0)
    layers[15] = layers[15] + jnp.sum(jnp.where(mine, over, 0.0), axis=0)
    modes = solved(layers, low, high, rho, scale_ref[...])
    aligned_ref[...] = lane_row([layers_total(layers, modes[1:-1])])
    for z, layer in enumerate(layers):
        residual_ref[z] = layer
    waves_ref[0] = low
    waves_ref[1] = high
    send_rims(out_ref, modes, table_ref[...], source_ref[:, 256:])


def first_image(message_ref, aligned_ref, table_ref, beta_x_ref, beta_y_ref, beta_z_ref, out_ref, slots_ref, applied_ref):
    table = table_ref[...]
    slots = from_rims(from_tiles(message_ref[...], 2), table)
    applied = applied_rows(slots, beta_x_ref[...], beta_y_ref[...], beta_z_ref[...])
    slots_ref[...] = slots
    applied_ref[...] = applied
    (message,) = to_messages(applied, table)
    curvature = total(slots[8:40] * applied)
    out_ref[:, 0, :] = message
    row = lane_row([aligned_ref[...][:, :1], curvature])
    out_ref[:, 1, :] = jnp.broadcast_to(row, message.shape)


def read_image(message_ref, table_ref, source_ref, rho_ref, gather_ref, layers_ref):
    tiles = message_ref[...]
    pair = jnp.concatenate([tiles[:, 0, :], tiles[:, 2, :]], axis=1)
    (layers,) = to_modes(row_blocks([pair], source_ref[:, :256]), table_ref[...])
    sums = jnp.sum(tiles[:, 1, :] + tiles[:, 3, :], axis=0, keepdims=True)
    upward, downward = moments(layers, rho_ref[...])
    sums = jnp.broadcast_to(sums, upward.shape)
    for device in range(gather_ref.shape[0]):
        gather_ref[device, 0:8] = upward
        gather_ref[device, 8:16] = downward
        gather_ref[device, 16:24] = sums
    for z, layer in enumerate(layers):
        layers_ref[z] = layer


def second_solve(gather_ref, layers_ref, residual_ref, waves_ref, rho_ref, scale_ref, weights_ref, table_ref, source_ref,
                 out_ref, scalars_ref):
    gathered = gather_ref[...]
    sums = jnp.sum(gathered[:, 16:24], axis=0)[:1]
    aligned, curvature = sums[:, 0:1], sums[:, 1:2]
    step = aligned / curvature
    low, high = incoming(gathered[:, 0:8], gathered[:, 8:16], weights_ref[...])
    layers = [residual_ref[z] - step * layers_ref[z] for z in range(16)]
    modes = solved(layers, waves_ref[0] - step * low, waves_ref[1] - step * high, rho_ref[...], scale_ref[...])
    scalars_ref[...] = lane_row([layers_total(layers, modes[1:-1]), aligned, curvature])
    send_rims(out_ref, modes, table_ref[...], source_ref[:, 256:])


def second_image(message_ref, scalars_ref, applied_ref, table_ref, beta_x_ref, beta_y_ref, beta_z_ref, slots_ref, out_ref):
    slots = from_rims(from_tiles(message_ref[...], 2), table_ref[...])
    slots_ref[...] = slots
    bent = total(slots[8:40] * applied_rows(slots, beta_x_ref[...], beta_y_ref[...], beta_z_ref[...]))
    crossed = total(slots[8:40] * applied_ref[...])
    row = lane_row([scalars_ref[...][:, 0:1], bent, crossed])
    out_ref[...] = jnp.broadcast_to(row[None], out_ref.shape)


def add_parts(parts_ref, out_ref):
    row = jnp.sum(parts_ref[...], axis=0)
    out_ref[...] = jnp.broadcast_to(row[None], out_ref.shape)


def finish(parts_ref, scalars_ref, first_ref, second_ref, beta_x_ref, beta_y_ref, beta_z_ref, provisional_ref, next_ref, pressure_ref):
    sums = jnp.sum(parts_ref[...], axis=0)
    renewed, bent, crossed = sums[:, 0:1], sums[:, 1:2], sums[:, 2:3]
    scalars = scalars_ref[...]
    aligned, curvature = scalars[:, 1:2], scalars[:, 2:3]
    ratio = renewed / aligned
    second_step = renewed / (bent + 2.0 * ratio * crossed + ratio * ratio * curvature)
    first = first_ref[...]
    slots = (aligned / curvature) * first + second_step * (second_ref[...] + ratio * first)
    parts = fluxes(slots, beta_x_ref[...], beta_y_ref[...], beta_z_ref[...])
    for y, (cells, fx, bx, fy, by, fz, bz) in enumerate(parts):
        pressure_ref[y] = cells
        next_ref[0, y] = provisional_ref[0, y] - 0.5 * (fx + bx)
        next_ref[1, y] = provisional_ref[1, y] - 0.5 * (fy + by)
        next_ref[2, y] = provisional_ref[2, y] - 0.5 * (fz + bz)


def run(kernel, outs, *arrays, last=False):
    whole = pl.BlockSpec(memory_space=pltpu.VMEM)
    scalar = pl.BlockSpec(memory_space=pltpu.SMEM)
    scalars = [array.ndim == 1 for array in arrays]
    kept = jax.ShapeDtypeStruct if last else pltpu.VMEM
    return pl.pallas_call(
        kernel,
        out_shape=[kept(shape, jnp.float32) for shape in outs],
        in_specs=[scalar if small else whole for small in scalars],
        out_specs=[whole] * len(outs),
        compiler_params=pltpu.CompilerParams(vmem_limit_bytes=8 << 20),
    )(
        *[
            array if small else pltpu.with_memory_space_constraint(array, pltpu.VMEM)
            for array, small in zip(arrays, scalars)
        ]
    )


def rim_slots():
    places = [(0, z + 1) for z in range(8)]
    places += [(y + 1, z + 1) for y in range(4) for z in range(8)]
    places += [(5, z + 1) for z in range(8)]
    places += [(y + 1, 0) for y in range(4)] + [(y + 1, 9) for y in range(4)]
    lanes = [
        [(y * 18 + 8 * core + z) * 4 + k for y, z in places] + [-1] * (64 - len(places))
        for core in range(2)
        for k in range(4)
    ]
    return np.array(lanes, np.int32).reshape(1, -1)


def on_device(velocity, fraction, wall_flags):
    rows, cols = (fraction.shape[0], fraction.shape[1])
    rows_devices = lax.axis_size("py")
    chips = lax.axis_size("px")
    cores = lax.axis_size("core")
    cols_devices = chips * cores
    total_rows = rows * rows_devices
    row_index = lax.axis_index("py")
    chip_index = lax.axis_index("px")
    core_index = lax.axis_index("core")

    def y_layers(part):
        return part.reshape(9, cols, NX)

    y_head = jnp.concatenate([y_layers(velocity[:, :3]), fraction[:1]], axis=0)
    y_tail = jnp.concatenate([y_layers(velocity[:, -3:]), fraction[-1:]], axis=0)
    y_low, y_high = shifted_pair(y_head, y_tail, "py")

    def z_layers(first, only):
        lanes = jnp.transpose(velocity[:, :, first : first + 3], (0, 2, 1, 3)).reshape(9, rows, NX)
        return jnp.concatenate([lanes, fraction[:, only][None]], axis=0)

    z_low, z_high = shifted_pair(z_layers(0, 0), z_layers(cols - 3, cols - 1), ("px", "core"))

    def unlayered(z_rim):
        return jnp.transpose(z_rim[:9].reshape(3, 3, rows, NX), (0, 2, 1, 3))

    provisional = predicted(
        velocity,
        wall_ghosts(velocity, wall_flags),
        jnp.concatenate([y_low[:9].reshape(3, 3, cols, NX), velocity, y_high[:9].reshape(3, 3, cols, NX)], axis=1),
        jnp.concatenate([unlayered(z_low), velocity, unlayered(z_high)], axis=2),
        fraction,
    )

    peers = rows_devices * cores
    part_x = NX // peers
    plain_x = cosine_table(NX).reshape(peers, part_x, NX).transpose(1, 0, 2).reshape(NX, NX)
    table_x = jnp.asarray(plain_x, dtype=jnp.float32)
    (message,) = run(send_fields, [(peers, 4, 128)], provisional, table_x)

    places = jnp.stack([row_index, chip_index, core_index]).astype(jnp.int32)

    plain_y = cosine_table(total_rows).T.reshape(rows_devices, rows, total_rows)
    plain_y = plain_y.transpose(1, 0, 2).reshape(total_rows, total_rows)
    table_y = jnp.asarray(plain_y, dtype=jnp.float32)
    inner = np.arange(256)
    row_source = inner // 32 % 2 * 128 + inner % 4 * 32 + inner // 64 * 8 + inner // 4 % 8
    sources = jnp.asarray(np.concatenate([row_source[None].astype(np.int32), rim_slots()], axis=1))

    half_x = jnp.asarray(half_eigenvalue(NX), dtype=jnp.float32)
    half_y = half_eigenvalue(total_rows).reshape(2, 1, 128)
    half_y = jnp.asarray(np.broadcast_to(half_y, (2, 4, 128)).reshape(8, 128), dtype=jnp.float32)
    size = cols * cores
    *betas, rho, scale, weights = run(
        prepare,
        [(rows, cols, NX), (rows + 1, cols, NX), (2, rows, cols, NX), (8, 128), (8, 128), (4, chips, 8, 128)],
        places, half_x, half_y, fraction, y_low[9], y_high[9], z_low[9], z_high[9],
    )
    place = places[1:2]

    across = ("py", "core")
    layers_shape = (size, 8, 128)
    rims_shape = (rows_devices, 4, 128)
    message = exchange(message, across)
    message = message.reshape(rows_devices, 8, 128)
    gather, layers = run(
        read_fields, [(chips, 32, 128), layers_shape], message, table_y, sources, rho
    )
    gather = exchange(gather, "px")
    message, residual, waves, aligned = run(
        first_solve,
        [rims_shape, layers_shape, (2, 8, 128), (1, 128)],
        place, gather, layers, rho, scale, weights, table_y, sources,
    )
    message = exchange(message.reshape(peers, 2, 128), across)
    message, first, applied = run(
        first_image, [(peers, 2, 128), (64, NX), (32, NX)], message, aligned, table_x, *betas
    )
    message = exchange(message, across).reshape(rows_devices, 4, 128)
    gather, layers = run(
        read_image, [(chips, 24, 128), layers_shape], message, table_y, sources, rho
    )
    gather = exchange(gather, "px")
    message, scalars = run(
        second_solve,
        [rims_shape, (1, 128)],
        gather, layers, residual, waves, rho, scale, weights, table_y, sources,
    )
    message = exchange(message.reshape(peers, 2, 128), across)
    second, parts = run(
        second_image, [(64, NX), (rows_devices, 1, 128)], message, scalars, applied, table_x, *betas
    )
    (parts,) = run(add_parts, [(cols_devices, 1, 128)], exchange(parts, "py"))
    parts = exchange(parts, ("px", "core"))
    next_velocity, pressure = run(
        finish,
        [velocity.shape, fraction.shape],
        parts, scalars, first, second, *betas, provisional,
        last=True,
    )
    return next_velocity, pressure


def solution(mesh):
    rows = mesh.shape["py"]
    split = Mesh(mesh.devices.reshape(rows, -1, 2), ("py", "px", "core"))
    wide = P(None, "py", ("px", "core"), None)
    flat = P("py", ("px", "core"), None)
    return jax.shard_map(
        on_device,
        mesh=split,
        in_specs=(wide, flat, P(None, "py", ("px", "core"))),
        out_specs=(wide, flat),
        check_vma=False,
    )
```

```python
import jax
import jax.numpy as jnp
import numpy as np
from jax import lax
from jax.experimental import pallas as pl
from jax.experimental.pallas import tpu as pltpu
from jax.sharding import Mesh, PartitionSpec as P

NX = 512


time_step = 0.05
heavy_density = 8.0
light_viscosity = 0.3
heavy_viscosity = 0.6
compressibility = 0.001
mean_inverse = 0.5
weno_epsilon = 1e-06
highest = lax.Precision.HIGHEST


def weno_blend(slope_one, slope_two, slope_three, slope_four, slope_five):
    smooth_one = (
        13.0 / 12.0 * (slope_one - 2.0 * slope_two + slope_three) ** 2
        + 0.25 * (slope_one - 4.0 * slope_two + 3.0 * slope_three) ** 2
    )
    smooth_two = (
        13.0 / 12.0 * (slope_two - 2.0 * slope_three + slope_four) ** 2
        + 0.25 * (slope_two - slope_four) ** 2
    )
    smooth_three = (
        13.0 / 12.0 * (slope_three - 2.0 * slope_four + slope_five) ** 2
        + 0.25 * (3.0 * slope_three - 4.0 * slope_four + slope_five) ** 2
    )
    scale_one = weno_epsilon + smooth_one
    scale_two = weno_epsilon + smooth_two
    scale_three = weno_epsilon + smooth_three
    alpha_one = 0.1 * (scale_two * scale_three) ** 2
    alpha_two = 0.6 * (scale_one * scale_three) ** 2
    alpha_three = 0.3 * (scale_one * scale_two) ** 2
    weight_sum = alpha_one + alpha_two + alpha_three
    blended = alpha_one * (slope_one / 3.0 - 7.0 * slope_two / 6.0 + 11.0 * slope_three / 6.0)
    blended = blended + alpha_two * (-slope_two / 6.0 + 5.0 * slope_three / 6.0 + slope_four / 3.0)
    blended = blended + alpha_three * (
        slope_three / 3.0 + 5.0 * slope_four / 6.0 - slope_five / 6.0
    )
    return blended / weight_sum


def upwind_derivative(padded, direction_axis, advecting):
    length = padded.shape[direction_axis] - 6
    differences = jnp.diff(padded, axis=direction_axis)
    rightward = advecting > 0

    def window(offset):
        return lax.slice_in_dim(differences, offset, offset + length, axis=direction_axis)

    return weno_blend(*[jnp.where(rightward, window(k), window(5 - k)) for k in range(5)])


def predicted(center, along_x, along_y, along_z, fraction):
    slope_x = upwind_derivative(along_x, 3, center[0][None])
    slope_y = upwind_derivative(along_y, 1, center[1][None])
    slope_z = upwind_derivative(along_z, 2, center[2][None])
    transport = center[0] * slope_x + center[1] * slope_y + center[2] * slope_z
    spread = along_x[..., 4:-2] + along_x[..., 2:-4] - 2.0 * center
    spread = spread + (along_y[:, 4:-2] + along_y[:, 2:-4] - 2.0 * center)
    spread = spread + (along_z[:, :, 4:-2] + along_z[:, :, 2:-4] - 2.0 * center)
    density = 1.0 + (heavy_density - 1.0) * fraction
    kinematic = (light_viscosity + (heavy_viscosity - light_viscosity) * fraction) / density
    return center + time_step * (kinematic * spread - transport)


def wall_ghosts(velocity, wall_flags):
    component = lax.broadcasted_iota(jnp.int32, (3, *wall_flags.shape), 0)
    mirror_signs = jnp.where((component == 0) | (wall_flags[None] == 0), -1.0, 1.0)
    lower_ghost = velocity[..., :3][..., ::-1] * mirror_signs[:, 0, :, :, None]
    upper_ghost = velocity[..., -3:][..., ::-1] * mirror_signs[:, 1, :, :, None]
    return jnp.concatenate([lower_ghost, velocity, upper_ghost], axis=-1)


def swapped(values, axis, pairs):
    return lax.ppermute(values, axis, pairs)


def shifted_pair(head, tail, axis):
    count = lax.axis_size(axis)
    even = (lax.axis_index(axis) & 1) == 0
    inner = [(i, i + 1) for i in range(0, count, 2)]
    outer = [(i, i + 1) for i in range(1, count - 1, 2)]
    one = swapped(jnp.where(even, tail, head), axis, inner + [(j, i) for i, j in inner])
    two = swapped(jnp.where(even, head, tail), axis, outer + [(j, i) for i, j in outer])
    return jnp.where(even, two, one), jnp.where(even, one, two)


def cosine_table(length):
    wave_index = np.arange(length)[:, None]
    position = np.arange(length)[None, :]
    angle = np.pi / (2 * length) * (wave_index * (2 * position + 1) % (4 * length))
    weight = np.where(wave_index == 0, np.sqrt(1.0 / length), np.sqrt(2.0 / length))
    return weight * np.cos(angle)


def half_eigenvalue(length):
    return mean_inverse * 4.0 * np.sin(np.pi * np.arange(length) / (2 * length)) ** 2


def exchange(message, axis):
    return lax.all_to_all(message, axis, split_axis=0, concat_axis=0, tiled=True)


def dot(left, right):
    return lax.dot_general(
        left, right, (((1,), (0,)), ((), ())), precision=highest, preferred_element_type=jnp.float32
    )


def dot_nt(left, right):
    return lax.dot_general(
        left, right, (((1,), (1,)), ((), ())), precision=highest, preferred_element_type=jnp.float32
    )


def rolled(values, shift, axis):
    return pltpu.roll(values, shift % values.shape[axis], axis)


def moved(values, step):
    row = lax.broadcasted_iota(jnp.int32, values.shape, 0)
    edge = 0 if step == 1 else values.shape[0] - 1
    return jnp.where(row == edge, 0.0, rolled(values, step, 0))


def picked(values, source):
    lane = lax.broadcasted_iota(jnp.int32, (values.shape[1], source.shape[1]), 0)
    chosen = jnp.where(lane == source, 1.0, 0.0).astype(jnp.bfloat16)
    total = None
    rest = values
    for _ in range(3):
        piece = rest.astype(jnp.bfloat16)
        rest = rest - piece.astype(jnp.float32)
        term = jnp.dot(piece, chosen, preferred_element_type=jnp.float32)
        total = term if total is None else total + term
    return total


def from_tiles(tiles, count):
    return jnp.concatenate([tiles[:, t, :] for t in range(count)], axis=1)


def into_tiles(ref, values):
    for t in range(values.shape[1] // 128):
        ref[:, t, :] = values[:, 128 * t : 128 * t + 128]


def to_message(rows, table_x):
    spectral = dot_nt(table_x, rows)
    devices = spectral.shape[0] // 4
    blocks = [spectral[devices * k : devices * k + devices] for k in range(4)]
    return jnp.concatenate(blocks, axis=1)


def to_layers(blocks, table_y):
    modes = dot(jnp.concatenate(blocks, axis=0).T, table_y)
    return [
        jnp.concatenate([modes[4 * r : 4 * r + 4, :128], modes[4 * r : 4 * r + 4, 128:]], axis=0)
        for r in range(modes.shape[0] // 4)
    ]


def from_layers(layers):
    return jnp.concatenate(
        [jnp.concatenate([layer[:4], layer[4:]], axis=1) for layer in layers], axis=0
    )


def moments(layers, rho):
    upward = layers[0]
    for layer in layers[1:]:
        upward = rho * upward + layer
    downward = layers[-1]
    for layer in layers[-2::-1]:
        downward = rho * downward + layer
    return upward, downward


def incoming(upward, downward, weights):
    low = jnp.sum(weights[0] * upward + weights[1] * downward, axis=0)
    high = jnp.sum(weights[2] * upward + weights[3] * downward, axis=0)
    return low, high


def solved(layers, low, high, rho, scale):
    inverse = 1.0 / rho
    wave = low * inverse
    forward = [wave]
    for layer in layers:
        wave = rho * wave + layer
        forward.append(wave)
    forward.append(rho * wave)
    wave = high
    backward = [high * inverse, high]
    for layer in layers[::-1]:
        wave = rho * (wave + layer)
        backward.append(wave)
    backward = backward[::-1]
    return [scale * (f + b) for f, b in zip(forward, backward)]


def layers_total(left, right):
    product = left[0] * right[0]
    for one, other in zip(left[1:], right[1:]):
        product = product + one * other
    return total(product)


def send_rims(out_ref, layers, table_y, source):
    rows = dot_nt(table_y, from_layers(layers))
    devices = rows.shape[0] // 4
    blocks = [rows[devices * y : devices * y + devices] for y in range(4)]
    blocks = [moved(blocks[3], 1), *blocks, moved(blocks[0], -1)]
    into_tiles(out_ref, picked(jnp.concatenate(blocks, axis=1), source))


def from_rims(message, table_x):
    stacked = jnp.concatenate([message[:, 64 * k : 64 * k + 64] for k in range(4)], axis=0)
    return dot(stacked.T, table_x)


def fluxes(slots, beta_x, beta_y, beta_z):
    tiles = [slots[8 * y : 8 * y + 8] for y in range(6)]
    flux_y = [beta_y[y] * (tiles[y + 1] - tiles[y]) for y in range(5)]
    layer = lax.broadcasted_iota(jnp.int32, tiles[0].shape, 0)
    results = []
    for y in range(4):
        cells = tiles[y + 1]
        forward_x = beta_x[y] * (rolled(cells, -1, 1) - cells)
        above = jnp.where(layer == 7, slots[52 + y : 53 + y], rolled(cells, -1, 0))
        below = jnp.where(layer == 0, slots[48 + y : 49 + y], rolled(cells, 1, 0))
        results.append(
            (
                cells,
                forward_x,
                rolled(forward_x, 1, 1),
                flux_y[y + 1],
                flux_y[y],
                beta_z[0, y] * (above - cells),
                beta_z[1, y] * (cells - below),
            )
        )
    return results


def applied_rows(slots, beta_x, beta_y, beta_z):
    rows = []
    for cells, fx, bx, fy, by, fz, bz in fluxes(slots, beta_x, beta_y, beta_z):
        rows.append(compressibility * cells - (fx - bx + (fy - by) + (fz - bz)))
    return jnp.concatenate(rows, axis=0)


def total(values):
    return jnp.sum(jnp.sum(values, axis=0, keepdims=True), axis=1, keepdims=True)


def lane_row(values):
    lane = lax.broadcasted_iota(jnp.int32, (1, 128), 1)
    row = jnp.zeros((1, 128), jnp.float32)
    for index, value in enumerate(values):
        row = jnp.where(lane == index, value, row)
    return row


def send_fields(provisional_ref, table_ref, out_ref):
    normal = provisional_ref[0].reshape(32, NX)
    lane = lax.broadcasted_iota(jnp.int32, normal.shape, 1)
    after = jnp.where(lane == NX - 1, -normal, rolled(normal, -1, 1))
    before = jnp.where(lane == 0, -normal, rolled(normal, 1, 1))
    across = -0.5 * (after - before)
    along_y = [provisional_ref[1, y] for y in range(4)]
    along_z = [provisional_ref[2, y] for y in range(4)]
    zero = jnp.zeros_like(along_y[0])
    layer = lax.broadcasted_iota(jnp.int32, zero.shape, 0)
    rows = []
    for y in range(4):
        rise = (along_y[y + 1] if y < 3 else zero) - (along_y[y - 1] if y > 0 else zero)
        above = jnp.where(layer == 7, 0.0, rolled(along_z[y], -1, 0))
        below = jnp.where(layer == 0, 0.0, rolled(along_z[y], 1, 0))
        rows.append(across[8 * y : 8 * y + 8] - 0.5 * rise - 0.5 * (above - below))
    rows += [along_y[0], along_y[3]]
    rows += [part[:1] for part in along_z] + [part[7:] for part in along_z] + [zero]
    into_tiles(out_ref, to_message(jnp.concatenate(rows, axis=0), table_ref[...]))


def prepare(place_ref, half_x_ref, half_y_ref, fraction_ref, y_low_ref, y_high_ref, z_low_ref, z_high_ref,
            beta_x_ref, beta_y_ref, beta_z_ref, rho_ref, scale_ref, weights_ref):
    row, chip, core = place_ref[0], place_ref[1], place_ref[2]

    def density_of(part):
        return 1.0 + (heavy_density - 1.0) * part

    cells = [density_of(fraction_ref[y]) for y in range(4)]
    under, over = density_of(z_low_ref[...]), density_of(z_high_ref[...])
    lane = lax.broadcasted_iota(jnp.int32, cells[0].shape, 1)
    layer = lax.broadcasted_iota(jnp.int32, cells[0].shape, 0)
    first_z = (layer == 0) & (chip == 0) & (core == 0)
    last_z = (layer == 7) & (chip == weights_ref.shape[1] - 1) & (core == 1)
    for y, own in enumerate(cells):
        beta_x_ref[y] = jnp.where(lane == NX - 1, 0.0, 2.0 / (own + rolled(own, -1, 1)))
        above = jnp.where(layer == 7, over[y : y + 1], rolled(own, -1, 0))
        below = jnp.where(layer == 0, under[y : y + 1], rolled(own, 1, 0))
        beta_z_ref[0, y] = jnp.where(last_z, 0.0, 2.0 / (own + above))
        beta_z_ref[1, y] = jnp.where(first_z, 0.0, 2.0 / (own + below))
    column = [density_of(y_low_ref[...]), *cells, density_of(y_high_ref[...])]
    for y in range(5):
        wall = (lane >= 0) & (row == (0 if y == 0 else 63)) if y in (0, 4) else lane < 0
        beta_y_ref[y] = jnp.where(wall, 0.0, 2.0 / (column[y + 1] + column[y]))
    mode = lax.broadcasted_iota(jnp.int32, rho_ref.shape, 0) % 4
    half_x = jnp.zeros(rho_ref.shape, jnp.float32)
    for k in range(4):
        half_x = jnp.where(mode == k, half_x_ref[(row * 2 + core) * 4 + k], half_x)
    shift = compressibility + half_x + half_y_ref[...]
    root = jnp.sqrt(shift * (shift + 2.0))
    rho = 1.0 / (1.0 + shift + root)
    rho_ref[...] = rho
    scale_ref[...] = 1.0 / root
    log_rho = jnp.log(rho)
    count, size = weights_ref.shape[1], 16
    period = 2 * size * count
    norm = 1.0 / (1.0 - jnp.exp(period * log_rho))
    for block in range(count):
        behind = size * (chip - block) - size + 1 + jnp.where(block < chip, 0, period)
        ahead = size * (block - chip) - size + 1 + jnp.where(block > chip, 0, period)
        low = size * (chip + block) + 1
        high = period - 2 * size + 1 - size * (chip + block)
        for side, exponent in enumerate((behind, low, high, ahead)):
            weights_ref[side, block] = jnp.exp(exponent.astype(jnp.float32) * log_rho) * norm


def read_fields(message_ref, table_ref, source_ref, rho_ref, gather_ref, layers_ref):
    tiles = message_ref[...]
    ordered = picked(from_tiles(tiles, 4), source_ref[:, 768:])
    blocks = [ordered[:, 128 * y : 128 * y + 128] for y in range(4)]
    blocks[0] = blocks[0] + 0.5 * moved(ordered[:, 640:768], 1)
    blocks[3] = blocks[3] - 0.5 * moved(ordered[:, 512:640], -1)
    layers = to_layers([block[:, :80] for block in blocks], table_ref[...])
    layers, edges = layers[:16], layers[16:]
    layers[7] = layers[7] - 0.5 * edges[2]
    layers[8] = layers[8] + 0.5 * edges[1]
    upward, downward = moments(layers, rho_ref[...])
    for device in range(gather_ref.shape[0]):
        gather_ref[device, 0:8] = upward
        gather_ref[device, 8:16] = downward
        gather_ref[device, 16:24] = edges[0]
        gather_ref[device, 24:32] = edges[3]
    for z, layer in enumerate(layers):
        layers_ref[z] = layer


def first_solve(place_ref, gather_ref, layers_ref, rho_ref, scale_ref, weights_ref, table_ref, source_ref,
                out_ref, residual_ref, waves_ref, aligned_ref):
    rho = rho_ref[...]
    square = rho * rho
    fourth = square * square
    power = fourth * fourth * fourth * square * rho
    gathered = gather_ref[...]
    first, last = gathered[:, 16:24], gathered[:, 24:32]
    zero = jnp.zeros_like(first[:1])
    under = 0.5 * jnp.concatenate([zero, last[:-1]], axis=0)
    over = -0.5 * jnp.concatenate([first[1:], zero], axis=0)
    upward = gathered[:, 0:8] + power * under + over
    downward = gathered[:, 8:16] + under + power * over
    low, high = incoming(upward, downward, weights_ref[...])
    mine = lax.broadcasted_iota(jnp.int32, under.shape, 0) == place_ref[0]
    layers = [layers_ref[z] for z in range(16)]
    layers[0] = layers[0] + jnp.sum(jnp.where(mine, under, 0.0), axis=0)
    layers[15] = layers[15] + jnp.sum(jnp.where(mine, over, 0.0), axis=0)
    modes = solved(layers, low, high, rho, scale_ref[...])
    aligned_ref[...] = lane_row([layers_total(layers, modes[1:-1])])
    for z, layer in enumerate(layers):
        residual_ref[z] = layer
    waves_ref[0] = low
    waves_ref[1] = high
    send_rims(out_ref, modes, table_ref[...], source_ref[:, 256:768])


def first_image(message_ref, aligned_ref, table_ref, beta_x_ref, beta_y_ref, beta_z_ref, out_ref, slots_ref, applied_ref):
    table = table_ref[...]
    slots = from_rims(from_tiles(message_ref[...], 2), table)
    applied = applied_rows(slots, beta_x_ref[...], beta_y_ref[...], beta_z_ref[...])
    slots_ref[...] = slots
    applied_ref[...] = applied
    message = to_message(applied, table)
    curvature = total(slots[8:40] * applied)
    out_ref[:, 0, :] = message
    row = lane_row([aligned_ref[...][:, :1], curvature])
    out_ref[:, 1, :] = jnp.broadcast_to(row, message.shape)


def read_image(message_ref, table_ref, source_ref, rho_ref, gather_ref, layers_ref):
    tiles = message_ref[...]
    pair = jnp.concatenate([tiles[:, 0, :], tiles[:, 2, :]], axis=1)
    ordered = picked(pair, source_ref[:, :256])
    layers = to_layers([ordered[:, 64 * y : 64 * y + 64] for y in range(4)], table_ref[...])
    sums = jnp.sum(tiles[:, 1, :] + tiles[:, 3, :], axis=0, keepdims=True)
    upward, downward = moments(layers, rho_ref[...])
    sums = jnp.broadcast_to(sums, upward.shape)
    for device in range(gather_ref.shape[0]):
        gather_ref[device, 0:8] = upward
        gather_ref[device, 8:16] = downward
        gather_ref[device, 16:24] = sums
    for z, layer in enumerate(layers):
        layers_ref[z] = layer


def second_solve(gather_ref, layers_ref, residual_ref, waves_ref, rho_ref, scale_ref, weights_ref, table_ref, source_ref,
                 out_ref, scalars_ref):
    gathered = gather_ref[...]
    sums = jnp.sum(gathered[:, 16:24], axis=0)[:1]
    aligned, curvature = sums[:, 0:1], sums[:, 1:2]
    step = aligned / curvature
    low, high = incoming(gathered[:, 0:8], gathered[:, 8:16], weights_ref[...])
    layers = [residual_ref[z] - step * layers_ref[z] for z in range(16)]
    modes = solved(layers, waves_ref[0] - step * low, waves_ref[1] - step * high, rho_ref[...], scale_ref[...])
    scalars_ref[...] = lane_row([layers_total(layers, modes[1:-1]), aligned, curvature])
    send_rims(out_ref, modes, table_ref[...], source_ref[:, 256:768])


def second_image(message_ref, scalars_ref, applied_ref, table_ref, beta_x_ref, beta_y_ref, beta_z_ref, slots_ref, out_ref):
    slots = from_rims(from_tiles(message_ref[...], 2), table_ref[...])
    slots_ref[...] = slots
    bent = total(slots[8:40] * applied_rows(slots, beta_x_ref[...], beta_y_ref[...], beta_z_ref[...]))
    crossed = total(slots[8:40] * applied_ref[...])
    row = lane_row([scalars_ref[...][:, 0:1], bent, crossed])
    out_ref[...] = jnp.broadcast_to(row[None], out_ref.shape)


def add_parts(parts_ref, out_ref):
    row = jnp.sum(parts_ref[...], axis=0)
    out_ref[...] = jnp.broadcast_to(row[None], out_ref.shape)


def finish(parts_ref, scalars_ref, first_ref, second_ref, beta_x_ref, beta_y_ref, beta_z_ref, provisional_ref, next_ref, pressure_ref):
    sums = jnp.sum(parts_ref[...], axis=0)
    renewed, bent, crossed = sums[:, 0:1], sums[:, 1:2], sums[:, 2:3]
    scalars = scalars_ref[...]
    aligned, curvature = scalars[:, 1:2], scalars[:, 2:3]
    ratio = renewed / aligned
    second_step = renewed / (bent + 2.0 * ratio * crossed + ratio * ratio * curvature)
    first = first_ref[...]
    slots = (aligned / curvature) * first + second_step * (second_ref[...] + ratio * first)
    parts = fluxes(slots, beta_x_ref[...], beta_y_ref[...], beta_z_ref[...])
    for y, (cells, fx, bx, fy, by, fz, bz) in enumerate(parts):
        pressure_ref[y] = cells
        next_ref[0, y] = provisional_ref[0, y] - 0.5 * (fx + bx)
        next_ref[1, y] = provisional_ref[1, y] - 0.5 * (fy + by)
        next_ref[2, y] = provisional_ref[2, y] - 0.5 * (fz + bz)


def run(kernel, outs, *arrays, last=False):
    whole = pl.BlockSpec(memory_space=pltpu.VMEM)
    scalar = pl.BlockSpec(memory_space=pltpu.SMEM)
    scalars = [array.ndim == 1 for array in arrays]
    kept = jax.ShapeDtypeStruct if last else pltpu.VMEM
    return pl.pallas_call(
        kernel,
        out_shape=[kept(shape, jnp.float32) for shape in outs],
        in_specs=[scalar if small else whole for small in scalars],
        out_specs=[whole] * len(outs),
        compiler_params=pltpu.CompilerParams(vmem_limit_bytes=8 << 20),
    )(
        *[
            array if small else pltpu.with_memory_space_constraint(array, pltpu.VMEM)
            for array, small in zip(arrays, scalars)
        ]
    )


def rim_slots():
    places = [(0, z + 1) for z in range(8)]
    places += [(y + 1, z + 1) for y in range(4) for z in range(8)]
    places += [(5, z + 1) for z in range(8)]
    places += [(y + 1, 0) for y in range(4)] + [(y + 1, 9) for y in range(4)]
    lanes = [
        [(y * 18 + 8 * core + z) * 4 + k for y, z in places] + [-1] * (64 - len(places))
        for core in range(2)
        for k in range(4)
    ]
    return np.array(lanes, np.int32).reshape(1, -1)


def field_slots():
    def lane(core, k, row):
        return core * 256 + k * 64 + row

    lanes = []
    for y in range(4):
        lanes += [lane(z // 8, k, 8 * y + z % 8) for z in range(16) for k in range(4)]
        for core, row in ((0, 48), (0, 52), (1, 48), (1, 52)):
            lanes += [lane(core, k, row + y) for k in range(4)]
        lanes += [-1] * 48
    for row in (32, 40):
        lanes += [lane(z // 8, k, row + z % 8) for z in range(16) for k in range(4)] + [-1] * 64
    return np.array(lanes, np.int32).reshape(1, -1)


def on_device(velocity, fraction, wall_flags):
    rows, cols = (fraction.shape[0], fraction.shape[1])
    rows_devices = lax.axis_size("py")
    chips = lax.axis_size("px")
    cores = lax.axis_size("core")
    cols_devices = chips * cores
    total_rows = rows * rows_devices
    row_index = lax.axis_index("py")
    chip_index = lax.axis_index("px")
    core_index = lax.axis_index("core")

    def y_layers(part):
        return part.reshape(9, cols, NX)

    y_head = jnp.concatenate([y_layers(velocity[:, :3]), fraction[:1]], axis=0)
    y_tail = jnp.concatenate([y_layers(velocity[:, -3:]), fraction[-1:]], axis=0)
    y_low, y_high = shifted_pair(y_head, y_tail, "py")

    def z_layers(first, only):
        lanes = jnp.transpose(velocity[:, :, first : first + 3], (0, 2, 1, 3)).reshape(9, rows, NX)
        return jnp.concatenate([lanes, fraction[:, only][None]], axis=0)

    z_low, z_high = shifted_pair(z_layers(0, 0), z_layers(cols - 3, cols - 1), ("px", "core"))

    def unlayered(z_rim):
        return jnp.transpose(z_rim[:9].reshape(3, 3, rows, NX), (0, 2, 1, 3))

    provisional = predicted(
        velocity,
        wall_ghosts(velocity, wall_flags),
        jnp.concatenate([y_low[:9].reshape(3, 3, cols, NX), velocity, y_high[:9].reshape(3, 3, cols, NX)], axis=1),
        jnp.concatenate([unlayered(z_low), velocity, unlayered(z_high)], axis=2),
        fraction,
    )

    peers = rows_devices * cores
    part_x = NX // peers
    plain_x = cosine_table(NX).reshape(peers, part_x, NX).transpose(1, 0, 2).reshape(NX, NX)
    table_x = jnp.asarray(plain_x, dtype=jnp.float32)
    (message,) = run(send_fields, [(peers, 2, 128)], provisional, table_x)

    places = jnp.stack([row_index, chip_index, core_index]).astype(jnp.int32)

    plain_y = cosine_table(total_rows).T.reshape(rows_devices, rows, total_rows)
    plain_y = plain_y.transpose(1, 0, 2).reshape(total_rows, total_rows)
    table_y = jnp.asarray(plain_y, dtype=jnp.float32)
    inner = np.arange(256)
    row_source = inner // 32 % 2 * 128 + inner % 4 * 32 + inner // 64 * 8 + inner // 4 % 8
    sources = jnp.asarray(np.concatenate([row_source[None].astype(np.int32), rim_slots(), field_slots()], axis=1))

    half_x = jnp.asarray(half_eigenvalue(NX), dtype=jnp.float32)
    half_y = half_eigenvalue(total_rows).reshape(2, 1, 128)
    half_y = jnp.asarray(np.broadcast_to(half_y, (2, 4, 128)).reshape(8, 128), dtype=jnp.float32)
    size = cols * cores
    *betas, rho, scale, weights = run(
        prepare,
        [(rows, cols, NX), (rows + 1, cols, NX), (2, rows, cols, NX), (8, 128), (8, 128), (4, chips, 8, 128)],
        places, half_x, half_y, fraction, y_low[9], y_high[9], z_low[9], z_high[9],
    )
    place = places[1:2]

    across = ("py", "core")
    layers_shape = (size, 8, 128)
    rims_shape = (rows_devices, 4, 128)
    message = exchange(message, across)
    message = message.reshape(rows_devices, 4, 128)
    gather, layers = run(
        read_fields, [(chips, 32, 128), layers_shape], message, table_y, sources, rho
    )
    gather = exchange(gather, "px")
    message, residual, waves, aligned = run(
        first_solve,
        [rims_shape, layers_shape, (2, 8, 128), (1, 128)],
        place, gather, layers, rho, scale, weights, table_y, sources,
    )
    message = exchange(message.reshape(peers, 2, 128), across)
    message, first, applied = run(
        first_image, [(peers, 2, 128), (64, NX), (32, NX)], message, aligned, table_x, *betas
    )
    message = exchange(message, across).reshape(rows_devices, 4, 128)
    gather, layers = run(
        read_image, [(chips, 24, 128), layers_shape], message, table_y, sources, rho
    )
    gather = exchange(gather, "px")
    message, scalars = run(
        second_solve,
        [rims_shape, (1, 128)],
        gather, layers, residual, waves, rho, scale, weights, table_y, sources,
    )
    message = exchange(message.reshape(peers, 2, 128), across)
    second, parts = run(
        second_image, [(64, NX), (rows_devices, 1, 128)], message, scalars, applied, table_x, *betas
    )
    (parts,) = run(add_parts, [(cols_devices, 1, 128)], exchange(parts, "py"))
    parts = exchange(parts, ("px", "core"))
    next_velocity, pressure = run(
        finish,
        [velocity.shape, fraction.shape],
        parts, scalars, first, second, *betas, provisional,
        last=True,
    )
    return next_velocity, pressure


def solution(mesh):
    rows = mesh.shape["py"]
    split = Mesh(mesh.devices.reshape(rows, -1, 2), ("py", "px", "core"))
    wide = P(None, "py", ("px", "core"), None)
    flat = P("py", ("px", "core"), None)
    return jax.shard_map(
        on_device,
        mesh=split,
        in_specs=(wide, flat, P(None, "py", ("px", "core"))),
        out_specs=(wide, flat),
        check_vma=False,
    )
```

```python
import jax
import jax.numpy as jnp
import numpy as np
from jax import lax
from jax.experimental import pallas as pl
from jax.experimental.pallas import tpu as pltpu
from jax.sharding import Mesh, PartitionSpec as P

NX = 512


time_step = 0.05
heavy_density = 8.0
light_viscosity = 0.3
heavy_viscosity = 0.6
compressibility = 0.001
mean_inverse = 0.5
weno_epsilon = 1e-06


def weno_blend(slope_one, slope_two, slope_three, slope_four, slope_five):
    smooth_one = (
        13.0 / 12.0 * (slope_one - 2.0 * slope_two + slope_three) ** 2
        + 0.25 * (slope_one - 4.0 * slope_two + 3.0 * slope_three) ** 2
    )
    smooth_two = (
        13.0 / 12.0 * (slope_two - 2.0 * slope_three + slope_four) ** 2
        + 0.25 * (slope_two - slope_four) ** 2
    )
    smooth_three = (
        13.0 / 12.0 * (slope_three - 2.0 * slope_four + slope_five) ** 2
        + 0.25 * (3.0 * slope_three - 4.0 * slope_four + slope_five) ** 2
    )
    scale_one = weno_epsilon + smooth_one
    scale_two = weno_epsilon + smooth_two
    scale_three = weno_epsilon + smooth_three
    alpha_one = 0.1 * (scale_two * scale_three) ** 2
    alpha_two = 0.6 * (scale_one * scale_three) ** 2
    alpha_three = 0.3 * (scale_one * scale_two) ** 2
    weight_sum = alpha_one + alpha_two + alpha_three
    blended = alpha_one * (slope_one / 3.0 - 7.0 * slope_two / 6.0 + 11.0 * slope_three / 6.0)
    blended = blended + alpha_two * (-slope_two / 6.0 + 5.0 * slope_three / 6.0 + slope_four / 3.0)
    blended = blended + alpha_three * (
        slope_three / 3.0 + 5.0 * slope_four / 6.0 - slope_five / 6.0
    )
    return blended / weight_sum


def upwind_derivative(padded, direction_axis, advecting):
    length = padded.shape[direction_axis] - 6
    differences = jnp.diff(padded, axis=direction_axis)
    rightward = advecting > 0

    def window(offset):
        return lax.slice_in_dim(differences, offset, offset + length, axis=direction_axis)

    return weno_blend(*[jnp.where(rightward, window(k), window(5 - k)) for k in range(5)])


def predicted(center, along_x, along_y, along_z, fraction):
    slope_x = upwind_derivative(along_x, 3, center[0][None])
    slope_y = upwind_derivative(along_y, 1, center[1][None])
    slope_z = upwind_derivative(along_z, 2, center[2][None])
    transport = center[0] * slope_x + center[1] * slope_y + center[2] * slope_z
    spread = along_x[..., 4:-2] + along_x[..., 2:-4] - 2.0 * center
    spread = spread + (along_y[:, 4:-2] + along_y[:, 2:-4] - 2.0 * center)
    spread = spread + (along_z[:, :, 4:-2] + along_z[:, :, 2:-4] - 2.0 * center)
    density = 1.0 + (heavy_density - 1.0) * fraction
    kinematic = (light_viscosity + (heavy_viscosity - light_viscosity) * fraction) / density
    return center + time_step * (kinematic * spread - transport)


def wall_ghosts(velocity, wall_flags):
    component = lax.broadcasted_iota(jnp.int32, (3, *wall_flags.shape), 0)
    mirror_signs = jnp.where((component == 0) | (wall_flags[None] == 0), -1.0, 1.0)
    lower_ghost = velocity[..., :3][..., ::-1] * mirror_signs[:, 0, :, :, None]
    upper_ghost = velocity[..., -3:][..., ::-1] * mirror_signs[:, 1, :, :, None]
    return jnp.concatenate([lower_ghost, velocity, upper_ghost], axis=-1)


def swapped(values, axis, pairs):
    return lax.ppermute(values, axis, pairs)


def shifted_pair(head, tail, axis):
    count = lax.axis_size(axis)
    even = (lax.axis_index(axis) & 1) == 0
    inner = [(i, i + 1) for i in range(0, count, 2)]
    outer = [(i, i + 1) for i in range(1, count - 1, 2)]
    two = swapped(jnp.where(even, head, tail), axis, outer + [(j, i) for i, j in outer])
    one = swapped(jnp.where(even, tail, head), axis, inner + [(j, i) for i, j in inner])
    return jnp.where(even, two, one), jnp.where(even, one, two)


def cosine_table(length):
    wave_index = np.arange(length)[:, None]
    position = np.arange(length)[None, :]
    angle = np.pi / (2 * length) * (wave_index * (2 * position + 1) % (4 * length))
    weight = np.where(wave_index == 0, np.sqrt(1.0 / length), np.sqrt(2.0 / length))
    return weight * np.cos(angle)


def half_eigenvalue(length):
    return mean_inverse * 4.0 * np.sin(np.pi * np.arange(length) / (2 * length)) ** 2


def exchange(message, axis):
    return lax.all_to_all(message, axis, split_axis=0, concat_axis=0, tiled=True)


def pieces_of(values):
    parts = []
    for _ in range(3):
        parts.append(values.astype(jnp.bfloat16))
        values = values - parts[-1].astype(jnp.float32)
    return parts


def dot(left, table_ref):
    parts = pieces_of(left)
    count = left.shape[0]
    total = None
    for order in (2, 1, 0):
        stacked = jnp.concatenate(parts[: 3 - order], axis=0)
        term = jnp.dot(stacked, table_ref[order], preferred_element_type=jnp.float32)
        for piece in range(3 - order):
            block = term[count * piece : count * piece + count]
            total = block if total is None else total + block
    return total


def dot_nt(table_ref, right):
    parts = pieces_of(right)
    total = None
    for order in (2, 1, 0):
        for part in parts[: 3 - order]:
            term = lax.dot_general(
                table_ref[order], part, (((1,), (1,)), ((), ())), preferred_element_type=jnp.float32
            )
            total = term if total is None else total + term
    return total


def rolled(values, shift, axis):
    return pltpu.roll(values, shift % values.shape[axis], axis)


def moved(values, step):
    row = lax.broadcasted_iota(jnp.int32, values.shape, 0)
    edge = 0 if step == 1 else values.shape[0] - 1
    return jnp.where(row == edge, 0.0, rolled(values, step, 0))


def picked(values, source):
    lane = lax.broadcasted_iota(jnp.int32, (values.shape[1], source.shape[1]), 0)
    chosen = jnp.where(lane == source, 1.0, 0.0).astype(jnp.bfloat16)
    count = values.shape[0]
    stacked = jnp.concatenate(pieces_of(values), axis=0)
    ordered = jnp.dot(stacked, chosen, preferred_element_type=jnp.float32)
    return ordered[:count] + ordered[count : 2 * count] + ordered[2 * count :]


def from_tiles(tiles, count):
    return jnp.concatenate([tiles[:, t, :] for t in range(count)], axis=1)


def into_tiles(ref, values):
    for t in range(values.shape[1] // 128):
        ref[:, t, :] = values[:, 128 * t : 128 * t + 128]


def to_message(rows, table_x):
    spectral = dot_nt(table_x, rows)
    devices = spectral.shape[0] // 4
    blocks = [spectral[devices * k : devices * k + devices] for k in range(4)]
    return jnp.concatenate(blocks, axis=1)


def to_layers(blocks, table_y):
    modes = dot(jnp.concatenate(blocks, axis=0).T, table_y)
    return [
        jnp.concatenate([modes[4 * r : 4 * r + 4, :128], modes[4 * r : 4 * r + 4, 128:]], axis=0)
        for r in range(modes.shape[0] // 4)
    ]


def from_layers(layers):
    return jnp.concatenate(
        [jnp.concatenate([layer[:4], layer[4:]], axis=1) for layer in layers], axis=0
    )


def moments(layers, rho):
    upward = layers[0]
    for layer in layers[1:]:
        upward = rho * upward + layer
    downward = layers[-1]
    for layer in layers[-2::-1]:
        downward = rho * downward + layer
    return upward, downward


def incoming(upward, downward, weights):
    low = jnp.sum(weights[0] * upward + weights[1] * downward, axis=0)
    high = jnp.sum(weights[2] * upward + weights[3] * downward, axis=0)
    return low, high


def solved(layers, low, high, rho, scale):
    inverse = 1.0 / rho
    wave = low * inverse
    forward = [wave]
    for layer in layers:
        wave = rho * wave + layer
        forward.append(wave)
    forward.append(rho * wave)
    wave = high
    backward = [high * inverse, high]
    for layer in layers[::-1]:
        wave = rho * (wave + layer)
        backward.append(wave)
    backward = backward[::-1]
    return [scale * (f + b) for f, b in zip(forward, backward)]


def layers_total(left, right):
    product = left[0] * right[0]
    for one, other in zip(left[1:], right[1:]):
        product = product + one * other
    return total(product)


def send_rims(out_ref, layers, table_y, source):
    rows = dot_nt(table_y, from_layers(layers))
    devices = rows.shape[0] // 4
    blocks = [rows[devices * y : devices * y + devices] for y in range(4)]
    blocks = [moved(blocks[3], 1), *blocks, moved(blocks[0], -1)]
    into_tiles(out_ref, picked(jnp.concatenate(blocks, axis=1), source))


def from_rims(message, table_x):
    stacked = jnp.concatenate([message[:, 64 * k : 64 * k + 64] for k in range(4)], axis=0)
    return dot(stacked.T, table_x)


def fluxes(slots, beta_x, beta_y, beta_z):
    tiles = [slots[8 * y : 8 * y + 8] for y in range(6)]
    flux_y = [beta_y[y] * (tiles[y + 1] - tiles[y]) for y in range(5)]
    layer = lax.broadcasted_iota(jnp.int32, tiles[0].shape, 0)
    results = []
    for y in range(4):
        cells = tiles[y + 1]
        forward_x = beta_x[y] * (rolled(cells, -1, 1) - cells)
        above = jnp.where(layer == 7, slots[52 + y : 53 + y], rolled(cells, -1, 0))
        below = jnp.where(layer == 0, slots[48 + y : 49 + y], rolled(cells, 1, 0))
        results.append(
            (
                cells,
                forward_x,
                rolled(forward_x, 1, 1),
                flux_y[y + 1],
                flux_y[y],
                beta_z[0, y] * (above - cells),
                beta_z[1, y] * (cells - below),
            )
        )
    return results


def applied_rows(slots, beta_x, beta_y, beta_z):
    rows = []
    for cells, fx, bx, fy, by, fz, bz in fluxes(slots, beta_x, beta_y, beta_z):
        rows.append(compressibility * cells - (fx - bx + (fy - by) + (fz - bz)))
    return jnp.concatenate(rows, axis=0)


def total(values):
    return jnp.sum(jnp.sum(values, axis=0, keepdims=True), axis=1, keepdims=True)


def lane_row(values):
    lane = lax.broadcasted_iota(jnp.int32, (1, 128), 1)
    row = jnp.zeros((1, 128), jnp.float32)
    for index, value in enumerate(values):
        row = jnp.where(lane == index, value, row)
    return row


def send_fields(provisional_ref, table_ref, out_ref, pieces_ref):
    for order, part in enumerate(pieces_of(table_ref[...])):
        pieces_ref[order] = part
    normal = provisional_ref[0].reshape(32, NX)
    lane = lax.broadcasted_iota(jnp.int32, normal.shape, 1)
    after = jnp.where(lane == NX - 1, -normal, rolled(normal, -1, 1))
    before = jnp.where(lane == 0, -normal, rolled(normal, 1, 1))
    across = -0.5 * (after - before)
    along_y = [provisional_ref[1, y] for y in range(4)]
    along_z = [provisional_ref[2, y] for y in range(4)]
    zero = jnp.zeros_like(along_y[0])
    layer = lax.broadcasted_iota(jnp.int32, zero.shape, 0)
    rows = []
    for y in range(4):
        rise = (along_y[y + 1] if y < 3 else zero) - (along_y[y - 1] if y > 0 else zero)
        above = jnp.where(layer == 7, 0.0, rolled(along_z[y], -1, 0))
        below = jnp.where(layer == 0, 0.0, rolled(along_z[y], 1, 0))
        rows.append(across[8 * y : 8 * y + 8] - 0.5 * rise - 0.5 * (above - below))
    rows += [along_y[0], along_y[3]]
    rows += [part[:1] for part in along_z] + [part[7:] for part in along_z] + [zero]
    into_tiles(out_ref, to_message(jnp.concatenate(rows, axis=0), pieces_ref))


def prepare(place_ref, half_x_ref, half_y_ref, table_ref, fraction_ref, y_low_ref, y_high_ref, z_low_ref, z_high_ref,
            beta_x_ref, beta_y_ref, beta_z_ref, rho_ref, scale_ref, weights_ref, pieces_ref):
    row, chip, core = place_ref[0], place_ref[1], place_ref[2]
    for order, part in enumerate(pieces_of(table_ref[...])):
        pieces_ref[order] = part

    def density_of(part):
        return 1.0 + (heavy_density - 1.0) * part

    cells = [density_of(fraction_ref[y]) for y in range(4)]
    under, over = density_of(z_low_ref[...]), density_of(z_high_ref[...])
    lane = lax.broadcasted_iota(jnp.int32, cells[0].shape, 1)
    layer = lax.broadcasted_iota(jnp.int32, cells[0].shape, 0)
    first_z = (layer == 0) & (chip == 0) & (core == 0)
    last_z = (layer == 7) & (chip == weights_ref.shape[1] - 1) & (core == 1)
    for y, own in enumerate(cells):
        beta_x_ref[y] = jnp.where(lane == NX - 1, 0.0, 2.0 / (own + rolled(own, -1, 1)))
        above = jnp.where(layer == 7, over[y : y + 1], rolled(own, -1, 0))
        below = jnp.where(layer == 0, under[y : y + 1], rolled(own, 1, 0))
        beta_z_ref[0, y] = jnp.where(last_z, 0.0, 2.0 / (own + above))
        beta_z_ref[1, y] = jnp.where(first_z, 0.0, 2.0 / (own + below))
    column = [density_of(y_low_ref[...]), *cells, density_of(y_high_ref[...])]
    for y in range(5):
        wall = (lane >= 0) & (row == (0 if y == 0 else 63)) if y in (0, 4) else lane < 0
        beta_y_ref[y] = jnp.where(wall, 0.0, 2.0 / (column[y + 1] + column[y]))
    mode = lax.broadcasted_iota(jnp.int32, rho_ref.shape, 0) % 4
    half_x = jnp.zeros(rho_ref.shape, jnp.float32)
    for k in range(4):
        half_x = jnp.where(mode == k, half_x_ref[(row * 2 + core) * 4 + k], half_x)
    shift = compressibility + half_x + half_y_ref[...]
    root = jnp.sqrt(shift * (shift + 2.0))
    rho = 1.0 / (1.0 + shift + root)
    rho_ref[...] = rho
    scale_ref[...] = 1.0 / root
    log_rho = jnp.log(rho)
    count, size = weights_ref.shape[1], 16
    period = 2 * size * count
    norm = 1.0 / (1.0 - jnp.exp(period * log_rho))
    for block in range(count):
        behind = size * (chip - block) - size + 1 + jnp.where(block < chip, 0, period)
        ahead = size * (block - chip) - size + 1 + jnp.where(block > chip, 0, period)
        low = size * (chip + block) + 1
        high = period - 2 * size + 1 - size * (chip + block)
        for side, exponent in enumerate((behind, low, high, ahead)):
            weights_ref[side, block] = jnp.exp(exponent.astype(jnp.float32) * log_rho) * norm


def read_fields(message_ref, table_ref, source_ref, rho_ref, gather_ref, layers_ref):
    tiles = message_ref[...]
    ordered = picked(from_tiles(tiles, 4), source_ref[:, 768:])
    blocks = [ordered[:, 128 * y : 128 * y + 128] for y in range(4)]
    blocks[0] = blocks[0] + 0.5 * moved(ordered[:, 640:768], 1)
    blocks[3] = blocks[3] - 0.5 * moved(ordered[:, 512:640], -1)
    layers = to_layers([block[:, :80] for block in blocks], table_ref)
    layers, edges = layers[:16], layers[16:]
    layers[7] = layers[7] - 0.5 * edges[2]
    layers[8] = layers[8] + 0.5 * edges[1]
    upward, downward = moments(layers, rho_ref[...])
    for device in range(gather_ref.shape[0]):
        gather_ref[device, 0:8] = upward
        gather_ref[device, 8:16] = downward
        gather_ref[device, 16:24] = edges[0]
        gather_ref[device, 24:32] = edges[3]
    for z, layer in enumerate(layers):
        layers_ref[z] = layer


def first_solve(place_ref, gather_ref, layers_ref, rho_ref, scale_ref, weights_ref, table_ref, source_ref,
                out_ref, residual_ref, waves_ref, aligned_ref):
    rho = rho_ref[...]
    square = rho * rho
    fourth = square * square
    power = fourth * fourth * fourth * square * rho
    gathered = gather_ref[...]
    first, last = gathered[:, 16:24], gathered[:, 24:32]
    zero = jnp.zeros_like(first[:1])
    under = 0.5 * jnp.concatenate([zero, last[:-1]], axis=0)
    over = -0.5 * jnp.concatenate([first[1:], zero], axis=0)
    upward = gathered[:, 0:8] + power * under + over
    downward = gathered[:, 8:16] + under + power * over
    low, high = incoming(upward, downward, weights_ref[...])
    mine = lax.broadcasted_iota(jnp.int32, under.shape, 0) == place_ref[0]
    layers = [layers_ref[z] for z in range(16)]
    layers[0] = layers[0] + jnp.sum(jnp.where(mine, under, 0.0), axis=0)
    layers[15] = layers[15] + jnp.sum(jnp.where(mine, over, 0.0), axis=0)
    modes = solved(layers, low, high, rho, scale_ref[...])
    aligned_ref[...] = lane_row([layers_total(layers, modes[1:-1])])
    for z, layer in enumerate(layers):
        residual_ref[z] = layer
    waves_ref[0] = low
    waves_ref[1] = high
    send_rims(out_ref, modes, table_ref, source_ref[:, 256:768])


def first_image(message_ref, aligned_ref, table_ref, beta_x_ref, beta_y_ref, beta_z_ref, out_ref, slots_ref, applied_ref):
    table = table_ref
    slots = from_rims(from_tiles(message_ref[...], 2), table)
    applied = applied_rows(slots, beta_x_ref[...], beta_y_ref[...], beta_z_ref[...])
    slots_ref[...] = slots
    applied_ref[...] = applied
    message = to_message(applied, table)
    curvature = total(slots[8:40] * applied)
    out_ref[:, 0, :] = message
    row = lane_row([aligned_ref[...][:, :1], curvature])
    out_ref[:, 1, :] = jnp.broadcast_to(row, message.shape)


def read_image(message_ref, table_ref, source_ref, rho_ref, gather_ref, layers_ref):
    tiles = message_ref[...]
    pair = jnp.concatenate([tiles[:, 0, :], tiles[:, 2, :]], axis=1)
    ordered = picked(pair, source_ref[:, :256])
    layers = to_layers([ordered[:, 64 * y : 64 * y + 64] for y in range(4)], table_ref)
    sums = jnp.sum(tiles[:, 1, :] + tiles[:, 3, :], axis=0, keepdims=True)
    upward, downward = moments(layers, rho_ref[...])
    sums = jnp.broadcast_to(sums, upward.shape)
    for device in range(gather_ref.shape[0]):
        gather_ref[device, 0:8] = upward
        gather_ref[device, 8:16] = downward
        gather_ref[device, 16:24] = sums
    for z, layer in enumerate(layers):
        layers_ref[z] = layer


def second_solve(gather_ref, layers_ref, residual_ref, waves_ref, rho_ref, scale_ref, weights_ref, table_ref, source_ref,
                 out_ref, scalars_ref):
    gathered = gather_ref[...]
    sums = jnp.sum(gathered[:, 16:24], axis=0)[:1]
    aligned, curvature = sums[:, 0:1], sums[:, 1:2]
    step = aligned / curvature
    low, high = incoming(gathered[:, 0:8], gathered[:, 8:16], weights_ref[...])
    layers = [residual_ref[z] - step * layers_ref[z] for z in range(16)]
    modes = solved(layers, waves_ref[0] - step * low, waves_ref[1] - step * high, rho_ref[...], scale_ref[...])
    scalars_ref[...] = lane_row([layers_total(layers, modes[1:-1]), aligned, curvature])
    send_rims(out_ref, modes, table_ref, source_ref[:, 256:768])


def second_image(message_ref, scalars_ref, applied_ref, table_ref, beta_x_ref, beta_y_ref, beta_z_ref, slots_ref, out_ref):
    slots = from_rims(from_tiles(message_ref[...], 2), table_ref)
    slots_ref[...] = slots
    bent = total(slots[8:40] * applied_rows(slots, beta_x_ref[...], beta_y_ref[...], beta_z_ref[...]))
    crossed = total(slots[8:40] * applied_ref[...])
    row = lane_row([scalars_ref[...][:, 0:1], bent, crossed])
    out_ref[...] = jnp.broadcast_to(row[None], out_ref.shape)


def add_parts(parts_ref, out_ref):
    row = jnp.sum(parts_ref[...], axis=0)
    out_ref[...] = jnp.broadcast_to(row[None], out_ref.shape)


def finish(parts_ref, scalars_ref, first_ref, second_ref, beta_x_ref, beta_y_ref, beta_z_ref, provisional_ref, next_ref, pressure_ref):
    sums = jnp.sum(parts_ref[...], axis=0)
    renewed, bent, crossed = sums[:, 0:1], sums[:, 1:2], sums[:, 2:3]
    scalars = scalars_ref[...]
    aligned, curvature = scalars[:, 1:2], scalars[:, 2:3]
    ratio = renewed / aligned
    second_step = renewed / (bent + 2.0 * ratio * crossed + ratio * ratio * curvature)
    first = first_ref[...]
    slots = (aligned / curvature) * first + second_step * (second_ref[...] + ratio * first)
    parts = fluxes(slots, beta_x_ref[...], beta_y_ref[...], beta_z_ref[...])
    for y, (cells, fx, bx, fy, by, fz, bz) in enumerate(parts):
        pressure_ref[y] = cells
        next_ref[0, y] = provisional_ref[0, y] - 0.5 * (fx + bx)
        next_ref[1, y] = provisional_ref[1, y] - 0.5 * (fy + by)
        next_ref[2, y] = provisional_ref[2, y] - 0.5 * (fz + bz)


def run(kernel, outs, *arrays, last=False):
    whole = pl.BlockSpec(memory_space=pltpu.VMEM)
    scalar = pl.BlockSpec(memory_space=pltpu.SMEM)
    scalars = [array.ndim == 1 for array in arrays]
    kept = jax.ShapeDtypeStruct if last else pltpu.VMEM
    return pl.pallas_call(
        kernel,
        out_shape=[kept(shape, jnp.bfloat16 if shape[0] == 3 and not last else jnp.float32) for shape in outs],
        in_specs=[scalar if small else whole for small in scalars],
        out_specs=[whole] * len(outs),
        compiler_params=pltpu.CompilerParams(vmem_limit_bytes=8 << 20),
    )(
        *[
            array if small else pltpu.with_memory_space_constraint(array, pltpu.VMEM)
            for array, small in zip(arrays, scalars)
        ]
    )


def rim_slots():
    places = [(0, z + 1) for z in range(8)]
    places += [(y + 1, z + 1) for y in range(4) for z in range(8)]
    places += [(5, z + 1) for z in range(8)]
    places += [(y + 1, 0) for y in range(4)] + [(y + 1, 9) for y in range(4)]
    lanes = [
        [(y * 18 + 8 * core + z) * 4 + k for y, z in places] + [-1] * (64 - len(places))
        for core in range(2)
        for k in range(4)
    ]
    return np.array(lanes, np.int32).reshape(1, -1)


def field_slots():
    def lane(core, k, row):
        return core * 256 + k * 64 + row

    lanes = []
    for y in range(4):
        lanes += [lane(z // 8, k, 8 * y + z % 8) for z in range(16) for k in range(4)]
        for core, row in ((0, 48), (0, 52), (1, 48), (1, 52)):
            lanes += [lane(core, k, row + y) for k in range(4)]
        lanes += [-1] * 48
    for row in (32, 40):
        lanes += [lane(z // 8, k, row + z % 8) for z in range(16) for k in range(4)] + [-1] * 64
    return np.array(lanes, np.int32).reshape(1, -1)


def on_device(velocity, fraction, wall_flags):
    rows, cols = (fraction.shape[0], fraction.shape[1])
    rows_devices = lax.axis_size("py")
    chips = lax.axis_size("px")
    cores = lax.axis_size("core")
    cols_devices = chips * cores
    total_rows = rows * rows_devices
    row_index = lax.axis_index("py")
    chip_index = lax.axis_index("px")
    core_index = lax.axis_index("core")

    def y_layers(part):
        return part.reshape(9, cols, NX)

    y_head = jnp.concatenate([y_layers(velocity[:, :3]), fraction[:1]], axis=0)
    y_tail = jnp.concatenate([y_layers(velocity[:, -3:]), fraction[-1:]], axis=0)
    y_low, y_high = shifted_pair(y_head, y_tail, "py")

    def z_layers(first, only):
        lanes = jnp.transpose(velocity[:, :, first : first + 3], (0, 2, 1, 3)).reshape(9, rows, NX)
        return jnp.concatenate([lanes, fraction[:, only][None]], axis=0)

    z_low, z_high = shifted_pair(z_layers(0, 0), z_layers(cols - 3, cols - 1), ("px", "core"))

    def unlayered(z_rim):
        return jnp.transpose(z_rim[:9].reshape(3, 3, rows, NX), (0, 2, 1, 3))

    provisional = predicted(
        velocity,
        wall_ghosts(velocity, wall_flags),
        jnp.concatenate([y_low[:9].reshape(3, 3, cols, NX), velocity, y_high[:9].reshape(3, 3, cols, NX)], axis=1),
        jnp.concatenate([unlayered(z_low), velocity, unlayered(z_high)], axis=2),
        fraction,
    )

    peers = rows_devices * cores
    part_x = NX // peers
    plain_x = cosine_table(NX).reshape(peers, part_x, NX).transpose(1, 0, 2).reshape(NX, NX)
    table_x = jnp.asarray(plain_x, dtype=jnp.float32)
    message, table_x = run(send_fields, [(peers, 2, 128), (3, NX, NX)], provisional, table_x)

    places = jnp.stack([row_index, chip_index, core_index]).astype(jnp.int32)

    plain_y = cosine_table(total_rows).T.reshape(rows_devices, rows, total_rows)
    plain_y = plain_y.transpose(1, 0, 2).reshape(total_rows, total_rows)
    table_y = jnp.asarray(plain_y, dtype=jnp.float32)
    inner = np.arange(256)
    row_source = inner // 32 % 2 * 128 + inner % 4 * 32 + inner // 64 * 8 + inner // 4 % 8
    sources = jnp.asarray(np.concatenate([row_source[None].astype(np.int32), rim_slots(), field_slots()], axis=1))

    half_x = jnp.asarray(half_eigenvalue(NX), dtype=jnp.float32)
    half_y = half_eigenvalue(total_rows).reshape(2, 1, 128)
    half_y = jnp.asarray(np.broadcast_to(half_y, (2, 4, 128)).reshape(8, 128), dtype=jnp.float32)
    size = cols * cores
    *betas, rho, scale, weights, table_y = run(
        prepare,
        [(rows, cols, NX), (rows + 1, cols, NX), (2, rows, cols, NX), (8, 128), (8, 128), (4, chips, 8, 128), (3, total_rows, total_rows)],
        places, half_x, half_y, table_y, fraction, y_low[9], y_high[9], z_low[9], z_high[9],
    )
    place = places[1:2]

    across = ("py", "core")
    layers_shape = (size, 8, 128)
    rims_shape = (rows_devices, 4, 128)
    message = exchange(message, across)
    message = message.reshape(rows_devices, 4, 128)
    gather, layers = run(
        read_fields, [(chips, 32, 128), layers_shape], message, table_y, sources, rho
    )
    gather = exchange(gather, "px")
    message, residual, waves, aligned = run(
        first_solve,
        [rims_shape, layers_shape, (2, 8, 128), (1, 128)],
        place, gather, layers, rho, scale, weights, table_y, sources,
    )
    message = exchange(message.reshape(peers, 2, 128), across)
    message, first, applied = run(
        first_image, [(peers, 2, 128), (64, NX), (32, NX)], message, aligned, table_x, *betas
    )
    message = exchange(message, across).reshape(rows_devices, 4, 128)
    gather, layers = run(
        read_image, [(chips, 24, 128), layers_shape], message, table_y, sources, rho
    )
    gather = exchange(gather, "px")
    message, scalars = run(
        second_solve,
        [rims_shape, (1, 128)],
        gather, layers, residual, waves, rho, scale, weights, table_y, sources,
    )
    message = exchange(message.reshape(peers, 2, 128), across)
    second, parts = run(
        second_image, [(64, NX), (rows_devices, 1, 128)], message, scalars, applied, table_x, *betas
    )
    (parts,) = run(add_parts, [(cols_devices, 1, 128)], exchange(parts, "py"))
    parts = exchange(parts, ("px", "core"))
    next_velocity, pressure = run(
        finish,
        [velocity.shape, fraction.shape],
        parts, scalars, first, second, *betas, provisional,
        last=True,
    )
    return next_velocity, pressure


def solution(mesh):
    rows = mesh.shape["py"]
    split = Mesh(mesh.devices.reshape(rows, -1, 2), ("py", "px", "core"))
    wide = P(None, "py", ("px", "core"), None)
    flat = P("py", ("px", "core"), None)
    return jax.shard_map(
        on_device,
        mesh=split,
        in_specs=(wide, flat, P(None, "py", ("px", "core"))),
        out_specs=(wide, flat),
        check_vma=False,
    )
```

```python
import jax
import jax.numpy as jnp
import numpy as np
from jax import lax
from jax.experimental import pallas as pl
from jax.experimental.pallas import tpu as pltpu
from jax.sharding import Mesh, PartitionSpec as P

NX = 512


time_step = 0.05
heavy_density = 8.0
light_viscosity = 0.3
heavy_viscosity = 0.6
compressibility = 0.001
mean_inverse = 0.5
weno_epsilon = 1e-06


def weno_blend(slope_one, slope_two, slope_three, slope_four, slope_five):
    smooth_one = (
        13.0 / 12.0 * (slope_one - 2.0 * slope_two + slope_three) ** 2
        + 0.25 * (slope_one - 4.0 * slope_two + 3.0 * slope_three) ** 2
    )
    smooth_two = (
        13.0 / 12.0 * (slope_two - 2.0 * slope_three + slope_four) ** 2
        + 0.25 * (slope_two - slope_four) ** 2
    )
    smooth_three = (
        13.0 / 12.0 * (slope_three - 2.0 * slope_four + slope_five) ** 2
        + 0.25 * (3.0 * slope_three - 4.0 * slope_four + slope_five) ** 2
    )
    scale_one = weno_epsilon + smooth_one
    scale_two = weno_epsilon + smooth_two
    scale_three = weno_epsilon + smooth_three
    alpha_one = 0.1 * (scale_two * scale_three) ** 2
    alpha_two = 0.6 * (scale_one * scale_three) ** 2
    alpha_three = 0.3 * (scale_one * scale_two) ** 2
    weight_sum = alpha_one + alpha_two + alpha_three
    blended = alpha_one * (slope_one / 3.0 - 7.0 * slope_two / 6.0 + 11.0 * slope_three / 6.0)
    blended = blended + alpha_two * (-slope_two / 6.0 + 5.0 * slope_three / 6.0 + slope_four / 3.0)
    blended = blended + alpha_three * (
        slope_three / 3.0 + 5.0 * slope_four / 6.0 - slope_five / 6.0
    )
    return blended / weight_sum


def upwind_derivative(padded, direction_axis, advecting):
    length = padded.shape[direction_axis] - 6
    differences = jnp.diff(padded, axis=direction_axis)
    rightward = advecting > 0

    def window(offset):
        return lax.slice_in_dim(differences, offset, offset + length, axis=direction_axis)

    return weno_blend(*[jnp.where(rightward, window(k), window(5 - k)) for k in range(5)])


def predicted(center, along_x, along_y, along_z, fraction):
    slope_x = upwind_derivative(along_x, 3, center[0][None])
    slope_y = upwind_derivative(along_y, 1, center[1][None])
    slope_z = upwind_derivative(along_z, 2, center[2][None])
    transport = center[0] * slope_x + center[1] * slope_y + center[2] * slope_z
    spread = along_x[..., 4:-2] + along_x[..., 2:-4] - 2.0 * center
    spread = spread + (along_y[:, 4:-2] + along_y[:, 2:-4] - 2.0 * center)
    spread = spread + (along_z[:, :, 4:-2] + along_z[:, :, 2:-4] - 2.0 * center)
    density = 1.0 + (heavy_density - 1.0) * fraction
    kinematic = (light_viscosity + (heavy_viscosity - light_viscosity) * fraction) / density
    return center + time_step * (kinematic * spread - transport)


def wall_ghosts(velocity, wall_flags):
    component = lax.broadcasted_iota(jnp.int32, (3, *wall_flags.shape), 0)
    mirror_signs = jnp.where((component == 0) | (wall_flags[None] == 0), -1.0, 1.0)
    lower_ghost = velocity[..., :3][..., ::-1] * mirror_signs[:, 0, :, :, None]
    upper_ghost = velocity[..., -3:][..., ::-1] * mirror_signs[:, 1, :, :, None]
    return jnp.concatenate([lower_ghost, velocity, upper_ghost], axis=-1)


def swapped(values, axis, pairs):
    return lax.ppermute(values, axis, pairs)


def shifted_pair(one, two, axis):
    count = lax.axis_size(axis)
    even = (lax.axis_index(axis) & 1) == 0
    inner = [(i, i + 1) for i in range(0, count, 2)]
    outer = [(i, i + 1) for i in range(1, count - 1, 2)]
    one = swapped(one, axis, inner + [(j, i) for i, j in inner])
    two = swapped(two, axis, outer + [(j, i) for i, j in outer])
    return jnp.where(even, two, one), jnp.where(even, one, two)


def cosine_table(length):
    wave_index = np.arange(length)[:, None]
    position = np.arange(length)[None, :]
    angle = np.pi / (2 * length) * (wave_index * (2 * position + 1) % (4 * length))
    weight = np.where(wave_index == 0, np.sqrt(1.0 / length), np.sqrt(2.0 / length))
    return weight * np.cos(angle)


def half_eigenvalue(length):
    return mean_inverse * 4.0 * np.sin(np.pi * np.arange(length) / (2 * length)) ** 2


def exchange(message, axis):
    return lax.all_to_all(message, axis, split_axis=0, concat_axis=0, tiled=True)


def pieces_of(values):
    parts = []
    for _ in range(3):
        parts.append(values.astype(jnp.bfloat16))
        values = values - parts[-1].astype(jnp.float32)
    return parts


def dot(left, table_ref):
    parts = pieces_of(left)
    count = left.shape[0]
    total = None
    for order in (2, 1, 0):
        stacked = jnp.concatenate(parts[: 3 - order], axis=0)
        term = jnp.dot(stacked, table_ref[order], preferred_element_type=jnp.float32)
        for piece in range(3 - order):
            block = term[count * piece : count * piece + count]
            total = block if total is None else total + block
    return total


def dot_nt(table_ref, right):
    parts = pieces_of(right)
    total = None
    for order in (2, 1, 0):
        for part in parts[: 3 - order]:
            term = lax.dot_general(
                table_ref[order], part, (((1,), (1,)), ((), ())), preferred_element_type=jnp.float32
            )
            total = term if total is None else total + term
    return total


def rolled(values, shift, axis):
    return pltpu.roll(values, shift % values.shape[axis], axis)


def moved(values, step):
    row = lax.broadcasted_iota(jnp.int32, values.shape, 0)
    edge = 0 if step == 1 else values.shape[0] - 1
    return jnp.where(row == edge, 0.0, rolled(values, step, 0))


def picked(values, source):
    lane = lax.broadcasted_iota(jnp.int32, (values.shape[1], source.shape[1]), 0)
    chosen = jnp.where(lane == source, 1.0, 0.0).astype(jnp.bfloat16)
    count = values.shape[0]
    stacked = jnp.concatenate(pieces_of(values), axis=0)
    ordered = jnp.dot(stacked, chosen, preferred_element_type=jnp.float32)
    return ordered[:count] + ordered[count : 2 * count] + ordered[2 * count :]


def from_tiles(tiles, count):
    return jnp.concatenate([tiles[:, t, :] for t in range(count)], axis=1)


def into_tiles(ref, values):
    for t in range(values.shape[1] // 128):
        ref[:, t, :] = values[:, 128 * t : 128 * t + 128]


def to_message(rows, table_x):
    spectral = dot_nt(table_x, rows)
    devices = spectral.shape[0] // 4
    blocks = [spectral[devices * k : devices * k + devices] for k in range(4)]
    return jnp.concatenate(blocks, axis=1)


def to_layers(blocks, table_y):
    modes = dot(jnp.concatenate(blocks, axis=0).T, table_y)
    return [
        jnp.concatenate([modes[4 * r : 4 * r + 4, :128], modes[4 * r : 4 * r + 4, 128:]], axis=0)
        for r in range(modes.shape[0] // 4)
    ]


def from_layers(layers):
    return jnp.concatenate(
        [jnp.concatenate([layer[:4], layer[4:]], axis=1) for layer in layers], axis=0
    )


def moments(layers, rho):
    upward = layers[0]
    for layer in layers[1:]:
        upward = rho * upward + layer
    downward = layers[-1]
    for layer in layers[-2::-1]:
        downward = rho * downward + layer
    return upward, downward


def incoming(upward, downward, weights):
    low = jnp.sum(weights[0] * upward + weights[1] * downward, axis=0)
    high = jnp.sum(weights[2] * upward + weights[3] * downward, axis=0)
    return low, high


def solved(layers, low, high, rho, scale):
    inverse = 1.0 / rho
    wave = low * inverse
    forward = [wave]
    for layer in layers:
        wave = rho * wave + layer
        forward.append(wave)
    forward.append(rho * wave)
    wave = high
    backward = [high * inverse, high]
    for layer in layers[::-1]:
        wave = rho * (wave + layer)
        backward.append(wave)
    backward = backward[::-1]
    return [scale * (f + b) for f, b in zip(forward, backward)]


def layers_total(left, right):
    product = left[0] * right[0]
    for one, other in zip(left[1:], right[1:]):
        product = product + one * other
    return total(product)


def send_rims(out_ref, layers, table_y, source):
    rows = dot_nt(table_y, from_layers(layers))
    devices = rows.shape[0] // 4
    blocks = [rows[devices * y : devices * y + devices] for y in range(4)]
    blocks = [moved(blocks[3], 1), *blocks, moved(blocks[0], -1)]
    into_tiles(out_ref, picked(jnp.concatenate(blocks, axis=1), source))


def from_rims(message, table_x):
    stacked = jnp.concatenate([message[:, 64 * k : 64 * k + 64] for k in range(4)], axis=0)
    return dot(stacked.T, table_x)


def fluxes(slots, beta_x, beta_y, beta_z):
    tiles = [slots[8 * y : 8 * y + 8] for y in range(6)]
    flux_y = [beta_y[y] * (tiles[y + 1] - tiles[y]) for y in range(5)]
    layer = lax.broadcasted_iota(jnp.int32, tiles[0].shape, 0)
    results = []
    for y in range(4):
        cells = tiles[y + 1]
        forward_x = beta_x[y] * (rolled(cells, -1, 1) - cells)
        above = jnp.where(layer == 7, slots[52 + y : 53 + y], rolled(cells, -1, 0))
        below = jnp.where(layer == 0, slots[48 + y : 49 + y], rolled(cells, 1, 0))
        results.append(
            (
                cells,
                forward_x,
                rolled(forward_x, 1, 1),
                flux_y[y + 1],
                flux_y[y],
                beta_z[0, y] * (above - cells),
                beta_z[1, y] * (cells - below),
            )
        )
    return results


def applied_rows(slots, beta_x, beta_y, beta_z):
    rows = []
    for cells, fx, bx, fy, by, fz, bz in fluxes(slots, beta_x, beta_y, beta_z):
        rows.append(compressibility * cells - (fx - bx + (fy - by) + (fz - bz)))
    return jnp.concatenate(rows, axis=0)


def total(values):
    return jnp.sum(jnp.sum(values, axis=0, keepdims=True), axis=1, keepdims=True)


def lane_row(values):
    lane = lax.broadcasted_iota(jnp.int32, (1, 128), 1)
    row = jnp.zeros((1, 128), jnp.float32)
    for index, value in enumerate(values):
        row = jnp.where(lane == index, value, row)
    return row


def rims(odd_ref, velocity_ref, fraction_ref, y_one_ref, y_two_ref, z_one_ref, z_two_ref):
    odd_y, odd_z = odd_ref[0] == 1, odd_ref[1] == 1

    def place(one_ref, two_ref, index, head, tail, odd):
        one_ref[index] = jnp.where(odd, head, tail)
        two_ref[index] = jnp.where(odd, tail, head)

    for c in range(3):
        for m in range(3):
            place(y_one_ref, y_two_ref, 3 * c + m, velocity_ref[c, m], velocity_ref[c, m + 1], odd_y)
            place(z_one_ref, z_two_ref, 3 * c + m, velocity_ref[c, :, m, :], velocity_ref[c, :, m + 5, :], odd_z)
    place(y_one_ref, y_two_ref, 9, fraction_ref[0], fraction_ref[3], odd_y)
    place(z_one_ref, z_two_ref, 9, fraction_ref[:, 0, :], fraction_ref[:, 7, :], odd_z)


def send_fields(provisional_ref, table_ref, out_ref, pieces_ref):
    for order, part in enumerate(pieces_of(table_ref[...])):
        pieces_ref[order] = part
    normal = provisional_ref[0].reshape(32, NX)
    lane = lax.broadcasted_iota(jnp.int32, normal.shape, 1)
    after = jnp.where(lane == NX - 1, -normal, rolled(normal, -1, 1))
    before = jnp.where(lane == 0, -normal, rolled(normal, 1, 1))
    across = -0.5 * (after - before)
    along_y = [provisional_ref[1, y] for y in range(4)]
    along_z = [provisional_ref[2, y] for y in range(4)]
    zero = jnp.zeros_like(along_y[0])
    layer = lax.broadcasted_iota(jnp.int32, zero.shape, 0)
    rows = []
    for y in range(4):
        rise = (along_y[y + 1] if y < 3 else zero) - (along_y[y - 1] if y > 0 else zero)
        above = jnp.where(layer == 7, 0.0, rolled(along_z[y], -1, 0))
        below = jnp.where(layer == 0, 0.0, rolled(along_z[y], 1, 0))
        rows.append(across[8 * y : 8 * y + 8] - 0.5 * rise - 0.5 * (above - below))
    rows += [along_y[0], along_y[3]]
    rows += [part[:1] for part in along_z] + [part[7:] for part in along_z] + [zero]
    into_tiles(out_ref, to_message(jnp.concatenate(rows, axis=0), pieces_ref))


def prepare(place_ref, half_x_ref, half_y_ref, table_ref, fraction_ref, y_low_ref, y_high_ref, z_low_ref, z_high_ref,
            beta_x_ref, beta_y_ref, beta_z_ref, rho_ref, scale_ref, weights_ref, pieces_ref):
    row, chip, core = place_ref[0], place_ref[1], place_ref[2]
    for order, part in enumerate(pieces_of(table_ref[...])):
        pieces_ref[order] = part

    def density_of(part):
        return 1.0 + (heavy_density - 1.0) * part

    cells = [density_of(fraction_ref[y]) for y in range(4)]
    under, over = density_of(z_low_ref[...]), density_of(z_high_ref[...])
    lane = lax.broadcasted_iota(jnp.int32, cells[0].shape, 1)
    layer = lax.broadcasted_iota(jnp.int32, cells[0].shape, 0)
    first_z = (layer == 0) & (chip == 0) & (core == 0)
    last_z = (layer == 7) & (chip == weights_ref.shape[1] - 1) & (core == 1)
    for y, own in enumerate(cells):
        beta_x_ref[y] = jnp.where(lane == NX - 1, 0.0, 2.0 / (own + rolled(own, -1, 1)))
        above = jnp.where(layer == 7, over[y : y + 1], rolled(own, -1, 0))
        below = jnp.where(layer == 0, under[y : y + 1], rolled(own, 1, 0))
        beta_z_ref[0, y] = jnp.where(last_z, 0.0, 2.0 / (own + above))
        beta_z_ref[1, y] = jnp.where(first_z, 0.0, 2.0 / (own + below))
    column = [density_of(y_low_ref[...]), *cells, density_of(y_high_ref[...])]
    for y in range(5):
        wall = (lane >= 0) & (row == (0 if y == 0 else 63)) if y in (0, 4) else lane < 0
        beta_y_ref[y] = jnp.where(wall, 0.0, 2.0 / (column[y + 1] + column[y]))
    mode = lax.broadcasted_iota(jnp.int32, rho_ref.shape, 0) % 4
    half_x = jnp.zeros(rho_ref.shape, jnp.float32)
    for k in range(4):
        half_x = jnp.where(mode == k, half_x_ref[(row * 2 + core) * 4 + k], half_x)
    shift = compressibility + half_x + half_y_ref[...]
    root = jnp.sqrt(shift * (shift + 2.0))
    rho = 1.0 / (1.0 + shift + root)
    rho_ref[...] = rho
    scale_ref[...] = 1.0 / root
    log_rho = jnp.log(rho)
    count, size = weights_ref.shape[1], 16
    period = 2 * size * count
    norm = 1.0 / (1.0 - jnp.exp(period * log_rho))
    for block in range(count):
        behind = size * (chip - block) - size + 1 + jnp.where(block < chip, 0, period)
        ahead = size * (block - chip) - size + 1 + jnp.where(block > chip, 0, period)
        low = size * (chip + block) + 1
        high = period - 2 * size + 1 - size * (chip + block)
        for side, exponent in enumerate((behind, low, high, ahead)):
            weights_ref[side, block] = jnp.exp(exponent.astype(jnp.float32) * log_rho) * norm


def read_fields(message_ref, table_ref, source_ref, rho_ref, gather_ref, layers_ref):
    tiles = message_ref[...]
    ordered = picked(from_tiles(tiles, 4), source_ref[:, 768:])
    blocks = [ordered[:, 128 * y : 128 * y + 128] for y in range(4)]
    blocks[0] = blocks[0] + 0.5 * moved(ordered[:, 640:768], 1)
    blocks[3] = blocks[3] - 0.5 * moved(ordered[:, 512:640], -1)
    layers = to_layers([block[:, :80] for block in blocks], table_ref)
    layers, edges = layers[:16], layers[16:]
    layers[7] = layers[7] - 0.5 * edges[2]
    layers[8] = layers[8] + 0.5 * edges[1]
    upward, downward = moments(layers, rho_ref[...])
    for device in range(gather_ref.shape[0]):
        gather_ref[device, 0:8] = upward
        gather_ref[device, 8:16] = downward
        gather_ref[device, 16:24] = edges[0]
        gather_ref[device, 24:32] = edges[3]
    for z, layer in enumerate(layers):
        layers_ref[z] = layer


def first_solve(place_ref, gather_ref, layers_ref, rho_ref, scale_ref, weights_ref, table_ref, source_ref,
                out_ref, residual_ref, waves_ref, aligned_ref):
    rho = rho_ref[...]
    square = rho * rho
    fourth = square * square
    power = fourth * fourth * fourth * square * rho
    gathered = gather_ref[...]
    first, last = gathered[:, 16:24], gathered[:, 24:32]
    zero = jnp.zeros_like(first[:1])
    under = 0.5 * jnp.concatenate([zero, last[:-1]], axis=0)
    over = -0.5 * jnp.concatenate([first[1:], zero], axis=0)
    upward = gathered[:, 0:8] + power * under + over
    downward = gathered[:, 8:16] + under + power * over
    low, high = incoming(upward, downward, weights_ref[...])
    mine = lax.broadcasted_iota(jnp.int32, under.shape, 0) == place_ref[0]
    layers = [layers_ref[z] for z in range(16)]
    layers[0] = layers[0] + jnp.sum(jnp.where(mine, under, 0.0), axis=0)
    layers[15] = layers[15] + jnp.sum(jnp.where(mine, over, 0.0), axis=0)
    modes = solved(layers, low, high, rho, scale_ref[...])
    aligned_ref[...] = lane_row([layers_total(layers, modes[1:-1])])
    for z, layer in enumerate(layers):
        residual_ref[z] = layer
    waves_ref[0] = low
    waves_ref[1] = high
    send_rims(out_ref, modes, table_ref, source_ref[:, 256:768])


def first_image(message_ref, aligned_ref, table_ref, beta_x_ref, beta_y_ref, beta_z_ref, out_ref, slots_ref, applied_ref):
    table = table_ref
    slots = from_rims(from_tiles(message_ref[...], 2), table)
    applied = applied_rows(slots, beta_x_ref[...], beta_y_ref[...], beta_z_ref[...])
    slots_ref[...] = slots
    applied_ref[...] = applied
    message = to_message(applied, table)
    curvature = total(slots[8:40] * applied)
    out_ref[:, 0, :] = message
    row = lane_row([aligned_ref[...][:, :1], curvature])
    out_ref[:, 1, :] = jnp.broadcast_to(row, message.shape)


def read_image(message_ref, table_ref, source_ref, rho_ref, gather_ref, layers_ref):
    tiles = message_ref[...]
    pair = jnp.concatenate([tiles[:, 0, :], tiles[:, 2, :]], axis=1)
    ordered = picked(pair, source_ref[:, :256])
    layers = to_layers([ordered[:, 64 * y : 64 * y + 64] for y in range(4)], table_ref)
    sums = jnp.sum(tiles[:, 1, :] + tiles[:, 3, :], axis=0, keepdims=True)
    upward, downward = moments(layers, rho_ref[...])
    sums = jnp.broadcast_to(sums, upward.shape)
    for device in range(gather_ref.shape[0]):
        gather_ref[device, 0:8] = upward
        gather_ref[device, 8:16] = downward
        gather_ref[device, 16:24] = sums
    for z, layer in enumerate(layers):
        layers_ref[z] = layer


def second_solve(gather_ref, layers_ref, residual_ref, waves_ref, rho_ref, scale_ref, weights_ref, table_ref, source_ref,
                 out_ref, scalars_ref):
    gathered = gather_ref[...]
    sums = jnp.sum(gathered[:, 16:24], axis=0)[:1]
    aligned, curvature = sums[:, 0:1], sums[:, 1:2]
    step = aligned / curvature
    low, high = incoming(gathered[:, 0:8], gathered[:, 8:16], weights_ref[...])
    layers = [residual_ref[z] - step * layers_ref[z] for z in range(16)]
    modes = solved(layers, waves_ref[0] - step * low, waves_ref[1] - step * high, rho_ref[...], scale_ref[...])
    scalars_ref[...] = lane_row([layers_total(layers, modes[1:-1]), aligned, curvature])
    send_rims(out_ref, modes, table_ref, source_ref[:, 256:768])


def second_image(message_ref, scalars_ref, applied_ref, table_ref, beta_x_ref, beta_y_ref, beta_z_ref, slots_ref, out_ref):
    slots = from_rims(from_tiles(message_ref[...], 2), table_ref)
    slots_ref[...] = slots
    bent = total(slots[8:40] * applied_rows(slots, beta_x_ref[...], beta_y_ref[...], beta_z_ref[...]))
    crossed = total(slots[8:40] * applied_ref[...])
    row = lane_row([scalars_ref[...][:, 0:1], bent, crossed])
    out_ref[...] = jnp.broadcast_to(row[None], out_ref.shape)


def add_parts(parts_ref, out_ref):
    row = jnp.sum(parts_ref[...], axis=0)
    out_ref[...] = jnp.broadcast_to(row[None], out_ref.shape)


def finish(parts_ref, scalars_ref, first_ref, second_ref, beta_x_ref, beta_y_ref, beta_z_ref, provisional_ref, next_ref, pressure_ref):
    sums = jnp.sum(parts_ref[...], axis=0)
    renewed, bent, crossed = sums[:, 0:1], sums[:, 1:2], sums[:, 2:3]
    scalars = scalars_ref[...]
    aligned, curvature = scalars[:, 1:2], scalars[:, 2:3]
    ratio = renewed / aligned
    second_step = renewed / (bent + 2.0 * ratio * crossed + ratio * ratio * curvature)
    first = first_ref[...]
    slots = (aligned / curvature) * first + second_step * (second_ref[...] + ratio * first)
    parts = fluxes(slots, beta_x_ref[...], beta_y_ref[...], beta_z_ref[...])
    for y, (cells, fx, bx, fy, by, fz, bz) in enumerate(parts):
        pressure_ref[y] = cells
        next_ref[0, y] = provisional_ref[0, y] - 0.5 * (fx + bx)
        next_ref[1, y] = provisional_ref[1, y] - 0.5 * (fy + by)
        next_ref[2, y] = provisional_ref[2, y] - 0.5 * (fz + bz)


def run(kernel, outs, *arrays, last=False):
    whole = pl.BlockSpec(memory_space=pltpu.VMEM)
    scalar = pl.BlockSpec(memory_space=pltpu.SMEM)
    scalars = [array.ndim == 1 for array in arrays]
    kept = jax.ShapeDtypeStruct if last else pltpu.VMEM
    return pl.pallas_call(
        kernel,
        out_shape=[kept(shape, jnp.bfloat16 if shape[0] == 3 and not last else jnp.float32) for shape in outs],
        in_specs=[scalar if small else whole for small in scalars],
        out_specs=[whole] * len(outs),
        compiler_params=pltpu.CompilerParams(vmem_limit_bytes=8 << 20),
    )(
        *[
            array if small else pltpu.with_memory_space_constraint(array, pltpu.VMEM)
            for array, small in zip(arrays, scalars)
        ]
    )


def rim_slots():
    places = [(0, z + 1) for z in range(8)]
    places += [(y + 1, z + 1) for y in range(4) for z in range(8)]
    places += [(5, z + 1) for z in range(8)]
    places += [(y + 1, 0) for y in range(4)] + [(y + 1, 9) for y in range(4)]
    lanes = [
        [(y * 18 + 8 * core + z) * 4 + k for y, z in places] + [-1] * (64 - len(places))
        for core in range(2)
        for k in range(4)
    ]
    return np.array(lanes, np.int32).reshape(1, -1)


def field_slots():
    def lane(core, k, row):
        return core * 256 + k * 64 + row

    lanes = []
    for y in range(4):
        lanes += [lane(z // 8, k, 8 * y + z % 8) for z in range(16) for k in range(4)]
        for core, row in ((0, 48), (0, 52), (1, 48), (1, 52)):
            lanes += [lane(core, k, row + y) for k in range(4)]
        lanes += [-1] * 48
    for row in (32, 40):
        lanes += [lane(z // 8, k, row + z % 8) for z in range(16) for k in range(4)] + [-1] * 64
    return np.array(lanes, np.int32).reshape(1, -1)


def on_device(velocity, fraction, wall_flags):
    rows, cols = (fraction.shape[0], fraction.shape[1])
    rows_devices = lax.axis_size("py")
    chips = lax.axis_size("px")
    cores = lax.axis_size("core")
    cols_devices = chips * cores
    total_rows = rows * rows_devices
    row_index = lax.axis_index("py")
    chip_index = lax.axis_index("px")
    core_index = lax.axis_index("core")

    odd = jnp.stack([row_index & 1, core_index]).astype(jnp.int32)
    y_one, y_two, z_one, z_two = run(
        rims, [(10, cols, NX), (10, cols, NX), (10, rows, NX), (10, rows, NX)], odd, velocity, fraction
    )
    y_low, y_high = shifted_pair(y_one, y_two, "py")
    z_low, z_high = shifted_pair(z_one, z_two, ("px", "core"))

    def unlayered(z_rim):
        return jnp.transpose(z_rim[:9].reshape(3, 3, rows, NX), (0, 2, 1, 3))

    provisional = predicted(
        velocity,
        wall_ghosts(velocity, wall_flags),
        jnp.concatenate([y_low[:9].reshape(3, 3, cols, NX), velocity, y_high[:9].reshape(3, 3, cols, NX)], axis=1),
        jnp.concatenate([unlayered(z_low), velocity, unlayered(z_high)], axis=2),
        fraction,
    )

    peers = rows_devices * cores
    part_x = NX // peers
    plain_x = cosine_table(NX).reshape(peers, part_x, NX).transpose(1, 0, 2).reshape(NX, NX)
    table_x = jnp.asarray(plain_x, dtype=jnp.float32)
    message, table_x = run(send_fields, [(peers, 2, 128), (3, NX, NX)], provisional, table_x)

    places = jnp.stack([row_index, chip_index, core_index]).astype(jnp.int32)

    plain_y = cosine_table(total_rows).T.reshape(rows_devices, rows, total_rows)
    plain_y = plain_y.transpose(1, 0, 2).reshape(total_rows, total_rows)
    table_y = jnp.asarray(plain_y, dtype=jnp.float32)
    inner = np.arange(256)
    row_source = inner // 32 % 2 * 128 + inner % 4 * 32 + inner // 64 * 8 + inner // 4 % 8
    sources = jnp.asarray(np.concatenate([row_source[None].astype(np.int32), rim_slots(), field_slots()], axis=1))

    half_x = jnp.asarray(half_eigenvalue(NX), dtype=jnp.float32)
    half_y = half_eigenvalue(total_rows).reshape(2, 1, 128)
    half_y = jnp.asarray(np.broadcast_to(half_y, (2, 4, 128)).reshape(8, 128), dtype=jnp.float32)
    size = cols * cores
    *betas, rho, scale, weights, table_y = run(
        prepare,
        [(rows, cols, NX), (rows + 1, cols, NX), (2, rows, cols, NX), (8, 128), (8, 128), (4, chips, 8, 128), (3, total_rows, total_rows)],
        places, half_x, half_y, table_y, fraction, y_low[9], y_high[9], z_low[9], z_high[9],
    )
    place = places[1:2]

    across = ("py", "core")
    layers_shape = (size, 8, 128)
    rims_shape = (rows_devices, 4, 128)
    message = exchange(message, across)
    message = message.reshape(rows_devices, 4, 128)
    gather, layers = run(
        read_fields, [(chips, 32, 128), layers_shape], message, table_y, sources, rho
    )
    gather = exchange(gather, "px")
    message, residual, waves, aligned = run(
        first_solve,
        [rims_shape, layers_shape, (2, 8, 128), (1, 128)],
        place, gather, layers, rho, scale, weights, table_y, sources,
    )
    message = exchange(message.reshape(peers, 2, 128), across)
    message, first, applied = run(
        first_image, [(peers, 2, 128), (64, NX), (32, NX)], message, aligned, table_x, *betas
    )
    message = exchange(message, across).reshape(rows_devices, 4, 128)
    gather, layers = run(
        read_image, [(chips, 24, 128), layers_shape], message, table_y, sources, rho
    )
    gather = exchange(gather, "px")
    message, scalars = run(
        second_solve,
        [rims_shape, (1, 128)],
        gather, layers, residual, waves, rho, scale, weights, table_y, sources,
    )
    message = exchange(message.reshape(peers, 2, 128), across)
    second, parts = run(
        second_image, [(64, NX), (rows_devices, 1, 128)], message, scalars, applied, table_x, *betas
    )
    (parts,) = run(add_parts, [(cols_devices, 1, 128)], exchange(parts, "py"))
    parts = exchange(parts, ("px", "core"))
    next_velocity, pressure = run(
        finish,
        [velocity.shape, fraction.shape],
        parts, scalars, first, second, *betas, provisional,
        last=True,
    )
    return next_velocity, pressure


def solution(mesh):
    rows = mesh.shape["py"]
    split = Mesh(mesh.devices.reshape(rows, -1, 2), ("py", "px", "core"))
    wide = P(None, "py", ("px", "core"), None)
    flat = P("py", ("px", "core"), None)
    return jax.shard_map(
        on_device,
        mesh=split,
        in_specs=(wide, flat, P(None, "py", ("px", "core"))),
        out_specs=(wide, flat),
        check_vma=False,
    )
```
